512 devices in a mesh: wave: 32 (over x, y), freq: 16 (over z, core).
Axes of the slice: x: 4, y: 8, z: 8, core: 2. Of those that a mesh axis runs over, the one named last changes fastest.
Arguments:
- res_re: float32 [8192, 8192], P('wave', 'freq'), may hold values from -6 to 6
- res_im: float32 [8192, 8192], P('wave', 'freq'), may hold values from -6 to 6
- basis_re: float32 [256, 8192], P(None, 'freq'), may hold values from -0.046875 to 0.046875
- basis_im: float32 [256, 8192], P(None, 'freq'), may hold values from -0.046875 to 0.046875
- lengths: int32 [8192], P('wave'), may hold values from 8 to 64
- pivots: int32 [128], replicated, may hold values from 0 to 8191, as said below
Outputs:
- coef_re: float32 [8192, 128], P('wave')
- coef_im: float32 [8192, 128], P('wave')
- new_re: float32 [8192, 8192], P('wave', 'freq')
- new_im: float32 [8192, 8192], P('wave', 'freq')
- errors: float32 [8192], P('wave')
The draws below stay inside these ranges and needn't reach their ends.
Inputs may be any that keep to these rules, and one draw needn't show every extreme that they name: The 128 pivots are distinct waveform indices.
All inputs are finite; a program needn't handle non-finite values. Where the reference program divides by a largest or mean magnitude, that divisor is 1e-20 or more.
Results may differ from the reference program's by a relative error of at most 0.0003.
Values sent between devices are 32-bit elements; how exact they have to be, the bound alone decides.
A program may use at most 64 MiB of HBM per device.

```python
import jax
import jax.numpy as jnp
from jax import lax

NF = 8192
BIN_BLOCK = 128
NB = 256
NP = 128
NS_STEPS = 6
WAVES = 8192


def draw_pivots(key, part):
    chosen = jax.random.permutation(jax.random.fold_in(key, 7), WAVES)
    return chosen[:NP].astype(jnp.int32)


def touch_ends(result, stream_key, least, high):
    longest = result.shape.index(max(result.shape))
    spots = []
    for shift in (0, 1):
        where = [jax.random.randint(jax.random.fold_in(stream_key, axis), (), 0, length) for axis, length in enumerate(result.shape)]
        where[longest] = (where[longest] + shift) % result.shape[longest]
        spots.append(tuple(where))
    return result.at[spots[0]].set(least).at[spots[1]].set(high)


def shard_levels(rng, extent, split, least, high):
    loudness, own = 1.0, jax.random.fold_in(rng, 6)
    for position, blocks in split:
        draws = jnp.exp(jax.random.uniform(jax.random.fold_in(own, position), (blocks,), jnp.float32, least / len(split), high / len(split)))
        loudness = loudness * jnp.repeat(draws, extent[position] // blocks).reshape([-1 if axis == position else 1 for axis in range(len(extent))])
    return loudness


def normal_values(stream_key, shape, spread, most, cuts=(), kind=jnp.bfloat16):
    drawn = spread * jax.random.normal(stream_key, shape, jnp.float32)
    if cuts:
        drawn = drawn * shard_levels(stream_key, shape, cuts, -0.22, 0.18)
    return jnp.clip(drawn, -most, most).astype(kind)


def setup_inputs(seed: int = 0) -> dict:
    arg_keys = jax.random.split(jax.random.key(seed), 7)
    return {
        "res_re": normal_values(arg_keys[0], (WAVES, NF), 1.0, 6.0, ((0, 32), (1, 16)), jnp.float32),
        "res_im": normal_values(arg_keys[1], (WAVES, NF), 1.0, 6.0, ((0, 32), (1, 16)), jnp.float32),
        "basis_re": normal_values(arg_keys[2], (NB, NF), (2 * NF) ** -0.5, 0.046875, ((1, 16),), jnp.float32),
        "basis_im": normal_values(arg_keys[3], (NB, NF), (2 * NF) ** -0.5, 0.046875, ((1, 16),), jnp.float32),
        "lengths": touch_ends(jax.random.randint(arg_keys[4], (WAVES,), NF // BIN_BLOCK // 8, NF // BIN_BLOCK + 1), jax.random.fold_in(arg_keys[4], 1), NF // BIN_BLOCK // 8, (NF // BIN_BLOCK + 1) - 1).astype(jnp.int32),
        "pivots": draw_pivots(jax.random.fold_in(arg_keys[6], 71), 0),
    }


epsilon = 1e-06

def plain(left, right):
    return jnp.dot(left, right, precision=lax.Precision.HIGHEST, preferred_element_type=jnp.float32)

def against(left, right):
    return lax.dot_general(left, right, (((1,), (1,)), ((), ())), precision=lax.Precision.HIGHEST, preferred_element_type=jnp.float32)

def product(left_re, left_im, right_re, right_im):
    return (plain(left_re, right_re) - plain(left_im, right_im), plain(left_re, right_im) + plain(left_im, right_re))

def inner(left_re, left_im, right_re, right_im):
    return (against(left_re, right_re) + against(left_im, right_im), against(left_im, right_re) - against(left_re, right_im))

def whiten(gram_re, gram_im, pivot_re, pivot_im):
    scale = 1.0 / jnp.sqrt(jnp.diagonal(gram_re) + epsilon)
    outer = scale[:, None] * scale[None, :]
    gram_re = gram_re * outer
    gram_im = gram_im * outer
    unit_re = pivot_re * scale[:, None]
    unit_im = pivot_im * scale[:, None]
    bound = jnp.max(lax.optimization_barrier(jnp.sum(jnp.abs(gram_re) + jnp.abs(gram_im), axis=1)))
    ident = jnp.eye(gram_re.shape[0], dtype=jnp.float32)
    your_re = gram_re / bound
    your_im = gram_im / bound
    zed_re = ident
    zed_im = jnp.zeros_like(ident)
    for step in range(NS_STEPS):
        mix_re, mix_im = product(zed_re, zed_im, your_re, your_im)
        step_re = 1.5 * ident - 0.5 * mix_re
        step_im = -0.5 * mix_im
        your_re, your_im = product(your_re, your_im, step_re, step_im)
        zed_re, zed_im = product(step_re, step_im, zed_re, zed_im)
    factor = 1.0 / jnp.sqrt(bound)
    return product(zed_re * factor, zed_im * factor, unit_re, unit_im)

def reference(res_re, res_im, basis_re, basis_im, lengths, pivots):
    bins = jnp.arange(NF, dtype=jnp.int32)
    mask = (bins[None, :] < BIN_BLOCK * lengths[:, None]).astype(jnp.float32)
    live_re = res_re * mask
    live_im = res_im * mask
    pivot_re = live_re[pivots]
    pivot_im = live_im[pivots]
    for sweep in range(2):
        proj_re, proj_im = inner(pivot_re, pivot_im, basis_re, basis_im)
        back_re, back_im = product(proj_re, proj_im, basis_re, basis_im)
        pivot_re = pivot_re - back_re
        pivot_im = pivot_im - back_im
    gram_re, gram_im = inner(pivot_re, pivot_im, pivot_re, pivot_im)
    block_re, block_im = whiten(gram_re, gram_im, pivot_re, pivot_im)
    coef_re, coef_im = inner(live_re, live_im, block_re, block_im)
    back_re, back_im = product(coef_re, coef_im, block_re, block_im)
    new_re = (live_re - back_re) * mask
    new_im = (live_im - back_im) * mask
    errors = lax.optimization_barrier(jnp.sum(new_re * new_re + new_im * new_im, axis=1)) / (BIN_BLOCK * lengths).astype(jnp.float32)
    return (coef_re, coef_im, new_re, new_im, errors)
```

```python
import functools

import jax
import jax.numpy as jnp
from jax import lax
from jax.experimental import pallas as pl
from jax.experimental.pallas import tpu as pltpu
from jax.sharding import Mesh
from jax.sharding import PartitionSpec as P

BIN_BLOCK = 128
NS_STEPS = 6
EPSILON = 1e-06
TORUS = (4, 8, 8, 2)
AXES = ("x", "y", "z", "core")
F32 = jnp.float32
BF16 = jnp.bfloat16


def dot(left, right, dims):
    return lax.dot_general(left, right, (dims, ((), ())), preferred_element_type=F32)


NN = ((1,), (0,))
NT = ((1,), (1,))


def halves(a):
    high = a.astype(BF16)
    return high, (a - high.astype(F32)).astype(BF16)


def thirds(a):
    high = a.astype(BF16)
    rest = a - high.astype(F32)
    mid = rest.astype(BF16)
    return high, mid, (rest - mid.astype(F32)).astype(BF16)


def product(left, right, dims):
    lh, ll = left
    rh, rl = right
    along = dims[1][0]
    return dot(jnp.concatenate([lh, ll, lh], axis=1), jnp.concatenate([rh, rh, rl], axis=along), dims)


def chosen(select, a):
    parts = thirds(a)
    return dot(jnp.concatenate([select] * 3, axis=1), jnp.concatenate(parts, axis=0), NN)


def swapped(a, part, axis):
    n = a.shape[axis]
    return jnp.where(part == 0, pltpu.roll(a, n - 4, axis), pltpu.roll(a, 4, axis))


def short_product(chunk, rights, dims):
    high = chunk.astype(BF16).astype(F32)
    both = jnp.concatenate([high, chunk - high], axis=0).astype(BF16)
    out = []
    for rh, rl in rights:
        a = dot(both, rh, dims)
        b = dot(both, rl, dims)
        out.append((a[:8] + a[8:]) + (b[:8] + b[8:]))
    return out


def kernel(
    torus,
    res_re, res_im, basis_re, basis_im, lens, lens_row, piv,
    coef_re, coef_im, new_re, new_im, err,
    live, base, picked, xr, ysum, yr, kout, kin, pall, wt,
    gpart, gpair, ghalf, gin, gfull, cpart, cpair, chalf, cin, cfull, eout, ein,
    xs_s, xs_r, ys_s, ys_r, k_s, k_r, ay_s, ay_r, ax_s, ax_r,
    p_s, p_r, gz_s, gz_r, gt_s, gt_r, gc_s, gc_r, cz_s, cz_r, ct_s, ct_r, cc_s, cc_r, e_s, e_r,
):
    nx, ny, nz, nc = torus
    x, y, z, c = (lax.axis_index(a) for a in AXES)
    f = z * nc + c
    rows, bins = res_re.shape
    emb = 8 * nx * ny
    nb = basis_re.shape[0]
    xs = [lax.rem(x + d, nx) for d in range(1, nx)]
    ys = [lax.rem(y + d, ny) for d in range(1, ny)]
    zs = [lax.rem(z + d, nz) for d in range(1, nz)]
    fs = [(lax.rem(z + dz, nz), lax.rem(c + dc, nc)) for dz in range(nz) for dc in range(nc) if dz or dc]

    barrier = pltpu.get_barrier_semaphore()
    peers = [(p, y, z, c) for p in xs] + [(x, p, z, c) for p in ys] + [(x, y, p, q) for p, q in fs]
    for peer in peers:
        pl.semaphore_signal(barrier, inc=1, device_id=peer, device_id_type=pl.DeviceIdType.MESH)

    started = []

    def push(src, dst, send, recv, to):
        copy = pltpu.make_async_remote_copy(
            src_ref=src, dst_ref=dst, send_sem=send, recv_sem=recv, device_id=to,
            device_id_type=pl.DeviceIdType.MESH,
        )
        copy.start()
        started.append(copy)
        return copy

    def arrived(copies):
        for copy in copies:
            copy.wait_recv()

    first_bin = f * bins
    for r in range(0, rows, 64):
        part = slice(r, min(r + 64, rows))
        count = part.stop - part.start
        at = first_bin + lax.broadcasted_iota(jnp.int32, (count, bins), 1)
        mask = (at < BIN_BLOCK * lens[part, :]).astype(F32)
        live[part, :bins] = res_re[part, :] * mask
        live[part, bins:] = res_im[part, :] * mask
    own = (x * ny + y) * rows + lax.broadcasted_iota(jnp.int32, (emb, rows), 1)
    select = (piv[...] == own).astype(F32).astype(BF16)
    is_im = lax.rem(lax.broadcasted_iota(jnp.int32, (emb, bins), 0), 8) // 4
    picked[...] = jnp.where(is_im == 0, chosen(select, live[:, :bins]), chosen(select, live[:, bins:]))

    pl.semaphore_wait(barrier, len(peers))

    span = 8 * ny

    def chunk_of(i, size):
        return pl.ds(pl.multiple_of(i * size, size), size)

    copies = [
        push(picked.at[chunk_of(p, span)], xr.at[i], xs_s.at[i], xs_r.at[i], (p, y, z, c)) for i, p in enumerate(xs)
    ]
    for i, ref in enumerate((basis_re, basis_im)):
        high, low = halves(ref[...])
        base[2 * i] = high
        base[2 * i + 1] = low
    arrived(copies)
    total = picked[chunk_of(x, span), :]
    for i in range(nx - 1):
        total = total + xr[i]
    ysum[...] = total
    copies = [
        push(ysum.at[chunk_of(p, 8)], yr.at[i], ys_s.at[i], ys_r.at[i], (x, p, z, c)) for i, p in enumerate(ys)
    ]
    arrived(copies)
    chunk = ysum[chunk_of(y, 8), :]
    for i in range(ny - 1):
        chunk = chunk + yr[i]

    b_re = (base[0], base[1])
    b_im = (base[2], base[3])
    sign_b = jnp.where(lax.broadcasted_iota(jnp.int32, (8, bins), 0) < 4, 1.0, -1.0).astype(F32)
    sign_k = jnp.where(lax.broadcasted_iota(jnp.int32, (8, nb), 0) < 4, 1.0, -1.0).astype(F32)
    for sweep in range(2):
        a, b = short_product(chunk, (b_re, b_im), NT)
        kout[sweep] = a + sign_k * pltpu.roll(b, 4, 0)
        copies = [
            push(kout.at[sweep], kin.at[sweep, i], k_s.at[sweep, i], k_r.at[sweep, i], (x, y, p, q))
            for i, (p, q) in enumerate(fs)
        ]
        arrived(copies)
        proj = kout[sweep]
        for i in range(len(fs)):
            proj = proj + kin[sweep, i]
        a, b = short_product(proj, (b_re, b_im), NN)
        chunk = chunk - (a - sign_b * pltpu.roll(b, 4, 0))

    mine = x * ny + y
    pall[chunk_of(mine, 8), :] = chunk
    copies = [
        push(pall.at[chunk_of(mine, 8)], pall.at[chunk_of(mine, 8)], ay_s.at[i], ay_r.at[i], (x, p, z, c))
        for i, p in enumerate(ys)
    ]
    arrived(copies)
    copies = [
        push(pall.at[chunk_of(x, span)], pall.at[chunk_of(x, span)], ax_s.at[i], ax_r.at[i], (p, y, z, c))
        for i, p in enumerate(xs)
    ]
    live_halves = halves(live[...])
    arrived(copies)

    sign = jnp.where(is_im == 0, 1.0, -1.0).astype(F32)
    for half, both in enumerate((halves(sign * pall[...]), halves(swapped(pall[...], is_im, 0)))):
        for i in range(2):
            wt[i, :, half * bins : (half + 1) * bins] = both[i]

    npiv = emb // 2
    to_row = lax.broadcasted_iota(jnp.int32, (npiv, emb), 0)
    from_row = lax.broadcasted_iota(jnp.int32, (npiv, emb), 1)
    real_row = (to_row // 4) * 8 + lax.rem(to_row, 4)
    take_real = (from_row == real_row).astype(F32).astype(BF16)
    take_imag = (from_row == real_row + 4).astype(F32).astype(BF16)
    w = (wt[0], wt[1])
    top = tuple(dot(take_real, half, NN).astype(BF16) for half in w)
    gram = product(top, w, NT)
    gr = npiv // (nz * nc)
    cr = rows // (nz * nc)
    for i in range(nc):
        for j in range(nz):
            at = (i * nz + j) * gr
            gpart[i, j] = gram[at : at + gr]
    g_pair = push(gpart.at[1 - c], gpair, p_s.at[0], p_r.at[0], (x, y, z, 1 - c))
    cross = product(live_halves, w, NT)
    for i in range(nc):
        for j in range(nz):
            at = (i * nz + j) * cr
            cpart[i, j] = cross[at : at + cr]
    c_pair = push(cpart.at[1 - c], cpair, p_s.at[1], p_r.at[1], (x, y, z, 1 - c))

    def scatter(pair, part, got, half, inward, s, r):
        arrived([pair])
        half[...] = part[c] + got[...]
        return [push(half.at[p], inward.at[i], s.at[i], r.at[i], (x, y, p, c)) for i, p in enumerate(zs)]

    def spread(copies, half, inward, full, s, r):
        arrived(copies)
        total = half[z]
        for i in range(nz - 1):
            total = total + inward[i]
        full[c, z] = total
        return [push(full.at[c, z], full.at[c, z], s.at[i], r.at[i], (x, y, p, c)) for i, p in enumerate(zs)]

    g_scatter = scatter(g_pair, gpart, gpair, ghalf, gin, gz_s, gz_r)
    c_scatter = scatter(c_pair, cpart, cpair, chalf, cin, cz_s, cz_r)
    g_spread = spread(g_scatter, ghalf, gin, gfull, gt_s, gt_r)
    c_spread = spread(c_scatter, chalf, cin, cfull, ct_s, ct_r)
    arrived(g_spread)
    g_last = push(gfull.at[c], gfull.at[c], gc_s.at[0], gc_r.at[0], (x, y, z, 1 - c))
    arrived(c_spread)
    c_last = push(cfull.at[c], cfull.at[c], cc_s.at[0], cc_r.at[0], (x, y, z, 1 - c))
    arrived([g_last])

    gram = gfull[...].reshape(npiv, emb)
    col_part = lax.rem(lax.broadcasted_iota(jnp.int32, (npiv, emb), 1), 8) // 4
    turned = jnp.where(col_part == 0, -1.0, 1.0).astype(F32) * swapped(gram, col_part, 1)
    place = jnp.concatenate([take_real, take_imag], axis=0)
    spread_rows = jnp.concatenate([gram, turned], axis=0)
    parts = thirds(spread_rows)
    gram = sum(dot(place, part, ((0,), (0,))) for part in parts)
    eye = lax.broadcasted_iota(jnp.int32, (emb, emb), 0) == lax.broadcasted_iota(jnp.int32, (emb, emb), 1)
    ident = eye.astype(F32)
    diag = gram * ident
    scale_col = 1.0 / jnp.sqrt(jnp.sum(diag, axis=1, keepdims=True) + EPSILON)
    scale_row = 1.0 / jnp.sqrt(jnp.sum(diag, axis=0, keepdims=True) + EPSILON)
    gram = gram * (scale_col * scale_row)
    bound = jnp.max(jnp.sum(jnp.abs(gram), axis=1, keepdims=True), axis=0, keepdims=True)
    your = gram / bound
    zed = None
    for step in range(NS_STEPS):
        yh = halves(your)
        mix = your if zed is None else product(halves(zed), yh, NN)
        s = 1.5 * ident - 0.5 * mix
        sh = halves(s)
        if step < NS_STEPS - 1:
            your = product(yh, sh, NN)
        zed = s if zed is None else product(sh, halves(zed), NN)
    zed = zed * (1.0 / jnp.sqrt(bound))

    zed_out = tuple(dot(place, half, NN).astype(BF16) for half in halves(zed))
    arrived([c_last])
    cross = cfull[...].reshape(rows, emb)
    coef = product(halves(cross * scale_row), zed_out, NT)
    coef_re[...] = coef[:, :npiv]
    coef_im[...] = coef[:, npiv:]
    block = product(halves((zed_out[0].astype(F32) + zed_out[1].astype(F32)) * scale_row), w, NN)
    block = halves(block)
    ones = jnp.ones((8, 2 * bins), BF16)
    for r in range(0, rows, 64):
        part = slice(r, min(r + 64, rows))
        count = part.stop - part.start
        at = first_bin + lax.broadcasted_iota(jnp.int32, (count, bins), 1)
        mask = (at < BIN_BLOCK * lens[part, :]).astype(F32)
        back = product(halves(coef[part, :]), block, NN)
        new_re[part, :] = (live[part, :bins] - back[:, :bins]) * mask
        new_im[part, :] = (live[part, bins:] - back[:, bins:]) * mask
    squares = [thirds(ref[...] * ref[...]) for ref in (new_re, new_im)]
    summed = sum(dot(ones[:, :bins], p, NT) for three in squares for p in three)
    eout[...] = summed[0:1, :]
    here = f
    ein[here] = eout[...]
    copies = [
        push(eout, ein.at[here], e_s.at[i], e_r.at[i], (x, y, p, q)) for i, (p, q) in enumerate(fs)
    ]
    arrived(copies)
    total = ein[0]
    for i in range(1, nz * nc):
        total = total + ein[i]
    err[...] = total / (BIN_BLOCK * lens_row[...]).astype(F32)

    for copy in started:
        copy.wait_send()


def body(torus, res_re, res_im, basis_re, basis_im, lengths, pivots):
    nx, ny, nz, nc = torus
    rows, bins = res_re.shape
    nb = basis_re.shape[0]
    owners = nx * ny
    emb = 8 * owners
    nf = nz * nc
    piv = jnp.broadcast_to(pivots.reshape(owners, 1, 4), (owners, 2, 4)).reshape(emb, 1)
    gr = emb // 2 // nf
    cr = rows // nf
    vmem = pltpu.VMEM
    dma = pltpu.SemaphoreType.DMA
    out = [
        jax.ShapeDtypeStruct((rows, emb // 2), F32),
        jax.ShapeDtypeStruct((rows, emb // 2), F32),
        jax.ShapeDtypeStruct((rows, bins), F32),
        jax.ShapeDtypeStruct((rows, bins), F32),
        jax.ShapeDtypeStruct((1, rows), F32),
    ]
    scratch = [
        vmem((rows, 2 * bins), F32),
        vmem((4, nb, bins), BF16),
        vmem((emb, bins), F32),
        vmem((nx - 1, 8 * ny, bins), F32),
        vmem((8 * ny, bins), F32),
        vmem((ny - 1, 8, bins), F32),
        vmem((2, 8, nb), F32),
        vmem((2, nf - 1, 8, nb), F32),
        vmem((emb, bins), F32),
        vmem((2, emb, 2 * bins), BF16),
        vmem((nc, nz, gr, emb), F32), vmem((nz, gr, emb), F32), vmem((nz, gr, emb), F32),
        vmem((nz - 1, gr, emb), F32), vmem((nc, nz, gr, emb), F32),
        vmem((nc, nz, cr, emb), F32), vmem((nz, cr, emb), F32), vmem((nz, cr, emb), F32),
        vmem((nz - 1, cr, emb), F32), vmem((nc, nz, cr, emb), F32),
        vmem((1, rows), F32), vmem((nf, 1, rows), F32),
        dma((nx - 1,)), dma((nx - 1,)), dma((ny - 1,)), dma((ny - 1,)),
        dma((2, nf - 1)), dma((2, nf - 1)),
        dma((ny - 1,)), dma((ny - 1,)), dma((nx - 1,)), dma((nx - 1,)),
        dma((2,)), dma((2,)),
        dma((nz - 1,)), dma((nz - 1,)), dma((nz - 1,)), dma((nz - 1,)), dma((1,)), dma((1,)),
        dma((nz - 1,)), dma((nz - 1,)), dma((nz - 1,)), dma((nz - 1,)), dma((1,)), dma((1,)),
        dma((nf - 1,)), dma((nf - 1,)),
    ]
    whole = pl.BlockSpec(memory_space=pltpu.VMEM)
    coef_re, coef_im, new_re, new_im, err = pl.pallas_call(
        functools.partial(kernel, torus),
        out_shape=out,
        in_specs=[whole] * 7,
        out_specs=[whole] * 5,
        scratch_shapes=scratch,
        compiler_params=pltpu.CompilerParams(collective_id=0, has_side_effects=True),
    )(res_re, res_im, basis_re, basis_im, lengths[:, None], lengths[None, :], piv)
    return coef_re, coef_im, new_re, new_im, err.reshape(rows)


def build(mesh, torus):
    axes = Mesh(mesh.devices.reshape(torus), AXES)
    wave, freq = ("x", "y"), ("z", "core")
    in_specs = (P(wave, freq), P(wave, freq), P(None, freq), P(None, freq), P(wave), P())
    out_specs = (P(wave, None), P(wave, None), P(wave, freq), P(wave, freq), P(wave))
    return jax.shard_map(
        functools.partial(body, torus), mesh=axes, in_specs=in_specs, out_specs=out_specs, check_vma=False
    )


def solution(mesh):
    return build(mesh, TORUS)
```

```python
import functools

import jax
import jax.numpy as jnp
from jax import lax
from jax.experimental import pallas as pl
from jax.experimental.pallas import tpu as pltpu
from jax.sharding import Mesh
from jax.sharding import PartitionSpec as P

BIN_BLOCK = 128
NS_STEPS = 6
EPSILON = 1e-06
TORUS = (4, 8, 8, 2)
AXES = ("x", "y", "z", "core")
F32 = jnp.float32
BF16 = jnp.bfloat16


def dot(left, right, dims):
    return lax.dot_general(left, right, (dims, ((), ())), preferred_element_type=F32)


NN = ((1,), (0,))
NT = ((1,), (1,))


def halves(a):
    high = a.astype(BF16)
    return high, (a - high.astype(F32)).astype(BF16)


def thirds(a):
    high = a.astype(BF16)
    rest = a - high.astype(F32)
    mid = rest.astype(BF16)
    return high, mid, (rest - mid.astype(F32)).astype(BF16)


def product(left, right, dims):
    lh, ll = left
    rh, rl = right
    along = dims[1][0]
    return dot(jnp.concatenate([lh, ll, lh], axis=1), jnp.concatenate([rh, rh, rl], axis=along), dims)


def chosen(select, a):
    parts = thirds(a)
    return dot(jnp.concatenate([select] * 3, axis=1), jnp.concatenate(parts, axis=0), NN)


def swapped(a, part, axis):
    n = a.shape[axis]
    return jnp.where(part == 0, pltpu.roll(a, n - 4, axis), pltpu.roll(a, 4, axis))


def short_product(chunk, rights, dims):
    high = chunk.astype(BF16).astype(F32)
    both = jnp.concatenate([high, chunk - high], axis=0).astype(BF16)
    out = []
    for rh, rl in rights:
        a = dot(both, rh, dims)
        b = dot(both, rl, dims)
        out.append((a[:8] + a[8:]) + (b[:8] + b[8:]))
    return out


def kernel(
    torus,
    res_re, res_im, basis_re, basis_im, lens, piv,
    coef_re, coef_im, new_re, new_im, err,
    live, live_h, basis, base, vlen, vpiv, picked, far, relay, near, ysum, yr, kout, kin, pall, tall, wt,
    xpart, xpair, xhalf, xin, xfull,
    gpart, gpair, ghalf, gin, gfull, cpart, cpair, chalf, cin, cfull, eout, ein,
    in_s, rx_s, rx_r, ry_s, ry_r, k_s, k_r, p_s, p_r, py_s, py_r, px_s, px_r, pr_s, pr_r,
    ty_s, ty_r, tx_s, tx_r, tr_s, tr_r, zs_s, zs_r, zg_s, zg_r, c_s, c_r, e_s, e_r,
):
    nx, ny, nz, nc = torus
    x, y, z, c = (lax.axis_index(a) for a in AXES)
    f = z * nc + c
    rows, bins = res_re.shape
    emb = 8 * nx * ny
    npiv = emb // 2
    nb = basis_re.shape[0]
    span = 8 * ny
    right, left = lax.rem(x + 1, nx), lax.rem(x + nx - 1, nx)
    across = lax.rem(x + 2, nx)
    ys = [lax.rem(y + d, ny) for d in range(1, ny)]
    zs = [lax.rem(z + d, nz) for d in range(1, nz)]
    fs = [(lax.rem(z + dz, nz), lax.rem(c + dc, nc)) for dz in range(nz) for dc in range(nc) if dz or dc]

    loads = [(lens, vlen), (piv, vpiv), (res_re, live.at[:, pl.ds(0, bins)]), (res_im, live.at[:, pl.ds(bins, bins)])]
    loads += [(basis_re, basis.at[0]), (basis_im, basis.at[1])]
    loads = [pltpu.make_async_copy(src, dst, in_s.at[i]) for i, (src, dst) in enumerate(loads)]
    for load in loads:
        load.start()
    barrier = pltpu.get_barrier_semaphore()
    peers = [(right, y, z, c), (left, y, z, c)] + [(x, p, z, c) for p in ys] + [(x, y, p, q) for p, q in fs]
    for peer in peers:
        pl.semaphore_signal(barrier, inc=1, device_id=peer, device_id_type=pl.DeviceIdType.MESH)

    started = []

    def push(src, dst, send, recv, to):
        copy = pltpu.make_async_remote_copy(
            src_ref=src, dst_ref=dst, send_sem=send, recv_sem=recv, device_id=to,
            device_id_type=pl.DeviceIdType.MESH,
        )
        copy.start()
        started.append(copy)
        return copy

    def arrived(copies):
        for copy in copies:
            copy.wait_recv()

    def chunk_of(i, size):
        return pl.ds(pl.multiple_of(i * size, size), size)

    for load in loads[:4]:
        load.wait()
    diagonal = lax.broadcasted_iota(jnp.int32, (rows, rows), 0) == lax.broadcasted_iota(jnp.int32, (rows, rows), 1)
    ends = jnp.sum(jnp.where(diagonal, vlen[...] * BIN_BLOCK, 0).astype(F32), axis=1, keepdims=True)
    first_bin = f * bins

    def mask_of(part):
        count = part.stop - part.start
        at = first_bin + lax.broadcasted_iota(jnp.int32, (count, bins), 1)
        return (at.astype(F32) < ends[part, :]).astype(F32)

    blocks = [slice(r, min(r + 64, rows)) for r in range(0, rows, 64)]
    for part in blocks:
        mask = mask_of(part)
        live[part, :bins] = live[part, :bins] * mask
        live[part, bins:] = live[part, bins:] * mask
    to_row = lax.broadcasted_iota(jnp.int32, (emb, npiv), 0)
    of_row = lax.broadcasted_iota(jnp.int32, (emb, npiv), 1) == (to_row // 8) * 4 + lax.rem(to_row, 4)
    wanted = jnp.sum(jnp.where(of_row, vpiv[...], 0).astype(F32), axis=1, keepdims=True)
    own = (x * ny + y) * rows + lax.broadcasted_iota(jnp.int32, (emb, rows), 1)
    select = (wanted == own.astype(F32)).astype(F32).astype(BF16)
    is_im = lax.rem(lax.broadcasted_iota(jnp.int32, (emb, bins), 0), 8) // 4
    picked[...] = jnp.where(is_im == 0, chosen(select, live[:, :bins]), chosen(select, live[:, bins:]))

    pl.semaphore_wait(barrier, len(peers))

    half = bins // 2
    ahead, behind = pl.ds(0, half), pl.ds(half, half)
    to_right, to_left = (right, y, z, c), (left, y, z, c)
    far_copies = [
        push(picked.at[chunk_of(across, span), ahead], far.at[0], rx_s.at[0], rx_r.at[0], to_right),
        push(picked.at[chunk_of(across, span), behind], far.at[1], rx_s.at[1], rx_r.at[1], to_left),
    ]
    near_copies = [
        push(picked.at[chunk_of(right, span), behind], near.at[0, :, behind], rx_s.at[2], rx_r.at[2], to_right),
        push(picked.at[chunk_of(left, span), ahead], near.at[1, :, ahead], rx_s.at[3], rx_r.at[3], to_left),
    ]

    for load in loads[4:]:
        load.wait()
    for i in range(2):
        high, low = halves(basis[i])
        base[2 * i] = high
        base[2 * i + 1] = low
    b_re = (base[0], base[1])
    b_im = (base[2], base[3])
    plus = jnp.concatenate([basis[0] + basis[1], basis[1] - basis[0]], axis=1)
    right_side = tuple(jnp.concatenate([base[i], base[2 + i]], axis=1) for i in range(2))
    both = product(halves(plus), right_side, NT)

    def scatter_rows(part, value):
        size = part.shape[2]
        for i in range(nc):
            for j in range(nz):
                at = (i * nz + j) * size
                part[i, j] = value[at : at + size]

    def pair_up(k, part, got):
        return push(part.at[1 - c], got, p_s.at[k], p_r.at[k], (x, y, z, 1 - c))

    def scatter(k, pair, part, got, summed, inward):
        arrived([pair])
        summed[...] = part[c] + got[...]
        return [push(summed.at[p], inward.at[i], zs_s.at[k, i], zs_r.at[k, i], (x, y, p, c)) for i, p in enumerate(zs)]

    def spread(k, copies, summed, inward, full):
        arrived(copies)
        total = summed[z]
        for i in range(nz - 1):
            total = total + inward[i]
        full[c, z] = total
        return [push(full.at[c, z], full.at[c, z], zg_s.at[k, i], zg_r.at[k, i], (x, y, p, c)) for i, p in enumerate(zs)]

    def share(k, copies, full):
        arrived(copies)
        return push(full.at[c], full.at[c], c_s.at[k], c_r.at[k], (x, y, z, 1 - c))

    scatter_rows(xpart, both)
    x_pair = pair_up(0, xpart, xpair)

    arrived(far_copies[:1])
    relay[0] = picked[chunk_of(right, span), :half] + far[0]
    near_copies.append(push(relay.at[0], near.at[0, :, ahead], rx_s.at[4], rx_r.at[4], to_right))
    arrived(far_copies[1:])
    relay[1] = picked[chunk_of(left, span), half:] + far[1]
    near_copies.append(push(relay.at[1], near.at[1, :, behind], rx_s.at[5], rx_r.at[5], to_left))
    x_scatter = scatter(0, x_pair, xpart, xpair, xhalf, xin)
    arrived(near_copies)
    ysum[...] = picked[chunk_of(x, span), :] + near[0] + near[1]
    y_copies = [
        push(ysum.at[chunk_of(p, 8)], yr.at[i], ry_s.at[i], ry_r.at[i], (x, p, z, c)) for i, p in enumerate(ys)
    ]
    for i, value in enumerate(halves(live[...])):
        live_h[i] = value
    x_spread = spread(0, x_scatter, xhalf, xin, xfull)
    arrived(y_copies)
    chunk = ysum[chunk_of(y, 8), :]
    for i in range(ny - 1):
        chunk = chunk + yr[i]

    mine = x * ny + y
    order = sorted(range(1, ny), key=lambda d: min(d, ny - d))

    def gather_steps(buf, ss, rs, wide):
        ysend, xsend, rsend = ss
        yrecv, xrecv, rrecv = rs
        lanes = (pl.ds(0, wide // 2), pl.ds(wide // 2, wide // 2))
        copies = {}

        def rows_of(i, d):
            return pl.ds(pl.multiple_of((i * ny + lax.rem(y + ny - d, ny)) * 8, 8), 8)

        def along_y():
            at = chunk_of(mine, 8)
            for i, p in enumerate(ys):
                copies["y", i + 1] = push(buf.at[at], buf.at[at], ysend.at[i], yrecv.at[i], (x, p, z, c))

        def along_x(d):
            if d:
                arrived([copies["y", d]])
            at = rows_of(x, d)
            for k, to in enumerate((to_right, to_left)):
                copies["x", d, k] = push(buf.at[at], buf.at[at], xsend.at[d, k], xrecv.at[d, k], to)

        def further(d):
            for k, (source, to) in enumerate(((left, to_right), (right, to_left))):
                arrived([copies["x", d, k]])
                at = rows_of(source, d)
                copies["r", d, k] = push(
                    buf.at[at, lanes[k]], buf.at[at, lanes[k]], rsend.at[d, k], rrecv.at[d, k], to
                )

        def finish():
            arrived([copies["r", d, k] for d in range(ny) for k in range(2)])

        return along_y, along_x, further, finish

    pall[chunk_of(mine, 8), :] = chunk
    p_y, p_x, p_further, p_finish = gather_steps(pall, (py_s, px_s, pr_s), (py_r, px_r, pr_r), bins)
    p_y()
    p_x(0)
    sign_k = jnp.where(lax.broadcasted_iota(jnp.int32, (8, nb), 0) < 4, 1.0, -1.0).astype(F32)
    a, b = short_product(chunk, (b_re, b_im), NT)
    kout[...] = a + sign_k * pltpu.roll(b, 4, 0)
    k_copies = [
        push(kout, kin.at[i], k_s.at[i], k_r.at[i], (x, y, p, q)) for i, (p, q) in enumerate(fs)
    ]
    x_last = share(0, x_spread, xfull)
    for d in order:
        p_x(d)
    late = [0] + order
    early, late = late[:3], late[3:]
    for d in early:
        p_further(d)
    arrived([x_last])
    arrived(k_copies)
    proj = kout[...]
    for i in range(len(fs)):
        proj = proj + kin[i]
    gram = halves(xfull[...].reshape(nb, nb))
    (straight,) = short_product(proj, (gram,), NN)
    (turned,) = short_product(proj, (gram,), NT)
    again = 0.5 * ((straight + turned) - sign_k * pltpu.roll(straight - turned, 4, 0))
    tall[chunk_of(mine, 8), :] = 2.0 * proj - again
    t_y, t_x, t_further, t_finish = gather_steps(tall, (ty_s, tx_s, tr_s), (ty_r, tx_r, tr_r), nb)
    t_y()
    t_x(0)
    for d in late:
        p_further(d)
    for d in order[:2]:
        t_x(d)
    t_further(0)
    for d in order[2:]:
        t_x(d)
    for d in order:
        t_further(d)
    p_finish()
    t_finish()

    sign = jnp.where(is_im == 0, 1.0, -1.0).astype(F32)
    taken = halves(tall[...])
    back = product(taken, b_re, NN) - sign * swapped(product(taken, b_im, NN), is_im, 0)
    ortho = pall[...] - back
    for k, two in enumerate((halves(sign * ortho), halves(swapped(ortho, is_im, 0)))):
        for i in range(2):
            wt[i, :, k * bins : (k + 1) * bins] = two[i]

    to_row = lax.broadcasted_iota(jnp.int32, (npiv, emb), 0)
    from_row = lax.broadcasted_iota(jnp.int32, (npiv, emb), 1)
    real_row = (to_row // 4) * 8 + lax.rem(to_row, 4)
    take_real = (from_row == real_row).astype(F32).astype(BF16)
    take_imag = (from_row == real_row + 4).astype(F32).astype(BF16)
    w = (wt[0], wt[1])
    top = tuple(dot(take_real, part, NN).astype(BF16) for part in w)
    scatter_rows(gpart, product(top, w, NT))
    g_pair = pair_up(1, gpart, gpair)
    scatter_rows(cpart, product((live_h[0], live_h[1]), w, NT))
    c_pair = pair_up(2, cpart, cpair)

    g_scatter = scatter(1, g_pair, gpart, gpair, ghalf, gin)
    c_scatter = scatter(2, c_pair, cpart, cpair, chalf, cin)
    g_spread = spread(1, g_scatter, ghalf, gin, gfull)
    c_spread = spread(2, c_scatter, chalf, cin, cfull)
    g_last = share(1, g_spread, gfull)
    arrived([g_last])

    gram = gfull[...].reshape(npiv, emb)
    col_part = lax.rem(lax.broadcasted_iota(jnp.int32, (npiv, emb), 1), 8) // 4
    turned = jnp.where(col_part == 0, -1.0, 1.0).astype(F32) * swapped(gram, col_part, 1)
    place = jnp.concatenate([take_real, take_imag], axis=0)
    parts = thirds(jnp.concatenate([gram, turned], axis=0))
    gram = sum(dot(place, part, ((0,), (0,))) for part in parts)
    eye = lax.broadcasted_iota(jnp.int32, (emb, emb), 0) == lax.broadcasted_iota(jnp.int32, (emb, emb), 1)
    ident = eye.astype(F32)
    diag = gram * ident
    scale_col = 1.0 / jnp.sqrt(jnp.sum(diag, axis=1, keepdims=True) + EPSILON)
    scale_row = 1.0 / jnp.sqrt(jnp.sum(diag, axis=0, keepdims=True) + EPSILON)
    gram = gram * (scale_col * scale_row)
    bound = jnp.max(jnp.sum(jnp.abs(gram), axis=1, keepdims=True), axis=0, keepdims=True)
    your = gram / bound
    zed = None
    for step in range(NS_STEPS):
        if step == 3:
            c_last = share(2, c_spread, cfull)
        yh = halves(your)
        mix = your if zed is None else product(halves(zed), yh, NN)
        s = 1.5 * ident - 0.5 * mix
        sh = halves(s)
        if step < NS_STEPS - 1:
            your = product(yh, sh, NN)
        zed = s if zed is None else product(sh, halves(zed), NN)
    zed = zed * (1.0 / jnp.sqrt(bound))

    zed_out = tuple(dot(place, part, NN).astype(BF16) for part in halves(zed))
    block = product(halves((zed_out[0].astype(F32) + zed_out[1].astype(F32)) * scale_row), w, NN)
    block = halves(block)
    arrived([c_last])
    cross = cfull[...].reshape(rows, emb)
    coef = product(halves(cross * scale_row), zed_out, NT)
    coef_re[...] = coef[:, :npiv]
    coef_im[...] = coef[:, npiv:]
    sums = []
    for part in blocks:
        mask = mask_of(part)
        back = product(halves(coef[part, :]), block, NN)
        real = (live[part, :bins] - back[:, :bins]) * mask
        imag = (live[part, bins:] - back[:, bins:]) * mask
        new_re[part, :] = real
        new_im[part, :] = imag
        square = real * real + imag * imag
        sums.append(sum(square[:, i : i + 128] for i in range(0, bins, 128)))
    ones = jnp.ones((8, 128), BF16)
    summed = sum(dot(ones, part, NT) for part in thirds(jnp.concatenate(sums, axis=0)))
    eout[...] = summed[0:1, :]
    ein[f] = summed[0:1, :]
    copies = [push(eout, ein.at[f], e_s.at[i], e_r.at[i], (x, y, p, q)) for i, (p, q) in enumerate(fs)]
    arrived(copies)
    total = ein[0]
    for i in range(1, nz * nc):
        total = total + ein[i]
    err[...] = total / (BIN_BLOCK * vlen[...]).astype(F32)

    for copy in started:
        copy.wait_send()


def handed_out(*refs):
    count = len(refs) // 2
    copies = [pltpu.make_async_copy(refs[i], refs[count + i], refs[-1].at[i]) for i in range(count)]
    for copy in copies:
        copy.start()
    for copy in copies:
        copy.wait()


def body(torus, res_re, res_im, basis_re, basis_im, lengths, pivots):
    nx, ny, nz, nc = torus
    rows, bins = res_re.shape
    nb = basis_re.shape[0]
    emb = 8 * nx * ny
    nf = nz * nc
    span = 8 * ny
    vmem = pltpu.VMEM
    dma = pltpu.SemaphoreType.DMA
    shapes = [(rows, emb // 2), (rows, emb // 2), (rows, bins), (rows, bins), (1, rows)]

    def summed(count, width):
        part = count // nf
        whole, across = vmem((nc, nz, part, width), F32), vmem((nz, part, width), F32)
        return [whole, across, across, vmem((nz - 1, part, width), F32), whole]

    scratch = [
        vmem((rows, 2 * bins), F32),
        vmem((2, rows, 2 * bins), BF16),
        vmem((2, nb, bins), F32),
        vmem((4, nb, bins), BF16),
        vmem((1, rows), jnp.int32),
        vmem((1, emb // 2), jnp.int32),
        vmem((emb, bins), F32),
        vmem((2, span, bins // 2), F32),
        vmem((2, span, bins // 2), F32),
        vmem((2, span, bins), F32),
        vmem((span, bins), F32),
        vmem((ny - 1, 8, bins), F32),
        vmem((8, nb), F32),
        vmem((nf - 1, 8, nb), F32),
        vmem((emb, bins), F32),
        vmem((emb, nb), F32),
        vmem((2, emb, 2 * bins), BF16),
        *summed(nb, nb),
        *summed(emb // 2, emb),
        *summed(rows, emb),
        vmem((1, rows), F32), vmem((nf, 1, rows), F32),
        dma((6,)), dma((6,)), dma((6,)), dma((ny - 1,)), dma((ny - 1,)), dma((nf - 1,)), dma((nf - 1,)),
        dma((3,)), dma((3,)),
        *[dma((ny - 1,)), dma((ny - 1,)), dma((ny, 2)), dma((ny, 2)), dma((ny, 2)), dma((ny, 2))] * 2,
        dma((3, nz - 1)), dma((3, nz - 1)), dma((3, nz - 1)), dma((3, nz - 1)), dma((3,)), dma((3,)),
        dma((nf - 1,)), dma((nf - 1,)),
    ]
    here = pl.BlockSpec(memory_space=pltpu.VMEM)
    there = pl.BlockSpec(memory_space=pl.ANY)
    results = pl.pallas_call(
        functools.partial(kernel, torus),
        out_shape=[vmem(shape, F32) for shape in shapes],
        in_specs=[there] * 6,
        out_specs=[here] * 5,
        scratch_shapes=scratch,
        compiler_params=pltpu.CompilerParams(collective_id=0, has_side_effects=True),
    )(res_re, res_im, basis_re, basis_im, lengths.reshape(1, rows), pivots.reshape(1, emb // 2))
    coef_re, coef_im, new_re, new_im, err = pl.pallas_call(
        handed_out,
        out_shape=[jax.ShapeDtypeStruct(shape, F32) for shape in shapes],
        in_specs=[here] * 5,
        out_specs=[there] * 5,
        scratch_shapes=[dma((5,))],
    )(*[pltpu.with_memory_space_constraint(result, pltpu.VMEM) for result in results])
    return coef_re, coef_im, new_re, new_im, err.reshape(rows)


def build(mesh, torus):
    axes = Mesh(mesh.devices.reshape(torus), AXES)
    wave, freq = ("x", "y"), ("z", "core")
    in_specs = (P(wave, freq), P(wave, freq), P(None, freq), P(None, freq), P(wave), P())
    out_specs = (P(wave, None), P(wave, None), P(wave, freq), P(wave, freq), P(wave))
    return jax.shard_map(
        functools.partial(body, torus), mesh=axes, in_specs=in_specs, out_specs=out_specs, check_vma=False
    )


def solution(mesh):
    return build(mesh, TORUS)
```

```python
import functools

import jax
import jax.numpy as jnp
from jax import lax
from jax.experimental import pallas as pl
from jax.experimental.pallas import tpu as pltpu
from jax.sharding import Mesh
from jax.sharding import PartitionSpec as P

BIN_BLOCK = 128
NS_STEPS = 6
EPSILON = 1e-06
TORUS = (4, 8, 8, 2)
AXES = ("x", "y", "z", "core")
F32 = jnp.float32
BF16 = jnp.bfloat16


def dot(left, right, dims):
    return lax.dot_general(left, right, (dims, ((), ())), preferred_element_type=F32)


NN = ((1,), (0,))
NT = ((1,), (1,))


def halves(a):
    high = a.astype(BF16)
    return high, (a - high.astype(F32)).astype(BF16)


def thirds(a):
    high = a.astype(BF16)
    rest = a - high.astype(F32)
    mid = rest.astype(BF16)
    return high, mid, (rest - mid.astype(F32)).astype(BF16)


def product(left, right, dims):
    lh, ll = left
    rh, rl = right
    along = dims[1][0]
    return dot(jnp.concatenate([lh, ll, lh], axis=1), jnp.concatenate([rh, rh, rl], axis=along), dims)


def chosen(select, a):
    parts = thirds(a)
    return dot(jnp.concatenate([select] * 3, axis=1), jnp.concatenate(parts, axis=0), NN)


def swapped(a, part, axis):
    n = a.shape[axis]
    return jnp.where(part == 0, pltpu.roll(a, n - 4, axis), pltpu.roll(a, 4, axis))


def short_product(chunk, rights, dims):
    high = chunk.astype(BF16).astype(F32)
    both = jnp.concatenate([high, chunk - high], axis=0).astype(BF16)
    out = []
    for rh, rl in rights:
        a = dot(both, rh, dims)
        b = dot(both, rl, dims)
        out.append((a[:8] + a[8:]) + (b[:8] + b[8:]))
    return out


def kernel(
    torus,
    res_re, res_im, basis_re, basis_im, lens, piv,
    out_coef_re, out_coef_im, out_new_re, out_new_im, out_err,
    live, live_h, basis, base, vlen, vpiv, picked, far, relay, near, ysum, yr, kout, kin, pall, kall, wt,
    coef_re, coef_im, new_re, new_im, err,
    xpart, xpair, xhalf, xin, xfull,
    gpart, gpair, ghalf, gin, gfull, cpart, cpair, chalf, cin, cfull, dpart, dpair, dhalf, din, eout, ein,
    in_s, rx_s, rx_r, ry_s, ry_r, k_s, k_r, p_s, p_r, py_s, py_r, px_s, px_r, pr_s, pr_r,
    kg_s, kg_r, zs_s, zs_r, zg_s, zg_r, c_s, c_r, e_s, e_r, out_s,
):
    nx, ny, nz, nc = torus
    x, y, z, c = (lax.axis_index(a) for a in AXES)
    f = z * nc + c
    rows, bins = res_re.shape
    emb = 8 * nx * ny
    npiv = emb // 2
    nb = basis_re.shape[0]
    span = 8 * ny
    right, left = lax.rem(x + 1, nx), lax.rem(x + nx - 1, nx)
    across = lax.rem(x + 2, nx)


    def hops(d, n):
        return min(d, n - d)

    ys = [(d - 1, lax.rem(y + d, ny)) for d in sorted(range(1, ny), key=lambda d: -hops(d, ny))]
    zs = [(d - 1, lax.rem(z + d, nz)) for d in sorted(range(1, nz), key=lambda d: -hops(d, nz))]
    fs = sorted(((dz, dc) for dz in range(nz) for dc in range(nc) if dz or dc), key=lambda d: -hops(d[0], nz))
    fs = [(dz * nc + dc - 1, (x, y, lax.rem(z + dz, nz), lax.rem(c + dc, nc))) for dz, dc in fs]
    plane = sorted(
        ((dx, dy) for dx in range(nx) for dy in range(ny) if dx or dy),
        key=lambda d: -hops(d[0], nx) - hops(d[1], ny),
    )
    plane = [(dx * ny + dy - 1, (lax.rem(x + dx, nx), lax.rem(y + dy, ny), z, c)) for dx, dy in plane]

    loads = [(lens, vlen), (piv, vpiv), (res_re, live.at[:, pl.ds(0, bins)]), (res_im, live.at[:, pl.ds(bins, bins)])]
    loads += [(basis_re, basis.at[0]), (basis_im, basis.at[1])]
    loads = [pltpu.make_async_copy(src, dst, in_s.at[i]) for i, (src, dst) in enumerate(loads)]
    for load in loads:
        load.start()
    barrier = pltpu.get_barrier_semaphore()
    peers = [to for _, to in fs + plane]
    for peer in peers:
        pl.semaphore_signal(barrier, inc=1, device_id=peer, device_id_type=pl.DeviceIdType.MESH)

    started = []

    def push(src, dst, send, recv, to):
        copy = pltpu.make_async_remote_copy(
            src_ref=src, dst_ref=dst, send_sem=send, recv_sem=recv, device_id=to,
            device_id_type=pl.DeviceIdType.MESH,
        )
        copy.start()
        started.append(copy)
        return copy

    def arrived(copies):
        for copy in copies:
            copy.wait_recv()

    def chunk_of(i, size):
        return pl.ds(pl.multiple_of(i * size, size), size)

    for load in loads[:4]:
        load.wait()
    diagonal = lax.broadcasted_iota(jnp.int32, (rows, rows), 0) == lax.broadcasted_iota(jnp.int32, (rows, rows), 1)
    ends = jnp.sum(jnp.where(diagonal, vlen[...] * BIN_BLOCK, 0).astype(F32), axis=1, keepdims=True)
    first_bin = f * bins

    def mask_of(part):
        count = part.stop - part.start
        at = first_bin + lax.broadcasted_iota(jnp.int32, (count, bins), 1)
        return (at.astype(F32) < ends[part, :]).astype(F32)

    blocks = [slice(r, min(r + 64, rows)) for r in range(0, rows, 64)]
    for part in blocks:
        mask = mask_of(part)
        live[part, :bins] = live[part, :bins] * mask
        live[part, bins:] = live[part, bins:] * mask
    to_row = lax.broadcasted_iota(jnp.int32, (emb, npiv), 0)
    of_row = lax.broadcasted_iota(jnp.int32, (emb, npiv), 1) == (to_row // 8) * 4 + lax.rem(to_row, 4)
    wanted = jnp.sum(jnp.where(of_row, vpiv[...], 0).astype(F32), axis=1, keepdims=True)
    own = (x * ny + y) * rows + lax.broadcasted_iota(jnp.int32, (emb, rows), 1)
    select = (wanted == own.astype(F32)).astype(F32).astype(BF16)
    is_im = lax.rem(lax.broadcasted_iota(jnp.int32, (emb, bins), 0), 8) // 4
    picked[...] = jnp.where(is_im == 0, chosen(select, live[:, :bins]), chosen(select, live[:, bins:]))

    pl.semaphore_wait(barrier, len(peers))

    half = bins // 2
    ahead, behind = pl.ds(0, half), pl.ds(half, half)
    to_right, to_left = (right, y, z, c), (left, y, z, c)
    far_copies = [
        push(picked.at[chunk_of(across, span), ahead], far.at[0], rx_s.at[0], rx_r.at[0], to_right),
        push(picked.at[chunk_of(across, span), behind], far.at[1], rx_s.at[1], rx_r.at[1], to_left),
    ]
    near_copies = [
        push(picked.at[chunk_of(right, span), behind], near.at[0, :, behind], rx_s.at[2], rx_r.at[2], to_right),
        push(picked.at[chunk_of(left, span), ahead], near.at[1, :, ahead], rx_s.at[3], rx_r.at[3], to_left),
    ]

    for i, value in enumerate(halves(live[...])):
        live_h[i] = value
    for load in loads[4:]:
        load.wait()
    for i in range(2):
        high, low = halves(basis[i])
        base[2 * i] = high
        base[2 * i + 1] = low
    b_re = (base[0], base[1])
    b_im = (base[2], base[3])
    plus = jnp.concatenate([basis[0] + basis[1], basis[1] - basis[0]], axis=1)
    right_side = tuple(jnp.concatenate([base[i], base[2 + i]], axis=1) for i in range(2))
    both = product(halves(plus), right_side, NT)

    def scatter_rows(part, value):
        size = part.shape[2]
        for i in range(nc):
            for j in range(nz):
                at = (i * nz + j) * size
                part[i, j] = value[at : at + size]

    def pair_up(k, part, got):
        return push(part.at[1 - c], got, p_s.at[k], p_r.at[k], (x, y, z, 1 - c))

    def scatter(k, pair, part, got, summed, inward):
        arrived([pair])
        summed[...] = part[c] + got[...]
        return [push(summed.at[p], inward.at[i], zs_s.at[k, i], zs_r.at[k, i], (x, y, p, c)) for i, p in zs]

    def gathered(copies, summed, inward):
        arrived(copies)
        total = summed[z]
        for i in range(nz - 1):
            total = total + inward[i]
        return total

    def spread(k, total, full):
        full[c, z] = total
        return [push(full.at[c, z], full.at[c, z], zg_s.at[k, i], zg_r.at[k, i], (x, y, p, c)) for i, p in zs]

    def share(k, copies, full):
        arrived(copies)
        return push(full.at[c], full.at[c], c_s.at[k], c_r.at[k], (x, y, z, 1 - c))

    scatter_rows(xpart, both)
    x_pair = pair_up(0, xpart, xpair)
    turned_side = tuple(jnp.concatenate([-base[2 + i], base[i]], axis=1) for i in range(2))
    both = tuple(jnp.concatenate([right_side[i], turned_side[i]], axis=0) for i in range(2))
    scatter_rows(dpart, product((live_h[0], live_h[1]), both, NT))
    x_scatter = scatter(0, x_pair, xpart, xpair, xhalf, xin)
    d_pair = pair_up(3, dpart, dpair)

    arrived(far_copies[:1])
    relay[0] = picked[chunk_of(right, span), :half] + far[0]
    near_copies.append(push(relay.at[0], near.at[0, :, ahead], rx_s.at[4], rx_r.at[4], to_right))
    arrived(far_copies[1:])
    relay[1] = picked[chunk_of(left, span), half:] + far[1]
    near_copies.append(push(relay.at[1], near.at[1, :, behind], rx_s.at[5], rx_r.at[5], to_left))
    d_scatter = scatter(3, d_pair, dpart, dpair, dhalf, din)
    arrived(near_copies)
    ysum[...] = picked[chunk_of(x, span), :] + near[0] + near[1]
    y_copies = [
        push(ysum.at[chunk_of(p, 8)], yr.at[i], ry_s.at[i], ry_r.at[i], (x, p, z, c)) for i, p in ys
    ]
    x_spread = spread(0, gathered(x_scatter, xhalf, xin), xfull)
    arrived(y_copies)
    chunk = ysum[chunk_of(y, 8), :]
    for i in range(ny - 1):
        chunk = chunk + yr[i]

    mine = x * ny + y
    order = sorted(range(1, ny), key=lambda d: min(d, ny - d))

    def gather_steps(buf, ss, rs, wide):
        ysend, xsend, rsend = ss
        yrecv, xrecv, rrecv = rs
        lanes = (pl.ds(0, wide // 2), pl.ds(wide // 2, wide // 2))
        copies = {}

        def rows_of(i, d):
            return pl.ds(pl.multiple_of((i * ny + lax.rem(y + ny - d, ny)) * 8, 8), 8)

        def along_y():
            at = chunk_of(mine, 8)
            for i, p in ys:
                copies["y", i + 1] = push(buf.at[at], buf.at[at], ysend.at[i], yrecv.at[i], (x, p, z, c))

        def along_x(d):
            if d:
                arrived([copies["y", d]])
            at = rows_of(x, d)
            for k, to in enumerate((to_right, to_left)):
                copies["x", d, k] = push(buf.at[at], buf.at[at], xsend.at[d, k], xrecv.at[d, k], to)

        def further(d):
            for k, (source, to) in enumerate(((left, to_right), (right, to_left))):
                arrived([copies["x", d, k]])
                at = rows_of(source, d)
                copies["r", d, k] = push(
                    buf.at[at, lanes[k]], buf.at[at, lanes[k]], rsend.at[d, k], rrecv.at[d, k], to
                )

        def finish():
            arrived([copies["r", d, k] for d in range(ny) for k in range(2)])

        return along_y, along_x, further, finish

    pall[chunk_of(mine, 8), :] = chunk
    p_y, p_x, p_further, p_finish = gather_steps(pall, (py_s, px_s, pr_s), (py_r, px_r, pr_r), bins)
    p_y()
    p_x(0)
    sign_k = jnp.where(lax.broadcasted_iota(jnp.int32, (8, nb), 0) < 4, 1.0, -1.0).astype(F32)
    a, b = short_product(chunk, (b_re, b_im), NT)
    kout[...] = a + sign_k * pltpu.roll(b, 4, 0)
    k_copies = [push(kout, kin.at[i], k_s.at[i], k_r.at[i], to) for i, to in fs]
    x_last = share(0, x_spread, xfull)
    for d in order:
        p_x(d)
    late = [0] + order
    early, late = late[:3], late[3:]
    for d in early:
        p_further(d)
    arrived(k_copies)
    proj = kout[...]
    for i in range(len(fs)):
        proj = proj + kin[i]
    at = chunk_of(mine, 8)
    kall[at, :] = proj
    k_gather = [push(kall.at[at], kall.at[at], kg_s.at[i], kg_r.at[i], to) for i, to in plane]
    for d in late:
        p_further(d)
    p_finish()

    sign = jnp.where(is_im == 0, 1.0, -1.0).astype(F32)
    sign_all = jnp.where(
        lax.rem(lax.broadcasted_iota(jnp.int32, (emb, nb), 0), 8) < 4, 1.0, -1.0
    ).astype(F32)
    part_all = lax.rem(lax.broadcasted_iota(jnp.int32, (emb, nb), 0), 8) // 4

    def both_parts(a, signs, parts):
        return halves(jnp.concatenate([signs * a, swapped(a, parts, 0)], axis=1))

    for i, value in enumerate(both_parts(pall[...], sign, is_im)):
        wt[i] = value
    to_row = lax.broadcasted_iota(jnp.int32, (npiv, emb), 0)
    from_row = lax.broadcasted_iota(jnp.int32, (npiv, emb), 1)
    real_row = (to_row // 4) * 8 + lax.rem(to_row, 4)
    take_real = (from_row == real_row).astype(F32).astype(BF16)
    take_imag = (from_row == real_row + 4).astype(F32).astype(BF16)
    w = (wt[0], wt[1])
    top = tuple(dot(take_real, part, NN).astype(BF16) for part in w)
    scatter_rows(gpart, product(top, w, NT))
    g_pair = pair_up(1, gpart, gpair)
    scatter_rows(cpart, product((live_h[0], live_h[1]), w, NT))
    c_pair = pair_up(2, cpart, cpair)

    g_scatter = scatter(1, g_pair, gpart, gpair, ghalf, gin)
    c_scatter = scatter(2, c_pair, cpart, cpair, chalf, cin)
    arrived([x_last])
    arrived(k_gather)

    inner = halves(xfull[...].reshape(nb, nb))

    def times_inner(a):
        both = halves(a)
        straight, across = product(both, inner, NN), product(both, inner, NT)
        return 0.5 * ((straight + across) - sign_all * swapped(straight - across, part_all, 0))

    taken = 2.0 * kall[...] - times_inner(kall[...])
    rest = both_parts(kall[...] - times_inner(taken), sign_all, part_all)
    k_both = both_parts(kall[...], sign_all, part_all)
    t_both = both_parts(taken, sign_all, part_all)
    less = product(t_both, k_both, NT) + product(rest, t_both, NT)
    g_spread = spread(1, gathered(g_scatter, ghalf, gin), gfull)
    kept = gathered(d_scatter, dhalf, din)
    total = gathered(c_scatter, chalf, cin)
    c_spread = spread(2, total - product(halves(kept), t_both, NT), cfull)
    taken = halves(taken)
    back = product(taken, b_re, NN) - sign * swapped(product(taken, b_im, NN), is_im, 0)
    for i, value in enumerate(both_parts(pall[...] - back, sign, is_im)):
        wt[i] = value
    w = (wt[0], wt[1])
    g_last = share(1, g_spread, gfull)
    arrived([g_last])

    gram = gfull[...].reshape(npiv, emb)
    col_part = lax.rem(lax.broadcasted_iota(jnp.int32, (npiv, emb), 1), 8) // 4
    turned = jnp.where(col_part == 0, -1.0, 1.0).astype(F32) * swapped(gram, col_part, 1)
    place = jnp.concatenate([take_real, take_imag], axis=0)
    parts = thirds(jnp.concatenate([gram, turned], axis=0))
    gram = sum(dot(place, part, ((0,), (0,))) for part in parts) - less
    eye = lax.broadcasted_iota(jnp.int32, (emb, emb), 0) == lax.broadcasted_iota(jnp.int32, (emb, emb), 1)
    ident = eye.astype(F32)
    diag = gram * ident
    scale_col = 1.0 / jnp.sqrt(jnp.sum(diag, axis=1, keepdims=True) + EPSILON)
    scale_row = 1.0 / jnp.sqrt(jnp.sum(diag, axis=0, keepdims=True) + EPSILON)
    gram = gram * (scale_col * scale_row)
    bound = jnp.max(jnp.sum(jnp.abs(gram), axis=1, keepdims=True), axis=0, keepdims=True)
    your = gram / bound
    zed = None
    for step in range(NS_STEPS):
        if step == 3:
            c_last = share(2, c_spread, cfull)
        yh = halves(your)
        mix = your if zed is None else product(halves(zed), yh, NN)
        s = 1.5 * ident - 0.5 * mix
        sh = halves(s)
        if step < NS_STEPS - 1:
            your = product(yh, sh, NN)
        zed = s if zed is None else product(sh, halves(zed), NN)
    zed = zed * (1.0 / jnp.sqrt(bound))

    zed_out = tuple(dot(place, part, NN).astype(BF16) for part in halves(zed))
    block = product(halves((zed_out[0].astype(F32) + zed_out[1].astype(F32)) * scale_row), w, NN)
    block = halves(block)
    arrived([c_last])
    cross = cfull[...].reshape(rows, emb)
    coef = product(halves(cross * scale_row), zed_out, NT)
    coef_re[...] = coef[:, :npiv]
    coef_im[...] = coef[:, npiv:]
    sums = []
    for part in blocks:
        mask = mask_of(part)
        back = product(halves(coef[part, :]), block, NN)
        real = (live[part, :bins] - back[:, :bins]) * mask
        imag = (live[part, bins:] - back[:, bins:]) * mask
        new_re[part, :] = real
        new_im[part, :] = imag
        square = real * real + imag * imag
        sums.append(sum(square[:, i : i + 128] for i in range(0, bins, 128)))
    ones = jnp.ones((8, 128), BF16)
    summed = sum(dot(ones, part, NT) for part in thirds(jnp.concatenate(sums, axis=0)))
    eout[...] = summed[0:1, :]
    ein[f] = summed[0:1, :]
    copies = [push(eout, ein.at[f], e_s.at[i], e_r.at[i], to) for i, to in fs]
    results = [(coef_re, out_coef_re), (coef_im, out_coef_im), (new_re, out_new_re), (new_im, out_new_im), (err, out_err)]
    results = [pltpu.make_async_copy(src, dst, out_s.at[i]) for i, (src, dst) in enumerate(results)]
    for result in results[:4]:
        result.start()
    arrived(copies)
    total = ein[0]
    for i in range(1, nz * nc):
        total = total + ein[i]
    err[...] = total / (BIN_BLOCK * vlen[...]).astype(F32)
    results[4].start()

    for copy in started:
        copy.wait_send()
    for result in results:
        result.wait()


def handed_out(*refs):
    count = len(refs) // 2
    copies = [pltpu.make_async_copy(refs[i], refs[count + i], refs[-1].at[i]) for i in range(count)]
    for copy in copies:
        copy.start()
    for copy in copies:
        copy.wait()


def body(torus, res_re, res_im, basis_re, basis_im, lengths, pivots):
    nx, ny, nz, nc = torus
    rows, bins = res_re.shape
    nb = basis_re.shape[0]
    emb = 8 * nx * ny
    nf = nz * nc
    span = 8 * ny
    vmem = pltpu.VMEM
    dma = pltpu.SemaphoreType.DMA
    shapes = [(rows, emb // 2), (rows, emb // 2), (rows, bins), (rows, bins), (1, rows)]

    def summed(count, width):
        part = count // nf
        whole, across = vmem((nc, nz, part, width), F32), vmem((nz, part, width), F32)
        return [whole, across, across, vmem((nz - 1, part, width), F32), whole]

    scratch = [
        vmem((rows, 2 * bins), F32),
        vmem((2, rows, 2 * bins), BF16),
        vmem((2, nb, bins), F32),
        vmem((4, nb, bins), BF16),
        vmem((1, rows), jnp.int32),
        vmem((1, emb // 2), jnp.int32),
        vmem((emb, bins), F32),
        vmem((2, span, bins // 2), F32),
        vmem((2, span, bins // 2), F32),
        vmem((2, span, bins), F32),
        vmem((span, bins), F32),
        vmem((ny - 1, 8, bins), F32),
        vmem((8, nb), F32),
        vmem((nf - 1, 8, nb), F32),
        vmem((emb, bins), F32),
        vmem((emb, nb), F32),
        vmem((2, emb, 2 * bins), BF16),
        *[vmem(shape, F32) for shape in shapes],
        *summed(nb, nb),
        *summed(emb // 2, emb),
        *summed(rows, emb),
        *summed(rows, 2 * nb)[:4],
        vmem((1, rows), F32), vmem((nf, 1, rows), F32),
        dma((6,)), dma((6,)), dma((6,)), dma((ny - 1,)), dma((ny - 1,)), dma((nf - 1,)), dma((nf - 1,)),
        dma((4,)), dma((4,)),
        dma((ny - 1,)), dma((ny - 1,)), dma((ny, 2)), dma((ny, 2)), dma((ny, 2)), dma((ny, 2)),
        dma((nx * ny - 1,)), dma((nx * ny - 1,)),
        dma((4, nz - 1)), dma((4, nz - 1)), dma((3, nz - 1)), dma((3, nz - 1)), dma((3,)), dma((3,)),
        dma((nf - 1,)), dma((nf - 1,)), dma((5,)),
    ]
    here = pl.BlockSpec(memory_space=pltpu.VMEM)
    there = pl.BlockSpec(memory_space=pl.ANY)
    results = pl.pallas_call(
        functools.partial(kernel, torus),
        out_shape=[vmem(shape, F32) for shape in shapes],
        in_specs=[there] * 6,
        out_specs=[there] * 5,
        scratch_shapes=scratch,
        compiler_params=pltpu.CompilerParams(collective_id=0, has_side_effects=True),
    )(res_re, res_im, basis_re, basis_im, lengths.reshape(1, rows), pivots.reshape(1, emb // 2))
    coef_re, coef_im, new_re, new_im, err = pl.pallas_call(
        handed_out,
        out_shape=[jax.ShapeDtypeStruct(shape, F32) for shape in shapes],
        in_specs=[here] * 5,
        out_specs=[there] * 5,
        scratch_shapes=[dma((5,))],
    )(*[pltpu.with_memory_space_constraint(result, pltpu.VMEM) for result in results])
    return coef_re, coef_im, new_re, new_im, err.reshape(rows)


def build(mesh, torus):
    axes = Mesh(mesh.devices.reshape(torus), AXES)
    wave, freq = ("x", "y"), ("z", "core")
    in_specs = (P(wave, freq), P(wave, freq), P(None, freq), P(None, freq), P(wave), P())
    out_specs = (P(wave, None), P(wave, None), P(wave, freq), P(wave, freq), P(wave))
    return jax.shard_map(
        functools.partial(body, torus), mesh=axes, in_specs=in_specs, out_specs=out_specs, check_vma=False
    )


def solution(mesh):
    return build(mesh, TORUS)
```

```python
import functools

import jax
import jax.numpy as jnp
from jax import lax
from jax.experimental import pallas as pl
from jax.experimental.pallas import tpu as pltpu
from jax.sharding import Mesh
from jax.sharding import PartitionSpec as P

BIN_BLOCK = 128
NS_STEPS = 6
EPSILON = 1e-06
TORUS = (4, 8, 8, 2)
AXES = ("x", "y", "z", "core")
F32 = jnp.float32
BF16 = jnp.bfloat16


def dot(left, right, dims):
    return lax.dot_general(left, right, (dims, ((), ())), preferred_element_type=F32)


NN = ((1,), (0,))
NT = ((1,), (1,))


def halves(a):
    high = a.astype(BF16)
    return high, (a - high.astype(F32)).astype(BF16)


def thirds(a):
    high = a.astype(BF16)
    rest = a - high.astype(F32)
    mid = rest.astype(BF16)
    return high, mid, (rest - mid.astype(F32)).astype(BF16)


def product(left, right, dims):
    lh, ll = left
    rh, rl = right
    along = dims[1][0]
    return dot(jnp.concatenate([lh, ll, lh], axis=1), jnp.concatenate([rh, rh, rl], axis=along), dims)


def chosen(select, a):
    parts = thirds(a)
    return dot(jnp.concatenate([select] * 3, axis=1), jnp.concatenate(parts, axis=0), NN)


def swapped(a, part, axis):
    n = a.shape[axis]
    return jnp.where(part == 0, pltpu.roll(a, n - 4, axis), pltpu.roll(a, 4, axis))


def short_product(chunk, rights, dims):
    high = chunk.astype(BF16).astype(F32)
    both = jnp.concatenate([high, chunk - high], axis=0).astype(BF16)
    out = []
    for rh, rl in rights:
        a = dot(both, rh, dims)
        b = dot(both, rl, dims)
        out.append((a[:8] + a[8:]) + (b[:8] + b[8:]))
    return out


def kernel(
    torus,
    res_re, res_im, basis_re, basis_im, lens, piv,
    out_coef_re, out_coef_im, out_new_re, out_new_im, out_err,
    live, live_h, basis, base, vlen, vpiv, picked, far, relay, near, ysum, yr, kout, kin, pall, kall, wt,
    coef_re, coef_im, new_re, new_im, err,
    xpart, xpair, xhalf, xin, xfull, gpart, gin, gfull, kspan,
    cpart, cpair, chalf, cin, cfull, dpart, dpair, dhalf, din, eout, ein,
    in_s, rf_s, rf_r, rn_s, rn_r, rr_s, rr_r, ry_s, ry_r, k_s, k_r, p_s, p_r, py_s, py_r, px_s, px_r, pr_s, pr_r,
    kg_s, kg_r, zs_s, zs_r, zg_s, zg_r, c_s, c_r, g_s, g_r, e_s, e_r, out_s,
):
    nx, ny, nz, nc = torus
    x, y, z, c = (lax.axis_index(a) for a in AXES)
    f = z * nc + c
    rows, bins = res_re.shape
    emb = 8 * nx * ny
    npiv = emb // 2
    nb = basis_re.shape[0]
    span = 8 * ny
    right, left = lax.rem(x + 1, nx), lax.rem(x + nx - 1, nx)
    across = lax.rem(x + 2, nx)


    def hops(d, n):
        return min(d, n - d)

    ys = [(d - 1, lax.rem(y + d, ny)) for d in sorted(range(1, ny), key=lambda d: -hops(d, ny))]
    zs = [(d - 1, lax.rem(z + d, nz)) for d in sorted(range(1, nz), key=lambda d: -hops(d, nz))]
    fs = sorted(((dz, dc) for dz in range(nz) for dc in range(nc) if dz or dc), key=lambda d: -hops(d[0], nz))
    fs = [(dz * nc + dc - 1, (x, y, lax.rem(z + dz, nz), lax.rem(c + dc, nc))) for dz, dc in fs]
    plane = sorted(
        ((dx, dy) for dx in range(nx) for dy in range(ny) if dx or dy),
        key=lambda d: -hops(d[0], nx) - hops(d[1], ny),
    )
    plane = [(dx * ny + dy - 1, (lax.rem(x + dx, nx), lax.rem(y + dy, ny), z, c)) for dx, dy in plane]

    loads = [(lens, vlen), (piv, vpiv), (res_re, live.at[:, pl.ds(0, bins)]), (res_im, live.at[:, pl.ds(bins, bins)])]
    loads += [(basis_re, basis.at[0]), (basis_im, basis.at[1])]
    loads = [pltpu.make_async_copy(src, dst, in_s.at[i]) for i, (src, dst) in enumerate(loads)]
    for load in loads:
        load.start()
    barrier = pltpu.get_barrier_semaphore()
    peers = [to for _, to in fs + plane]
    for peer in peers:
        pl.semaphore_signal(barrier, inc=1, device_id=peer, device_id_type=pl.DeviceIdType.MESH)

    started = []
    to_right, to_left = (right, y, z, c), (left, y, z, c)

    def push(src, dst, send, recv, to):
        copy = pltpu.make_async_remote_copy(
            src_ref=src, dst_ref=dst, send_sem=send, recv_sem=recv, device_id=to,
            device_id_type=pl.DeviceIdType.MESH,
        )
        copy.start()
        started.append(copy)
        return copy

    def arrived(copies):
        for copy in copies:
            copy.wait_recv()

    finals = []

    def fan(pairs, send, recv, extent):
        for src, dst, to in pairs:
            pltpu.make_async_remote_copy(
                src_ref=src, dst_ref=dst, send_sem=send, recv_sem=recv, device_id=to,
                device_id_type=pl.DeviceIdType.MESH,
            ).start()
        whole = pltpu.make_async_remote_copy(
            src_ref=extent, dst_ref=extent, send_sem=send, recv_sem=recv, device_id=to_right,
            device_id_type=pl.DeviceIdType.MESH,
        )
        finals.append(whole)
        return whole

    def chunk_of(i, size):
        return pl.ds(pl.multiple_of(i * size, size), size)

    for load in loads[:4]:
        load.wait()
    diagonal = lax.broadcasted_iota(jnp.int32, (rows, rows), 0) == lax.broadcasted_iota(jnp.int32, (rows, rows), 1)
    ends = jnp.sum(jnp.where(diagonal, vlen[...] * BIN_BLOCK, 0).astype(F32), axis=1, keepdims=True)
    first_bin = f * bins

    def mask_of(part):
        count = part.stop - part.start
        at = first_bin + lax.broadcasted_iota(jnp.int32, (count, bins), 1)
        return (at.astype(F32) < ends[part, :]).astype(F32)

    blocks = [slice(r, min(r + 64, rows)) for r in range(0, rows, 64)]
    for part in blocks:
        mask = mask_of(part)
        live[part, :bins] = live[part, :bins] * mask
        live[part, bins:] = live[part, bins:] * mask
    to_row = lax.broadcasted_iota(jnp.int32, (emb, npiv), 0)
    of_row = lax.broadcasted_iota(jnp.int32, (emb, npiv), 1) == (to_row // 8) * 4 + lax.rem(to_row, 4)
    wanted = jnp.sum(jnp.where(of_row, vpiv[...], 0).astype(F32), axis=1, keepdims=True)
    own = (x * ny + y) * rows + lax.broadcasted_iota(jnp.int32, (emb, rows), 1)
    select = (wanted == own.astype(F32)).astype(F32).astype(BF16)
    is_im = lax.rem(lax.broadcasted_iota(jnp.int32, (emb, bins), 0), 8) // 4
    picked[...] = jnp.where(is_im == 0, chosen(select, live[:, :bins]), chosen(select, live[:, bins:]))

    pl.semaphore_wait(barrier, len(peers))

    half, piece = bins // 2, span // 2
    ahead, behind = pl.ds(0, half), pl.ds(half, half)
    ways = ((to_right, right, ahead), (to_left, left, behind))
    far_copies = []
    for i in range(2):
        for k, (to, _, lanes) in enumerate(ways):
            at = pl.ds(pl.multiple_of(across * span + i * piece, piece), piece)
            far_copies.append(
                push(picked.at[at, lanes], far.at[k, pl.ds(i * piece, piece)], rf_s.at[i, k], rf_r.at[i, k], to)
            )

    for i, value in enumerate(halves(live[...])):
        live_h[i] = value
    for load in loads[4:]:
        load.wait()
    for i in range(2):
        high, low = halves(basis[i])
        base[2 * i] = high
        base[2 * i + 1] = low
    b_re = (base[0], base[1])
    b_im = (base[2], base[3])
    plus = jnp.concatenate([basis[0] + basis[1], basis[1] - basis[0]], axis=1)
    right_side = tuple(jnp.concatenate([base[i], base[2 + i]], axis=1) for i in range(2))
    both = product(halves(plus), right_side, NT)

    def scatter_rows(part, value):
        size = part.shape[2]
        for i in range(nc):
            for j in range(nz):
                at = (i * nz + j) * size
                part[i, j] = value[at : at + size]

    def pair_up(k, part, got):
        return push(part.at[1 - c], got, p_s.at[k], p_r.at[k], (x, y, z, 1 - c))

    def scatter(k, pair, part, got, summed, inward):
        arrived([pair])
        summed[...] = part[c] + got[...]
        return fan([(summed.at[p], inward.at[i], (x, y, p, c)) for i, p in zs], zs_s.at[k], zs_r.at[k], inward)

    def gathered(copies, summed, inward):
        arrived([copies])
        total = summed[z]
        for i in range(nz - 1):
            total = total + inward[i]
        return total

    def spread(k, total, full, extent):
        full[c, z] = total
        at = full.at[c, z]
        return fan([(at, at, (x, y, p, c)) for i, p in zs], zg_s.at[k], zg_r.at[k], extent)

    def share(k, copies, full):
        arrived([copies])
        return push(full.at[c], full.at[c], c_s.at[k], c_r.at[k], (x, y, z, 1 - c))

    near_started = [
        (picked.at[chunk_of(next_x, span), other], near.at[k, :, other], to)
        for k, ((to, next_x, _), other) in enumerate(zip(ways, (behind, ahead)))
    ]
    near_begun = fan(near_started, rn_s.at[0], rn_r.at[0], far)
    scatter_rows(xpart, both)
    x_pair = pair_up(0, xpart, xpair)
    turned_side = tuple(jnp.concatenate([-base[2 + i], base[i]], axis=1) for i in range(2))
    both = tuple(jnp.concatenate([right_side[i], turned_side[i]], axis=0) for i in range(2))
    scatter_rows(dpart, product((live_h[0], live_h[1]), both, NT))
    x_scatter = scatter(0, x_pair, xpart, xpair, xhalf, xin)
    d_pair = pair_up(2, dpart, dpair)

    relays = []
    for i in range(2):
        for k, (to, next_x, lanes) in enumerate(ways):
            arrived([far_copies[2 * i + k]])
            at = pl.ds(pl.multiple_of(next_x * span + i * piece, piece), piece)
            part = pl.ds(i * piece, piece)
            relay[k, i * piece : (i + 1) * piece] = (
                picked[at, k * half : (k + 1) * half] + far[k, i * piece : (i + 1) * piece]
            )
            relays.append(push(relay.at[k, part], near.at[k, part, lanes], rr_s.at[i, k], rr_r.at[i, k], to))
    d_scatter = scatter(2, d_pair, dpart, dpair, dhalf, din)
    arrived([near_begun, *relays])
    ysum[...] = picked[chunk_of(x, span), :] + near[0] + near[1]
    y_copies = fan([(ysum.at[chunk_of(p, 8)], yr.at[i], (x, p, z, c)) for i, p in ys], ry_s.at[0], ry_r.at[0], yr)
    x_spread = spread(0, gathered(x_scatter, xhalf, xin), xfull, xin)
    arrived([y_copies])
    chunk = ysum[chunk_of(y, 8), :]
    for i in range(ny - 1):
        chunk = chunk + yr[i]

    mine = x * ny + y
    order = sorted(range(1, ny), key=lambda d: min(d, ny - d))

    def gather_steps(buf, ss, rs, wide):
        ysend, xsend, rsend = ss
        yrecv, xrecv, rrecv = rs
        lanes = (pl.ds(0, wide // 2), pl.ds(wide // 2, wide // 2))
        copies = {}

        extents = []

        def rows_of(i, d):
            return pl.ds(pl.multiple_of((i * ny + lax.rem(y + ny - d, ny)) * 8, 8), 8)

        def along_y():
            at = chunk_of(mine, 8)
            for i, p in ys:
                copies["y", i + 1] = push(buf.at[at], buf.at[at], ysend.at[i], yrecv.at[i], (x, p, z, c))

        def along_x(d):
            if d:
                arrived([copies["y", d]])
            at = rows_of(x, d)
            for k, to in enumerate((to_right, to_left)):
                copies["x", d, k] = push(buf.at[at], buf.at[at], xsend.at[d, k], xrecv.at[d, k], to)

        def further(d):
            for k, (source, to) in enumerate(((left, to_right), (right, to_left))):
                arrived([copies["x", d, k]])
                at = rows_of(source, d)
                copies["r", d, k] = push(
                    buf.at[at, lanes[k]], buf.at[at, lanes[k]], rsend.at[d, k], rrecv.at[d, k], to
                )

        def finish():
            arrived([copies["r", d, k] for d in range(ny) for k in range(2)])

        return along_y, along_x, further, finish

    pall[chunk_of(mine, 8), :] = chunk
    p_y, p_x, p_further, p_finish = gather_steps(pall, (py_s, px_s, pr_s), (py_r, px_r, pr_r), bins)
    p_y()
    p_x(0)
    sign_k = jnp.where(lax.broadcasted_iota(jnp.int32, (8, nb), 0) < 4, 1.0, -1.0).astype(F32)
    a, b = short_product(chunk, (b_re, b_im), NT)
    kout[...] = a + sign_k * pltpu.roll(b, 4, 0)
    k_copies = fan([(kout, kin.at[i], to) for i, to in fs], k_s.at[0], k_r.at[0], kin)
    for d in order:
        p_x(d)
    late = [0] + order
    early, late = late[:3], late[3:]
    for d in early:
        p_further(d)
    arrived([k_copies])
    proj = kout[...]
    for i in range(len(fs)):
        proj = proj + kin[i]
    at = chunk_of(mine, 8)
    kall[at, :] = proj
    k_gather = fan([(kall.at[at], kall.at[at], to) for i, to in plane], kg_s.at[0], kg_r.at[0], kspan)
    for d in late:
        p_further(d)
    p_finish()

    sign = jnp.where(is_im == 0, 1.0, -1.0).astype(F32)
    sign_all = jnp.where(
        lax.rem(lax.broadcasted_iota(jnp.int32, (emb, nb), 0), 8) < 4, 1.0, -1.0
    ).astype(F32)
    part_all = lax.rem(lax.broadcasted_iota(jnp.int32, (emb, nb), 0), 8) // 4

    def both_parts(a, signs, parts):
        return halves(jnp.concatenate([signs * a, swapped(a, parts, 0)], axis=1))

    for i, value in enumerate(both_parts(pall[...], sign, is_im)):
        wt[i] = value
    to_row = lax.broadcasted_iota(jnp.int32, (npiv, emb), 0)
    from_row = lax.broadcasted_iota(jnp.int32, (npiv, emb), 1)
    real_row = (to_row // 4) * 8 + lax.rem(to_row, 4)
    take_real = (from_row == real_row).astype(F32).astype(BF16)
    take_imag = (from_row == real_row + 4).astype(F32).astype(BF16)
    w = (wt[0], wt[1])
    top = tuple(dot(take_real, part, NN).astype(BF16) for part in w)
    gram = product(top, w, NT)
    for i in range(nz * nc):
        gpart[i] = gram[i * gpart.shape[1] : (i + 1) * gpart.shape[1]]
    g_scatter = fan([(gpart.at[to[2] * nc + to[3]], gin.at[i], to) for i, to in fs], g_s.at[0], g_r.at[0], gin)
    x_last = share(0, x_spread, xfull)
    scatter_rows(cpart, product((live_h[0], live_h[1]), w, NT))
    c_pair = pair_up(1, cpart, cpair)

    c_scatter = scatter(1, c_pair, cpart, cpair, chalf, cin)
    arrived([g_scatter])
    total = gpart[f]
    for i in range(len(fs)):
        total = total + gin[i]
    gfull[f] = total
    g_gather = fan([(gfull.at[f], gfull.at[f], to) for _, to in fs], g_s.at[1], g_r.at[1], gin)
    arrived([x_last])
    arrived([k_gather])

    inner = halves(xfull[...].reshape(nb, nb))

    def times_inner(a):
        both = halves(a)
        straight, across = product(both, inner, NN), product(both, inner, NT)
        return 0.5 * ((straight + across) - sign_all * swapped(straight - across, part_all, 0))

    taken = 2.0 * kall[...] - times_inner(kall[...])
    rest = both_parts(kall[...] - times_inner(taken), sign_all, part_all)
    k_both = both_parts(kall[...], sign_all, part_all)
    t_both = both_parts(taken, sign_all, part_all)
    less = product(t_both, k_both, NT) + product(rest, t_both, NT)
    kept = gathered(d_scatter, dhalf, din)
    total = gathered(c_scatter, chalf, cin)
    c_spread = spread(1, total - product(halves(kept), t_both, NT), cfull, cin)
    taken = halves(taken)
    back = product(taken, b_re, NN) - sign * swapped(product(taken, b_im, NN), is_im, 0)
    for i, value in enumerate(both_parts(pall[...] - back, sign, is_im)):
        wt[i] = value
    w = (wt[0], wt[1])
    arrived([g_gather])

    gram = gfull[...].reshape(npiv, emb)
    col_part = lax.rem(lax.broadcasted_iota(jnp.int32, (npiv, emb), 1), 8) // 4
    turned = jnp.where(col_part == 0, -1.0, 1.0).astype(F32) * swapped(gram, col_part, 1)
    place = jnp.concatenate([take_real, take_imag], axis=0)
    parts = thirds(jnp.concatenate([gram, turned], axis=0))
    gram = sum(dot(place, part, ((0,), (0,))) for part in parts) - less
    eye = lax.broadcasted_iota(jnp.int32, (emb, emb), 0) == lax.broadcasted_iota(jnp.int32, (emb, emb), 1)
    ident = eye.astype(F32)
    diag = gram * ident
    scale_col = 1.0 / jnp.sqrt(jnp.sum(diag, axis=1, keepdims=True) + EPSILON)
    scale_row = 1.0 / jnp.sqrt(jnp.sum(diag, axis=0, keepdims=True) + EPSILON)
    gram = gram * (scale_col * scale_row)
    bound = jnp.max(jnp.sum(jnp.abs(gram), axis=1, keepdims=True), axis=0, keepdims=True)
    your = gram / bound
    zed = None
    for step in range(NS_STEPS):
        if step == 3:
            c_last = share(1, c_spread, cfull)
        yh = halves(your)
        mix = your if zed is None else product(halves(zed), yh, NN)
        s = 1.5 * ident - 0.5 * mix
        sh = halves(s)
        if step < NS_STEPS - 1:
            your = product(yh, sh, NN)
        zed = s if zed is None else product(sh, halves(zed), NN)
    zed = zed * (1.0 / jnp.sqrt(bound))

    zed_out = tuple(dot(place, part, NN).astype(BF16) for part in halves(zed))
    arrived([c_last])
    cross = cfull[...].reshape(rows, emb)
    coef = product(halves(cross * scale_row), zed_out, NT)
    coef_re[...] = coef[:, :npiv]
    coef_im[...] = coef[:, npiv:]
    weights = halves((zed_out[0].astype(F32) + zed_out[1].astype(F32)) * scale_row)
    back = product(halves(product(halves(coef), weights, NN)), w, NN)
    sums = []
    for part in blocks:
        mask = mask_of(part)
        real = (live[part, :bins] - back[part, :bins]) * mask
        imag = (live[part, bins:] - back[part, bins:]) * mask
        new_re[part, :] = real
        new_im[part, :] = imag
        square = real * real + imag * imag
        sums.append(sum(square[:, i : i + 128] for i in range(0, bins, 128)))
    ones = jnp.ones((8, 128), BF16)
    summed = sum(dot(ones, part, NT) for part in thirds(jnp.concatenate(sums, axis=0)))
    eout[...] = summed[0:1, :]
    ein[f] = summed[0:1, :]
    e_copies = fan([(eout, ein.at[f], to) for _, to in fs], e_s.at[0], e_r.at[0], ein.at[pl.ds(0, len(fs))])
    results = [(coef_re, out_coef_re), (coef_im, out_coef_im), (new_re, out_new_re), (new_im, out_new_im), (err, out_err)]
    results = [pltpu.make_async_copy(src, dst, out_s.at[i]) for i, (src, dst) in enumerate(results)]
    for result in results[:4]:
        result.start()
    arrived([e_copies])
    total = ein[0]
    for i in range(1, nz * nc):
        total = total + ein[i]
    err[...] = total / (BIN_BLOCK * vlen[...]).astype(F32)
    results[4].start()

    for copy in started + finals:
        copy.wait_send()
    for result in results:
        result.wait()


def handed_out(*refs):
    count = len(refs) // 2
    copies = [pltpu.make_async_copy(refs[i], refs[count + i], refs[-1].at[i]) for i in range(count)]
    for copy in copies:
        copy.start()
    for copy in copies:
        copy.wait()


def body(torus, res_re, res_im, basis_re, basis_im, lengths, pivots):
    nx, ny, nz, nc = torus
    rows, bins = res_re.shape
    nb = basis_re.shape[0]
    emb = 8 * nx * ny
    nf = nz * nc
    span = 8 * ny
    vmem = pltpu.VMEM
    dma = pltpu.SemaphoreType.DMA
    shapes = [(rows, emb // 2), (rows, emb // 2), (rows, bins), (rows, bins), (1, rows)]

    def summed(count, width):
        part = count // nf
        whole, across = vmem((nc, nz, part, width), F32), vmem((nz, part, width), F32)
        return [whole, across, across, vmem((nz - 1, part, width), F32), whole]

    scratch = [
        vmem((rows, 2 * bins), F32),
        vmem((2, rows, 2 * bins), BF16),
        vmem((2, nb, bins), F32),
        vmem((4, nb, bins), BF16),
        vmem((1, rows), jnp.int32),
        vmem((1, emb // 2), jnp.int32),
        vmem((emb, bins), F32),
        vmem((2, span, bins // 2), F32),
        vmem((2, span, bins // 2), F32),
        vmem((2, span, bins), F32),
        vmem((span, bins), F32),
        vmem((ny - 1, 8, bins), F32),
        vmem((8, nb), F32),
        vmem((nf - 1, 8, nb), F32),
        vmem((emb, bins), F32),
        vmem((emb, nb), F32),
        vmem((2, emb, 2 * bins), BF16),
        *[vmem(shape, F32) for shape in shapes],
        *summed(nb, nb),
        vmem((nf, emb // 2 // nf, emb), F32), vmem((nf - 1, emb // 2 // nf, emb), F32), vmem((nf, emb // 2 // nf, emb), F32),
        vmem((nx * ny - 1, 8, nb), F32),
        *summed(rows, emb),
        *summed(rows, 2 * nb)[:4],
        vmem((1, rows), F32), vmem((nf, 1, rows), F32),
        dma((6,)),
        *[dma((2, 2))] * 2, *[dma((1,))] * 2, *[dma((2, 2))] * 2, *[dma((1,))] * 2, *[dma((1,))] * 2, *[dma((3,))] * 2,
        *[dma((ny - 1,))] * 2, *[dma((ny, 2))] * 4,
        *[dma((1,))] * 2, *[dma((3,))] * 2, *[dma((2,))] * 2, *[dma((2,))] * 2, *[dma((2,))] * 2, *[dma((1,))] * 2,
        dma((5,)),
    ]
    here = pl.BlockSpec(memory_space=pltpu.VMEM)
    there = pl.BlockSpec(memory_space=pl.ANY)
    results = pl.pallas_call(
        functools.partial(kernel, torus),
        out_shape=[vmem(shape, F32) for shape in shapes],
        in_specs=[there] * 6,
        out_specs=[there] * 5,
        scratch_shapes=scratch,
        compiler_params=pltpu.CompilerParams(collective_id=0, has_side_effects=True),
    )(res_re, res_im, basis_re, basis_im, lengths.reshape(1, rows), pivots.reshape(1, emb // 2))
    coef_re, coef_im, new_re, new_im, err = pl.pallas_call(
        handed_out,
        out_shape=[jax.ShapeDtypeStruct(shape, F32) for shape in shapes],
        in_specs=[here] * 5,
        out_specs=[there] * 5,
        scratch_shapes=[dma((5,))],
    )(*[pltpu.with_memory_space_constraint(result, pltpu.VMEM) for result in results])
    return coef_re, coef_im, new_re, new_im, err.reshape(rows)


def build(mesh, torus):
    axes = Mesh(mesh.devices.reshape(torus), AXES)
    wave, freq = ("x", "y"), ("z", "core")
    in_specs = (P(wave, freq), P(wave, freq), P(None, freq), P(None, freq), P(wave), P())
    out_specs = (P(wave, None), P(wave, None), P(wave, freq), P(wave, freq), P(wave))
    return jax.shard_map(
        functools.partial(body, torus), mesh=axes, in_specs=in_specs, out_specs=out_specs, check_vma=False
    )


def solution(mesh):
    return build(mesh, TORUS)
```

```python
import functools

import jax
import jax.numpy as jnp
from jax import lax
from jax.experimental import pallas as pl
from jax.experimental.pallas import tpu as pltpu
from jax.sharding import Mesh
from jax.sharding import PartitionSpec as P

BIN_BLOCK = 128
NS_STEPS = 6
EPSILON = 1e-06
TORUS = (4, 8, 8, 2)
AXES = ("x", "y", "z", "core")
F32 = jnp.float32
BF16 = jnp.bfloat16


def dot(left, right, dims):
    return lax.dot_general(left, right, (dims, ((), ())), preferred_element_type=F32)


NN = ((1,), (0,))
NT = ((1,), (1,))


def halves(a):
    high = a.astype(BF16)
    return high, (a - high.astype(F32)).astype(BF16)


def thirds(a):
    high = a.astype(BF16)
    rest = a - high.astype(F32)
    mid = rest.astype(BF16)
    return high, mid, (rest - mid.astype(F32)).astype(BF16)


def product(left, right, dims):
    lh, ll = left
    rh, rl = right
    along = dims[1][0]
    return dot(jnp.concatenate([lh, ll, lh], axis=1), jnp.concatenate([rh, rh, rl], axis=along), dims)


def chosen(select, a):
    parts = thirds(a)
    return dot(jnp.concatenate([select] * 3, axis=1), jnp.concatenate(parts, axis=0), NN)


def embedded(row):
    n = row.shape[1] // 2
    return jnp.concatenate([row, jnp.concatenate([-row[:, n:], row[:, :n]], axis=1)], axis=0)


def crossed(a, b):
    n = a.shape[0] // 2
    return jnp.concatenate([a[:n] - b[n:], a[n:] + b[:n]], axis=0)


def as_rows(a):
    n = a.shape[0] // 2
    return jnp.concatenate([a[:n], a[n:]], axis=1)


def short_product(chunk, rights, dims):
    high = chunk.astype(BF16).astype(F32)
    both = jnp.concatenate([high, chunk - high], axis=0).astype(BF16)
    out = []
    for rh, rl in rights:
        a = dot(both, rh, dims)
        b = dot(both, rl, dims)
        out.append((a[:8] + a[8:]) + (b[:8] + b[8:]))
    return out


def kernel(
    torus,
    res_re, res_im, basis_re, basis_im, lens, piv,
    out_coef_re, out_coef_im, out_new_re, out_new_im, out_err,
    live, live_h, basis, base, vlen, vpiv, picked, xr, ysum, yr, kout, kin, pall, kall, wt,
    coef_re, coef_im, new_re, new_im, err,
    xpart, xpair, xhalf, xin, xfull, gpart, gin, gfull, kspan,
    cpart, cpair, chalf, cin, cfull, dpart, dpair, dhalf, din, eout, ein,
    in_s, rx_s, rx_r, ry_s, ry_r, k_s, k_r, p_s, p_r, py_s, py_r, px_s, px_r, ky_s, ky_r, kx_s, kx_r,
    zs_s, zs_r, zg_s, zg_r, c_s, c_r, g_s, g_r, e_s, e_r, out_s,
):
    nx, ny, nz, nc = torus
    x, y, z, c = (lax.axis_index(a) for a in AXES)
    f = z * nc + c
    rows, bins = res_re.shape
    emb = 8 * nx * ny
    npiv = emb // 2
    nb = basis_re.shape[0]
    span = 8 * ny

    def hops(d, n):
        return min(d, n - d)

    xs = [(d - 1, lax.rem(x + d, nx)) for d in sorted(range(1, nx), key=lambda d: -hops(d, nx))]
    ys = [(d - 1, lax.rem(y + d, ny)) for d in sorted(range(1, ny), key=lambda d: -hops(d, ny))]
    zs = [(d - 1, lax.rem(z + d, nz)) for d in sorted(range(1, nz), key=lambda d: -hops(d, nz))]
    fs = sorted(((dz, dc) for dz in range(nz) for dc in range(nc) if dz or dc), key=lambda d: -hops(d[0], nz))
    fs = [(dz * nc + dc - 1, (x, y, lax.rem(z + dz, nz), lax.rem(c + dc, nc))) for dz, dc in fs]
    barrier = pltpu.get_barrier_semaphore()
    peers = [to for _, to in fs] + [(x, p, z, c) for _, p in ys] + [(p, y, z, c) for _, p in xs]
    for peer in peers:
        pl.semaphore_signal(barrier, inc=1, device_id=peer, device_id_type=pl.DeviceIdType.MESH)
    loads = [(lens, vlen), (piv, vpiv), (res_re, live.at[:, pl.ds(0, bins)]), (res_im, live.at[:, pl.ds(bins, bins)])]
    loads += [(basis_re, basis.at[0]), (basis_im, basis.at[1])]
    loads = [pltpu.make_async_copy(src, dst, in_s.at[i]) for i, (src, dst) in enumerate(loads)]
    for load in loads:
        load.start()

    started = []
    anyone = fs[0][1]

    def described(src, dst, send, recv, to):
        return pltpu.make_async_remote_copy(
            src_ref=src, dst_ref=dst, send_sem=send, recv_sem=recv, device_id=to,
            device_id_type=pl.DeviceIdType.MESH,
        )

    def begin(src, dst, send, recv, to):
        copy = described(src, dst, send, recv, to)
        copy.start()
        return copy

    def push(src, dst, send, recv, to):
        copy = begin(src, dst, send, recv, to)
        started.append(copy)
        return copy

    def arrived(copies):
        for copy in copies:
            copy.wait_recv()

    finals = []

    def fan(pairs, send, recv, extent):
        for src, dst, to in pairs:
            begin(src, dst, send, recv, to)
        whole = described(extent, extent, send, recv, anyone)
        finals.append(whole)
        return whole

    def chunk_of(i, size):
        return pl.ds(pl.multiple_of(i * size, size), size)

    for load in loads[:4]:
        load.wait()
    diagonal = lax.broadcasted_iota(jnp.int32, (rows, rows), 0) == lax.broadcasted_iota(jnp.int32, (rows, rows), 1)
    ends = jnp.sum(jnp.where(diagonal, vlen[...] * BIN_BLOCK, 0).astype(F32), axis=1, keepdims=True)
    first_bin = f * bins

    def mask_of(part):
        count = part.stop - part.start
        at = first_bin + lax.broadcasted_iota(jnp.int32, (count, bins), 1)
        return (at.astype(F32) < ends[part, :]).astype(F32)

    blocks = [slice(r, min(r + 64, rows)) for r in range(0, rows, 64)]
    for part in blocks:
        mask = mask_of(part)
        live[part, :bins] = live[part, :bins] * mask
        live[part, bins:] = live[part, bins:] * mask
    to_row = lax.broadcasted_iota(jnp.int32, (emb, npiv), 0)
    of_row = lax.broadcasted_iota(jnp.int32, (emb, npiv), 1) == lax.rem(to_row, 4) * (nx * ny) + to_row // 8
    wanted = jnp.sum(jnp.where(of_row, vpiv[...], 0).astype(F32), axis=1, keepdims=True)
    own = (x * ny + y) * rows + lax.broadcasted_iota(jnp.int32, (emb, rows), 1)
    select = (wanted == own.astype(F32)).astype(F32).astype(BF16)
    is_im = lax.rem(lax.broadcasted_iota(jnp.int32, (emb, bins), 0), 8) // 4
    picked[...] = jnp.where(is_im == 0, chosen(select, live[:, :bins]), chosen(select, live[:, bins:]))

    pl.semaphore_wait(barrier, len(peers))

    x_copies = fan([(picked.at[chunk_of(p, span)], xr.at[i], (p, y, z, c)) for i, p in xs], rx_s.at[0], rx_r.at[0], xr)

    for i, value in enumerate(halves(live[...])):
        live_h[i] = value
    for load in loads[4:]:
        load.wait()
    for i in range(2):
        high, low = halves(basis[i])
        base[2 * i] = high
        base[2 * i + 1] = low
    b_re = (base[0], base[1])
    b_im = (base[2], base[3])
    plus = jnp.concatenate([basis[0] + basis[1], basis[1] - basis[0]], axis=1)
    right_side = tuple(jnp.concatenate([base[i], base[2 + i]], axis=1) for i in range(2))
    both = product(halves(plus), right_side, NT)

    def scatter_rows(part, value):
        size = part.shape[2]
        for i in range(nc):
            for j in range(nz):
                at = (i * nz + j) * size
                part[i, j] = value[at : at + size]

    def pair_up(k, part, got):
        return push(part.at[1 - c], got, p_s.at[k], p_r.at[k], (x, y, z, 1 - c))

    def scatter(k, pair, part, got, summed, inward):
        arrived([pair])
        summed[...] = part[c] + got[...]
        return fan([(summed.at[p], inward.at[i], (x, y, p, c)) for i, p in zs], zs_s.at[k], zs_r.at[k], inward)

    def gathered(copies, summed, inward):
        arrived([copies])
        total = summed[z]
        for i in range(nz - 1):
            total = total + inward[i]
        return total

    def spread(k, total, full, extent):
        full[c, z] = total
        at = full.at[c, z]
        return fan([(at, at, (x, y, p, c)) for i, p in zs], zg_s.at[k], zg_r.at[k], extent)

    def share(k, copies, full):
        arrived([copies])
        return push(full.at[c], full.at[c], c_s.at[k], c_r.at[k], (x, y, z, 1 - c))

    scatter_rows(xpart, both)
    x_pair = pair_up(0, xpart, xpair)
    turned_side = tuple(jnp.concatenate([-base[2 + i], base[i]], axis=1) for i in range(2))
    both = tuple(jnp.concatenate([right_side[i], turned_side[i]], axis=0) for i in range(2))
    scatter_rows(dpart, product((live_h[0], live_h[1]), both, NT))
    x_scatter = scatter(0, x_pair, xpart, xpair, xhalf, xin)
    d_pair = pair_up(2, dpart, dpair)

    d_scatter = scatter(2, d_pair, dpart, dpair, dhalf, din)
    arrived([x_copies])
    total = picked[chunk_of(x, span), :]
    for i in range(nx - 1):
        total = total + xr[i]
    ysum[...] = total
    y_copies = fan([(ysum.at[chunk_of(p, 8)], yr.at[i], (x, p, z, c)) for i, p in ys], ry_s.at[0], ry_r.at[0], yr)
    arrived([y_copies])
    chunk = ysum[chunk_of(y, 8), :]
    for i in range(ny - 1):
        chunk = chunk + yr[i]

    mine = x * ny + y
    order = sorted(range(1, ny), key=lambda d: min(d, ny - d))


    def gather(buf, sems, y_extent, x_extent):
        ysend, yrecv, xsend, xrecv = sems

        def rows_of(d):
            return buf.at[pl.ds(pl.multiple_of((x * ny + lax.rem(y + ny - d, ny)) * 8, 8), 8)]

        own_rows = rows_of(0)
        along_y = {
            i + 1: begin(own_rows, own_rows, ysend.at[0], yrecv.at[i], (x, p, z, c)) for i, p in ys
        }

        def forward(d):
            if d:
                arrived([along_y[d]])
            for _, p in xs:
                begin(rows_of(d), rows_of(d), xsend.at[0], xrecv.at[0], (p, y, z, c))

        forward(0)
        last = described(x_extent, x_extent, xsend.at[0], xrecv.at[0], anyone)
        finals.extend([described(y_extent, y_extent, ysend.at[0], yrecv.at[0], anyone), last])
        return forward, last

    pall[chunk_of(mine, 8), :] = chunk
    p_forward, p_last = gather(pall, (py_s, py_r, px_s, px_r), yr, xr)
    sign_k = jnp.where(lax.broadcasted_iota(jnp.int32, (8, nb), 0) < 4, 1.0, -1.0).astype(F32)
    a, b = short_product(chunk, (b_re, b_im), NT)
    kout[...] = a + sign_k * pltpu.roll(b, 4, 0)
    k_copies = fan([(kout, kin.at[i], to) for i, to in fs], k_s.at[0], k_r.at[0], kin)
    for d in order:
        p_forward(d)
    arrived([k_copies])
    proj = kout[...]
    for i in range(len(fs)):
        proj = proj + kin[i]
    kall[chunk_of(mine, 8), :] = proj
    k_forward, k_last = gather(kall, (ky_s, ky_r, kx_s, kx_r), kin.at[pl.ds(0, ny - 1)], kspan)
    x_spread = spread(0, gathered(x_scatter, xhalf, xin), xfull, xin)
    arrived([p_last])

    def set_block(rows_by_part):
        top = as_rows(rows_by_part)
        n = top.shape[1] // 2
        bottom = jnp.concatenate([-top[:, n:], top[:, :n]], axis=1)
        for i, (above, below) in enumerate(zip(halves(top), halves(bottom))):
            wt[i, :npiv] = above
            wt[i, npiv:] = below
        return top, bottom

    to_row = lax.broadcasted_iota(jnp.int32, (emb, emb), 0)
    from_row = lax.broadcasted_iota(jnp.int32, (emb, emb), 1)
    by_part = (from_row == lax.rem(to_row, nx * ny) * 8 + to_row // (nx * ny)).astype(F32).astype(BF16)
    pivots = chosen(by_part, pall[...])
    top, bottom = set_block(pivots)
    gram = product((wt[0, :npiv], wt[1, :npiv]), halves(top + bottom), NT)
    for i in range(nz * nc):
        gpart[i] = gram[i * gpart.shape[1] : (i + 1) * gpart.shape[1]]
    g_scatter = fan([(gpart.at[to[2] * nc + to[3]], gin.at[i], to) for i, to in fs], g_s.at[0], g_r.at[0], gin)
    for d in order:
        k_forward(d)
    scatter_rows(cpart, product((live_h[0], live_h[1]), (wt[0], wt[1]), NT))
    c_pair = pair_up(1, cpart, cpair)

    c_scatter = scatter(1, c_pair, cpart, cpair, chalf, cin)
    arrived([g_scatter])
    total = gpart[f]
    for i in range(len(fs)):
        total = total + gin[i]
    gfull[f] = total
    g_gather = fan([(gfull.at[f], gfull.at[f], to) for _, to in fs], g_s.at[1], g_r.at[1], gin)
    x_last = share(0, x_spread, xfull)
    arrived([x_last])
    arrived([k_last])

    inner = halves(xfull[...].reshape(nb, nb))

    def times_inner(a):
        both = halves(a)
        straight, across = product(both, inner, NN), product(both, inner, NT)
        return crossed(0.5 * (straight + across), 0.5 * (straight - across))

    def split_rows(a):
        parts = halves(as_rows(a))
        return parts, tuple(embedded(part) for part in parts)

    proj = chosen(by_part, kall[...])
    taken = 2.0 * proj - times_inner(proj)
    rest, _ = split_rows(proj - times_inner(taken))
    _, k_both = split_rows(proj)
    t_rows, t_both = split_rows(taken)
    less = product(t_rows, k_both, NT) + product(rest, t_both, NT)
    kept = gathered(d_scatter, dhalf, din)
    total = gathered(c_scatter, chalf, cin)
    c_spread = spread(1, total - product(halves(kept), t_both, NT), cfull, cin)
    taken = halves(taken)
    set_block(pivots - crossed(product(taken, b_re, NN), product(taken, b_im, NN)))
    w = (wt[0], wt[1])
    arrived([g_gather])

    gram = gfull[...].reshape(npiv, npiv)
    turned = gram.T
    gram = jnp.concatenate([0.5 * (gram + turned), 0.5 * (gram - turned)], axis=1) - less
    eye = lax.broadcasted_iota(jnp.int32, (npiv, emb), 0) == lax.broadcasted_iota(jnp.int32, (npiv, emb), 1)
    ident = eye.astype(F32)
    diag = gram * ident
    scale_col = 1.0 / jnp.sqrt(jnp.sum(diag, axis=1, keepdims=True) + EPSILON)
    scale_row = 1.0 / jnp.sqrt(jnp.sum(diag[:, :npiv], axis=0, keepdims=True) + EPSILON)
    scale_row = jnp.concatenate([scale_row, scale_row], axis=1)
    gram = gram * (scale_col * scale_row)
    bound = jnp.max(jnp.sum(jnp.abs(gram), axis=1, keepdims=True), axis=0, keepdims=True)
    your = gram / bound
    zed = None

    def times(left, right):
        return product(left, tuple(embedded(part) for part in right), NN)

    for step in range(NS_STEPS):
        if step == 3:
            c_last = share(1, c_spread, cfull)
        yh = halves(your)
        mix = your if zed is None else times(zh, yh)
        s = 1.5 * ident - 0.5 * mix
        sh = halves(s)
        if step < NS_STEPS - 1:
            your = times(yh, sh)
        zed = s if zed is None else times(sh, zh)
        zh = halves(zed)
    zed = zed * (1.0 / jnp.sqrt(bound))

    zed_e = tuple(embedded(part) for part in halves(zed))
    arrived([c_last])
    cross = cfull[...].reshape(rows, emb)
    coef = product(halves(cross * scale_row), zed_e, NT)
    coef_re[...] = coef[:, :npiv]
    coef_im[...] = coef[:, npiv:]
    back = product(halves(product(halves(coef), zed_e, NN) * scale_row), w, NN)
    sums = []
    for part in blocks:
        mask = mask_of(part)
        real = (live[part, :bins] - back[part, :bins]) * mask
        imag = (live[part, bins:] - back[part, bins:]) * mask
        new_re[part, :] = real
        new_im[part, :] = imag
        square = real * real + imag * imag
        sums.append(sum(square[:, i : i + 128] for i in range(0, bins, 128)))
    ones = jnp.ones((8, 128), BF16)
    summed = sum(dot(ones, part, NT) for part in thirds(jnp.concatenate(sums, axis=0)))
    eout[...] = summed[0:1, :]
    ein[f] = summed[0:1, :]
    e_copies = fan([(eout, ein.at[f], to) for _, to in fs], e_s.at[0], e_r.at[0], ein.at[pl.ds(0, len(fs))])
    results = [(coef_re, out_coef_re), (coef_im, out_coef_im), (new_re, out_new_re), (new_im, out_new_im), (err, out_err)]
    results = [pltpu.make_async_copy(src, dst, out_s.at[i]) for i, (src, dst) in enumerate(results)]
    for result in results[:4]:
        result.start()
    arrived([e_copies])
    total = ein[0]
    for i in range(1, nz * nc):
        total = total + ein[i]
    err[...] = total / (BIN_BLOCK * vlen[...]).astype(F32)
    results[4].start()

    for copy in started + finals:
        copy.wait_send()
    for result in results:
        result.wait()


def handed_out(*refs):
    count = len(refs) // 2
    copies = [pltpu.make_async_copy(refs[i], refs[count + i], refs[-1].at[i]) for i in range(count)]
    for copy in copies:
        copy.start()
    for copy in copies:
        copy.wait()


def body(torus, res_re, res_im, basis_re, basis_im, lengths, pivots):
    nx, ny, nz, nc = torus
    rows, bins = res_re.shape
    nb = basis_re.shape[0]
    emb = 8 * nx * ny
    nf = nz * nc
    span = 8 * ny
    vmem = pltpu.VMEM
    dma = pltpu.SemaphoreType.DMA
    shapes = [(rows, emb // 2), (rows, emb // 2), (rows, bins), (rows, bins), (1, rows)]

    def summed(count, width):
        part = count // nf
        whole, across = vmem((nc, nz, part, width), F32), vmem((nz, part, width), F32)
        return [whole, across, across, vmem((nz - 1, part, width), F32), whole]

    scratch = [
        vmem((rows, 2 * bins), F32),
        vmem((2, rows, 2 * bins), BF16),
        vmem((2, nb, bins), F32),
        vmem((4, nb, bins), BF16),
        vmem((1, rows), jnp.int32),
        vmem((1, emb // 2), jnp.int32),
        vmem((emb, bins), F32),
        vmem((nx - 1, span, bins), F32),
        vmem((span, bins), F32),
        vmem((ny - 1, 8, bins), F32),
        vmem((8, nb), F32),
        vmem((nf - 1, 8, nb), F32),
        vmem((emb, bins), F32),
        vmem((emb, nb), F32),
        vmem((2, emb, 2 * bins), BF16),
        *[vmem(shape, F32) for shape in shapes],
        *summed(nb, nb),
        *[vmem((count, emb // 2 // nf, emb // 2), F32) for count in (nf, nf - 1, nf)],
        vmem(((nx - 1) * ny, 8, nb), F32),
        *summed(rows, emb),
        *summed(rows, 2 * nb)[:4],
        vmem((1, rows), F32), vmem((nf, 1, rows), F32),
        dma((6,)),
        *[dma((1,))] * 6, *[dma((3,))] * 2,
        *[dma((1,)), dma((ny - 1,)), dma((1,)), dma((1,))] * 2,
        *[dma((3,))] * 2, *[dma((2,))] * 2, *[dma((2,))] * 2, *[dma((2,))] * 2, *[dma((1,))] * 2,
        dma((5,)),
    ]
    here = pl.BlockSpec(memory_space=pltpu.VMEM)
    there = pl.BlockSpec(memory_space=pl.ANY)
    results = pl.pallas_call(
        functools.partial(kernel, torus),
        out_shape=[vmem(shape, F32) for shape in shapes],
        in_specs=[there] * 6,
        out_specs=[there] * 5,
        scratch_shapes=scratch,
        compiler_params=pltpu.CompilerParams(collective_id=0, has_side_effects=True),
    )(res_re, res_im, basis_re, basis_im, lengths.reshape(1, rows), pivots.reshape(1, emb // 2))
    coef_re, coef_im, new_re, new_im, err = pl.pallas_call(
        handed_out,
        out_shape=[jax.ShapeDtypeStruct(shape, F32) for shape in shapes],
        in_specs=[here] * 5,
        out_specs=[there] * 5,
        scratch_shapes=[dma((5,))],
    )(*[pltpu.with_memory_space_constraint(result, pltpu.VMEM) for result in results])
    return coef_re, coef_im, new_re, new_im, err.reshape(rows)


def build(mesh, torus):
    axes = Mesh(mesh.devices.reshape(torus), AXES)
    wave, freq = ("x", "y"), ("z", "core")
    in_specs = (P(wave, freq), P(wave, freq), P(None, freq), P(None, freq), P(wave), P())
    out_specs = (P(wave, None), P(wave, None), P(wave, freq), P(wave, freq), P(wave))
    return jax.shard_map(
        functools.partial(body, torus), mesh=axes, in_specs=in_specs, out_specs=out_specs, check_vma=False
    )


def solution(mesh):
    return build(mesh, TORUS)
```

```python
import functools

import jax
import jax.numpy as jnp
from jax import lax
from jax.experimental import pallas as pl
from jax.experimental.pallas import tpu as pltpu
from jax.sharding import Mesh
from jax.sharding import PartitionSpec as P

BIN_BLOCK = 128
NS_STEPS = 6
EPSILON = 1e-06
TORUS = (4, 8, 8, 2)
AXES = ("x", "y", "z", "core")
F32 = jnp.float32
BF16 = jnp.bfloat16


def dot(left, right, dims):
    return lax.dot_general(left, right, (dims, ((), ())), preferred_element_type=F32)


NN = ((1,), (0,))
NT = ((1,), (1,))


def halves(a):
    high = a.astype(BF16)
    return high, (a - high.astype(F32)).astype(BF16)


def thirds(a):
    high = a.astype(BF16)
    rest = a - high.astype(F32)
    mid = rest.astype(BF16)
    return high, mid, (rest - mid.astype(F32)).astype(BF16)


def product(left, right, dims):
    lh, ll = left
    rh, rl = right
    along = dims[1][0]
    return dot(jnp.concatenate([lh, ll, lh], axis=1), jnp.concatenate([rh, rh, rl], axis=along), dims)


def chosen(select, a):
    parts = thirds(a)
    return dot(jnp.concatenate([select] * 3, axis=1), jnp.concatenate(parts, axis=0), NN)


def embedded(row):
    n = row.shape[1] // 2
    return jnp.concatenate([row, jnp.concatenate([-row[:, n:], row[:, :n]], axis=1)], axis=0)


def crossed(a, b):
    n = a.shape[0] // 2
    return jnp.concatenate([a[:n] - b[n:], a[n:] + b[:n]], axis=0)


def as_rows(a):
    n = a.shape[0] // 2
    return jnp.concatenate([a[:n], a[n:]], axis=1)


def short_product(chunk, rights, dims):
    high = chunk.astype(BF16).astype(F32)
    both = jnp.concatenate([high, chunk - high], axis=0).astype(BF16)
    out = []
    for rh, rl in rights:
        a = dot(both, rh, dims)
        b = dot(both, rl, dims)
        out.append((a[:8] + a[8:]) + (b[:8] + b[8:]))
    return out


def kernel(
    torus,
    res_re, res_im, basis_re, basis_im, lens, piv,
    out_coef_re, out_coef_im, out_new_re, out_new_im, out_err,
    live, live_h, basis, base, vlen, vpiv, picked, far, relay, near, ysum, yr, kout, kin, pall, kall, wt,
    coef_re, coef_im, new_re, new_im, err,
    xpart, xpair, xhalf, xin, xfull, gpart, gin, gfull, kspan,
    cpart, cpair, chalf, cin, cfull, dpart, dpair, dhalf, din, dfull, eout, ein,
    in_s, rf_s, rf_r, rn_s, rn_r, rr_s, rr_r, ry_s, ry_r, k_s, k_r, p_s, p_r, py_s, py_r, px_s, px_r, ky_s, ky_r, kx_s, kx_r,
    zs_s, zs_r, zg_s, zg_r, c_s, c_r, g_s, g_r, e_s, e_r, out_s,
):
    nx, ny, nz, nc = torus
    x, y, z, c = (lax.axis_index(a) for a in AXES)
    f = z * nc + c
    rows, bins = res_re.shape
    emb = 8 * nx * ny
    npiv = emb // 2
    nb = basis_re.shape[0]
    span = 8 * ny

    def hops(d, n):
        return min(d, n - d)

    xs = [(d - 1, lax.rem(x + d, nx)) for d in sorted(range(1, nx), key=lambda d: -hops(d, nx))]
    ys = [(d - 1, lax.rem(y + d, ny)) for d in sorted(range(1, ny), key=lambda d: -hops(d, ny))]
    zs = [(d - 1, lax.rem(z + d, nz)) for d in sorted(range(1, nz), key=lambda d: -hops(d, nz))]
    fs = sorted(((dz, dc) for dz in range(nz) for dc in range(nc) if dz or dc), key=lambda d: -hops(d[0], nz))
    fs = [(dz * nc + dc - 1, (x, y, lax.rem(z + dz, nz), lax.rem(c + dc, nc))) for dz, dc in fs]
    barrier = pltpu.get_barrier_semaphore()
    peers = [to for _, to in fs] + [(x, p, z, c) for _, p in ys] + [(p, y, z, c) for _, p in xs]
    for peer in peers:
        pl.semaphore_signal(barrier, inc=1, device_id=peer, device_id_type=pl.DeviceIdType.MESH)
    loads = [(lens, vlen), (piv, vpiv), (res_re, live.at[:, pl.ds(0, bins)]), (res_im, live.at[:, pl.ds(bins, bins)])]
    loads += [(basis_re, basis.at[0]), (basis_im, basis.at[1])]
    loads = [pltpu.make_async_copy(src, dst, in_s.at[i]) for i, (src, dst) in enumerate(loads)]
    for load in loads:
        load.start()

    started = []
    anyone = fs[0][1]

    def described(src, dst, send, recv, to):
        return pltpu.make_async_remote_copy(
            src_ref=src, dst_ref=dst, send_sem=send, recv_sem=recv, device_id=to,
            device_id_type=pl.DeviceIdType.MESH,
        )

    def begin(src, dst, send, recv, to):
        copy = described(src, dst, send, recv, to)
        copy.start()
        return copy

    def push(src, dst, send, recv, to):
        copy = begin(src, dst, send, recv, to)
        started.append(copy)
        return copy

    def arrived(copies):
        for copy in copies:
            copy.wait_recv()

    finals = []

    def fan(pairs, send, recv, extent):
        for src, dst, to in pairs:
            begin(src, dst, send, recv, to)
        whole = described(extent, extent, send, recv, anyone)
        finals.append(whole)
        return whole

    def chunk_of(i, size):
        return pl.ds(pl.multiple_of(i * size, size), size)

    for load in loads[:4]:
        load.wait()
    diagonal = lax.broadcasted_iota(jnp.int32, (rows, rows), 0) == lax.broadcasted_iota(jnp.int32, (rows, rows), 1)
    ends = jnp.sum(jnp.where(diagonal, vlen[...] * BIN_BLOCK, 0).astype(F32), axis=1, keepdims=True)
    first_bin = f * bins

    def mask_of(part):
        count = part.stop - part.start
        at = first_bin + lax.broadcasted_iota(jnp.int32, (count, bins), 1)
        return (at.astype(F32) < ends[part, :]).astype(F32)

    blocks = [slice(r, min(r + 64, rows)) for r in range(0, rows, 64)]
    for part in blocks:
        mask = mask_of(part)
        live[part, :bins] = live[part, :bins] * mask
        live[part, bins:] = live[part, bins:] * mask
    to_row = lax.broadcasted_iota(jnp.int32, (emb, npiv), 0)
    of_row = lax.broadcasted_iota(jnp.int32, (emb, npiv), 1) == lax.rem(to_row, 4) * (nx * ny) + to_row // 8
    wanted = jnp.sum(jnp.where(of_row, vpiv[...], 0).astype(F32), axis=1, keepdims=True)
    own = (x * ny + y) * rows + lax.broadcasted_iota(jnp.int32, (emb, rows), 1)
    select = (wanted == own.astype(F32)).astype(F32).astype(BF16)
    is_im = lax.rem(lax.broadcasted_iota(jnp.int32, (emb, bins), 0), 8) // 4
    picked[...] = jnp.where(is_im == 0, chosen(select, live[:, :bins]), chosen(select, live[:, bins:]))

    pl.semaphore_wait(barrier, len(peers))

    half, piece = bins // 2, span // 2
    ahead, behind = pl.ds(0, half), pl.ds(half, half)
    right, left, across = (lax.rem(x + d, nx) for d in (1, nx - 1, 2))
    ways = (((right, y, z, c), right, ahead), ((left, y, z, c), left, behind))
    far_copies = []
    for i in range(2):
        for k, (to, _, lanes) in enumerate(ways):
            at = pl.ds(pl.multiple_of(across * span + i * piece, piece), piece)
            far_copies.append(
                push(picked.at[at, lanes], far.at[k, pl.ds(i * piece, piece)], rf_s.at[i, k], rf_r.at[i, k], to)
            )

    for i, value in enumerate(halves(live[...])):
        live_h[i] = value
    for load in loads[4:]:
        load.wait()
    for i in range(2):
        high, low = halves(basis[i])
        base[2 * i] = high
        base[2 * i + 1] = low
    b_re = (base[0], base[1])
    b_im = (base[2], base[3])
    plus = jnp.concatenate([basis[0] + basis[1], basis[1] - basis[0]], axis=1)
    right_side = tuple(jnp.concatenate([base[i], base[2 + i]], axis=1) for i in range(2))
    both = product(halves(plus), right_side, NT)

    def scatter_rows(part, value):
        size = part.shape[2]
        for i in range(nc):
            for j in range(nz):
                at = (i * nz + j) * size
                part[i, j] = value[at : at + size]

    def pair_up(k, part, got):
        return push(part.at[1 - c], got, p_s.at[k], p_r.at[k], (x, y, z, 1 - c))

    def scatter(k, pair, part, got, summed, inward):
        arrived([pair])
        summed[...] = part[c] + got[...]
        return fan([(summed.at[p], inward.at[i], (x, y, p, c)) for i, p in zs], zs_s.at[k], zs_r.at[k], inward)

    def gathered(copies, summed, inward):
        arrived([copies])
        total = summed[z]
        for i in range(nz - 1):
            total = total + inward[i]
        return total

    def spread(k, total, full, extent):
        full[c, z] = total
        at = full.at[c, z]
        return fan([(at, at, (x, y, p, c)) for i, p in zs], zg_s.at[k], zg_r.at[k], extent)

    def share(k, copies, full):
        arrived([copies])
        return push(full.at[c], full.at[c], c_s.at[k], c_r.at[k], (x, y, z, 1 - c))

    near_started = [
        (picked.at[chunk_of(next_x, span), other], near.at[k, :, other], to)
        for k, ((to, next_x, _), other) in enumerate(zip(ways, (behind, ahead)))
    ]
    near_begun = fan(near_started, rn_s.at[0], rn_r.at[0], far)
    scatter_rows(xpart, both)
    x_pair = pair_up(0, xpart, xpair)
    turned_side = tuple(jnp.concatenate([-base[2 + i], base[i]], axis=1) for i in range(2))
    both = tuple(jnp.concatenate([right_side[i], turned_side[i]], axis=0) for i in range(2))
    scatter_rows(dpart, product((live_h[0], live_h[1]), both, NT))
    x_scatter = scatter(0, x_pair, xpart, xpair, xhalf, xin)
    d_pair = pair_up(2, dpart, dpair)

    relays = []
    for i in range(2):
        for k, (to, next_x, lanes) in enumerate(ways):
            arrived([far_copies[2 * i + k]])
            at = pl.ds(pl.multiple_of(next_x * span + i * piece, piece), piece)
            part = pl.ds(i * piece, piece)
            relay[k, i * piece : (i + 1) * piece] = (
                picked[at, k * half : (k + 1) * half] + far[k, i * piece : (i + 1) * piece]
            )
            relays.append(push(relay.at[k, part], near.at[k, part, lanes], rr_s.at[i, k], rr_r.at[i, k], to))
    d_scatter = scatter(2, d_pair, dpart, dpair, dhalf, din)
    arrived([near_begun, *relays])
    ysum[...] = picked[chunk_of(x, span), :] + near[0] + near[1]
    y_copies = fan([(ysum.at[chunk_of(p, 8)], yr.at[i], (x, p, z, c)) for i, p in ys], ry_s.at[0], ry_r.at[0], yr)
    arrived([y_copies])
    chunk = ysum[chunk_of(y, 8), :]
    for i in range(ny - 1):
        chunk = chunk + yr[i]

    mine = x * ny + y
    order = sorted(range(1, ny), key=lambda d: min(d, ny - d))


    def gather(buf, sems, y_extent, x_extent):
        ysend, yrecv, xsend, xrecv = sems

        def rows_of(d):
            return buf.at[pl.ds(pl.multiple_of((x * ny + lax.rem(y + ny - d, ny)) * 8, 8), 8)]

        own_rows = rows_of(0)
        along_y = {
            i + 1: begin(own_rows, own_rows, ysend.at[0], yrecv.at[i], (x, p, z, c)) for i, p in ys
        }

        def forward(d):
            if d:
                arrived([along_y[d]])
            for _, p in xs:
                begin(rows_of(d), rows_of(d), xsend.at[0], xrecv.at[0], (p, y, z, c))

        forward(0)
        last = described(x_extent, x_extent, xsend.at[0], xrecv.at[0], anyone)
        finals.extend([described(y_extent, y_extent, ysend.at[0], yrecv.at[0], anyone), last])
        return forward, last

    pall[chunk_of(mine, 8), :] = chunk
    p_forward, p_last = gather(pall, (py_s, py_r, px_s, px_r), yr, picked.at[pl.ds(0, (nx - 1) * span)])
    sign_k = jnp.where(lax.broadcasted_iota(jnp.int32, (8, nb), 0) < 4, 1.0, -1.0).astype(F32)
    a, b = short_product(chunk, (b_re, b_im), NT)
    kout[...] = a + sign_k * pltpu.roll(b, 4, 0)
    k_copies = fan([(kout, kin.at[i], to) for i, to in fs], k_s.at[0], k_r.at[0], kin)
    for d in order:
        p_forward(d)
    x_spread = spread(0, gathered(x_scatter, xhalf, xin), xfull, xin)
    d_spread = spread(2, gathered(d_scatter, dhalf, din), dfull, din)
    arrived([k_copies])
    proj = kout[...]
    for i in range(len(fs)):
        proj = proj + kin[i]
    kall[chunk_of(mine, 8), :] = proj
    k_forward, k_last = gather(kall, (ky_s, ky_r, kx_s, kx_r), kin.at[pl.ds(0, ny - 1)], kspan)
    arrived([p_last])

    def set_block(top):
        n = top[0].shape[1] // 2
        for i, above in enumerate(top):
            wt[i, :npiv] = above
            wt[i, npiv:, :n] = -above[:, n:]
            wt[i, npiv:, n:] = above[:, :n]

    to_row = lax.broadcasted_iota(jnp.int32, (emb, emb), 0)
    from_row = lax.broadcasted_iota(jnp.int32, (emb, emb), 1)
    by_part = (from_row == lax.rem(to_row, nx * ny) * 8 + to_row // (nx * ny)).astype(F32).astype(BF16)
    pivots = chosen(by_part, pall[...])
    mixed = jnp.concatenate([pivots[:npiv] - pivots[npiv:], pivots[:npiv] + pivots[npiv:]], axis=1)
    top = halves(as_rows(pivots))
    gram = product(top, halves(mixed), NT)
    for i in range(nz * nc):
        gpart[i] = gram[i * gpart.shape[1] : (i + 1) * gpart.shape[1]]
    g_scatter = fan([(gpart.at[to[2] * nc + to[3]], gin.at[i], to) for i, to in fs], g_s.at[0], g_r.at[0], gin)
    set_block(top)
    for d in order:
        k_forward(d)
    scatter_rows(cpart, product((live_h[0], live_h[1]), (wt[0], wt[1]), NT))
    c_pair = pair_up(1, cpart, cpair)
    x_last = share(0, x_spread, xfull)
    d_last = share(2, d_spread, dfull)

    c_scatter = scatter(1, c_pair, cpart, cpair, chalf, cin)
    arrived([g_scatter])
    total = gpart[f]
    for i in range(len(fs)):
        total = total + gin[i]
    gfull[f] = total
    g_gather = fan([(gfull.at[f], gfull.at[f], to) for _, to in fs], g_s.at[1], g_r.at[1], gin)
    c_spread = spread(1, gathered(c_scatter, chalf, cin), cfull, cin)
    arrived([x_last, d_last])
    arrived([k_last])

    inner = halves(xfull[...].reshape(nb, nb))

    def times_inner(a):
        both = halves(a)
        straight, across = product(both, inner, NN), product(both, inner, NT)
        return crossed(0.5 * (straight + across), 0.5 * (straight - across))

    def split_rows(a):
        parts = halves(as_rows(a))
        return parts, tuple(embedded(part) for part in parts)

    proj = chosen(by_part, kall[...])
    taken = 2.0 * proj - times_inner(proj)
    rest, _ = split_rows(proj - times_inner(taken))
    _, k_both = split_rows(proj)
    t_rows, t_both = split_rows(taken)
    less = product(t_rows, k_both, NT) + product(rest, t_both, NT)
    cross_less = product(halves(dfull[...].reshape(rows, 2 * nb)), t_both, NT)
    taken = halves(taken)
    set_block(halves(as_rows(pivots - crossed(product(taken, b_re, NN), product(taken, b_im, NN)))))
    w = (wt[0], wt[1])
    arrived([g_gather])

    gram = gfull[...].reshape(npiv, npiv)
    turned = gram.T
    gram = jnp.concatenate([0.5 * (gram + turned), 0.5 * (gram - turned)], axis=1) - less
    eye = lax.broadcasted_iota(jnp.int32, (npiv, emb), 0) == lax.broadcasted_iota(jnp.int32, (npiv, emb), 1)
    ident = eye.astype(F32)
    diag = gram * ident
    scale_col = 1.0 / jnp.sqrt(jnp.sum(diag, axis=1, keepdims=True) + EPSILON)
    scale_row = 1.0 / jnp.sqrt(jnp.sum(diag[:, :npiv], axis=0, keepdims=True) + EPSILON)
    scale_row = jnp.concatenate([scale_row, scale_row], axis=1)
    gram = gram * (scale_col * scale_row)
    bound = jnp.max(jnp.sum(jnp.abs(gram), axis=1, keepdims=True), axis=0, keepdims=True)
    your = gram / bound
    zed = None

    def times(left, right):
        return product(left, tuple(embedded(part) for part in right), NN)

    for step in range(NS_STEPS):
        if step == 3:
            c_last = share(1, c_spread, cfull)
        yh = halves(your)
        mix = your if zed is None else times(zh, yh)
        s = 1.5 * ident - 0.5 * mix
        sh = halves(s)
        if step < NS_STEPS - 1:
            your = times(yh, sh)
        zed = s if zed is None else times(sh, zh)
        zh = halves(zed)
    zed = zed * (1.0 / jnp.sqrt(bound))

    zed_e = tuple(embedded(part) for part in halves(zed))
    arrived([c_last])
    cross = cfull[...].reshape(rows, emb) - cross_less
    coef = product(halves(cross * scale_row), zed_e, NT)
    coef_re[...] = coef[:, :npiv]
    coef_im[...] = coef[:, npiv:]
    back = product(halves(product(halves(coef), zed_e, NN) * scale_row), w, NN)
    sums = []
    for part in blocks:
        mask = mask_of(part)
        real = (live[part, :bins] - back[part, :bins]) * mask
        imag = (live[part, bins:] - back[part, bins:]) * mask
        new_re[part, :] = real
        new_im[part, :] = imag
        square = real * real + imag * imag
        sums.append(sum(square[:, i : i + 128] for i in range(0, bins, 128)))
    ones = jnp.ones((8, 128), BF16)
    summed = sum(dot(ones, part, NT) for part in thirds(jnp.concatenate(sums, axis=0)))
    eout[...] = summed[0:1, :]
    ein[f] = summed[0:1, :]
    e_copies = fan([(eout, ein.at[f], to) for _, to in fs], e_s.at[0], e_r.at[0], ein.at[pl.ds(0, len(fs))])
    results = [(coef_re, out_coef_re), (coef_im, out_coef_im), (new_re, out_new_re), (new_im, out_new_im), (err, out_err)]
    results = [pltpu.make_async_copy(src, dst, out_s.at[i]) for i, (src, dst) in enumerate(results)]
    for result in results[:4]:
        result.start()
    arrived([e_copies])
    total = ein[0]
    for i in range(1, nz * nc):
        total = total + ein[i]
    err[...] = total / (BIN_BLOCK * vlen[...]).astype(F32)
    results[4].start()

    for copy in started + finals:
        copy.wait_send()
    for result in results:
        result.wait()


def handed_out(*refs):
    count = len(refs) // 2
    copies = [pltpu.make_async_copy(refs[i], refs[count + i], refs[-1].at[i]) for i in range(count)]
    for copy in copies:
        copy.start()
    for copy in copies:
        copy.wait()


def body(torus, res_re, res_im, basis_re, basis_im, lengths, pivots):
    nx, ny, nz, nc = torus
    rows, bins = res_re.shape
    nb = basis_re.shape[0]
    emb = 8 * nx * ny
    nf = nz * nc
    span = 8 * ny
    vmem = pltpu.VMEM
    dma = pltpu.SemaphoreType.DMA
    shapes = [(rows, emb // 2), (rows, emb // 2), (rows, bins), (rows, bins), (1, rows)]

    def summed(count, width):
        part = count // nf
        whole, across = vmem((nc, nz, part, width), F32), vmem((nz, part, width), F32)
        return [whole, across, across, vmem((nz - 1, part, width), F32), whole]

    scratch = [
        vmem((rows, 2 * bins), F32),
        vmem((2, rows, 2 * bins), BF16),
        vmem((2, nb, bins), F32),
        vmem((4, nb, bins), BF16),
        vmem((1, rows), jnp.int32),
        vmem((1, emb // 2), jnp.int32),
        vmem((emb, bins), F32),
        vmem((2, span, bins // 2), F32),
        vmem((2, span, bins // 2), F32),
        vmem((2, span, bins), F32),
        vmem((span, bins), F32),
        vmem((ny - 1, 8, bins), F32),
        vmem((8, nb), F32),
        vmem((nf - 1, 8, nb), F32),
        vmem((emb, bins), F32),
        vmem((emb, nb), F32),
        vmem((2, emb, 2 * bins), BF16),
        *[vmem(shape, F32) for shape in shapes],
        *summed(nb, nb),
        *[vmem((count, emb // 2 // nf, emb // 2), F32) for count in (nf, nf - 1, nf)],
        vmem(((nx - 1) * ny, 8, nb), F32),
        *summed(rows, emb),
        *summed(rows, 2 * nb),
        vmem((1, rows), F32), vmem((nf, 1, rows), F32),
        dma((6,)),
        *[dma((2, 2))] * 2, *[dma((1,))] * 2, *[dma((2, 2))] * 2, *[dma((1,))] * 4, *[dma((3,))] * 2,
        *[dma((1,)), dma((ny - 1,)), dma((1,)), dma((1,))] * 2,
        *[dma((3,))] * 6, *[dma((2,))] * 2, *[dma((1,))] * 2,
        dma((5,)),
    ]
    here = pl.BlockSpec(memory_space=pltpu.VMEM)
    there = pl.BlockSpec(memory_space=pl.ANY)
    results = pl.pallas_call(
        functools.partial(kernel, torus),
        out_shape=[vmem(shape, F32) for shape in shapes],
        in_specs=[there] * 6,
        out_specs=[there] * 5,
        scratch_shapes=scratch,
        compiler_params=pltpu.CompilerParams(collective_id=0, has_side_effects=True),
    )(res_re, res_im, basis_re, basis_im, lengths.reshape(1, rows), pivots.reshape(1, emb // 2))
    coef_re, coef_im, new_re, new_im, err = pl.pallas_call(
        handed_out,
        out_shape=[jax.ShapeDtypeStruct(shape, F32) for shape in shapes],
        in_specs=[here] * 5,
        out_specs=[there] * 5,
        scratch_shapes=[dma((5,))],
    )(*[pltpu.with_memory_space_constraint(result, pltpu.VMEM) for result in results])
    return coef_re, coef_im, new_re, new_im, err.reshape(rows)


def build(mesh, torus):
    axes = Mesh(mesh.devices.reshape(torus), AXES)
    wave, freq = ("x", "y"), ("z", "core")
    in_specs = (P(wave, freq), P(wave, freq), P(None, freq), P(None, freq), P(wave), P())
    out_specs = (P(wave, None), P(wave, None), P(wave, freq), P(wave, freq), P(wave))
    return jax.shard_map(
        functools.partial(body, torus), mesh=axes, in_specs=in_specs, out_specs=out_specs, check_vma=False
    )


def solution(mesh):
    return build(mesh, TORUS)
```

```python
import functools

import jax
import jax.numpy as jnp
from jax import lax
from jax.experimental import pallas as pl
from jax.experimental.pallas import tpu as pltpu
from jax.sharding import Mesh
from jax.sharding import PartitionSpec as P

BIN_BLOCK = 128
NS_STEPS = 6
EPSILON = 1e-06
TORUS = (4, 8, 8, 2)
AXES = ("x", "y", "z", "core")
F32 = jnp.float32
BF16 = jnp.bfloat16


def dot(left, right, dims):
    return lax.dot_general(left, right, (dims, ((), ())), preferred_element_type=F32)


NN = ((1,), (0,))
NT = ((1,), (1,))


def halves(a):
    high = a.astype(BF16)
    return high, (a - high.astype(F32)).astype(BF16)


def thirds(a):
    high = a.astype(BF16)
    rest = a - high.astype(F32)
    mid = rest.astype(BF16)
    return high, mid, (rest - mid.astype(F32)).astype(BF16)


def product(left, right, dims):
    lh, ll = left
    rh, rl = right
    along = dims[1][0]
    return dot(jnp.concatenate([lh, ll, lh], axis=1), jnp.concatenate([rh, rh, rl], axis=along), dims)


def chosen(select, a):
    parts = thirds(a)
    return dot(jnp.concatenate([select] * 3, axis=1), jnp.concatenate(parts, axis=0), NN)


def embedded(row):
    n = row.shape[1] // 2
    return jnp.concatenate([row, jnp.concatenate([-row[:, n:], row[:, :n]], axis=1)], axis=0)


def crossed(a, b):
    n = a.shape[0] // 2
    return jnp.concatenate([a[:n] - b[n:], a[n:] + b[:n]], axis=0)


def as_rows(a):
    n = a.shape[0] // 2
    return jnp.concatenate([a[:n], a[n:]], axis=1)


def short_product(chunk, rights, dims):
    high = chunk.astype(BF16).astype(F32)
    both = jnp.concatenate([high, chunk - high], axis=0).astype(BF16)
    out = []
    for rh, rl in rights:
        a = dot(both, rh, dims)
        b = dot(both, rl, dims)
        out.append((a[:8] + a[8:]) + (b[:8] + b[8:]))
    return out


def kernel(
    torus,
    res_re, res_im, basis_re, basis_im, lens, piv,
    out_coef_re, out_coef_im, out_new_re, out_new_im, out_err,
    live, live_h, basis, base, vlen, vpiv, picked, far, relay, near, ysum, yr, kout, kin, pall, kall, wt,
    coef_re, coef_im, new_re, new_im, err,
    xpart, xpair, xhalf, xin, xfull, gpart, gin, gfull, kspan,
    cpart, cpair, chalf, cin, cfull, dpart, dpair, dhalf, din, dfull, eout, ein,
    in_s, rf_s, rf_r, rn_s, rn_r, rr_s, rr_r, ry_s, ry_r, k_s, k_r, p_s, p_r, py_s, py_r, px_s, px_r, ky_s, ky_r, kx_s, kx_r,
    zs_s, zs_r, zg_s, zg_r, c_s, c_r, g_s, g_r, e_s, e_r, out_s,
):
    nx, ny, nz, nc = torus
    x, y, z, c = (lax.axis_index(a) for a in AXES)
    f = z * nc + c
    rows, bins = res_re.shape
    emb = 8 * nx * ny
    npiv = emb // 2
    nb = basis_re.shape[0]
    span = 8 * ny

    def hops(d, n):
        return min(d, n - d)

    xs = [(d - 1, lax.rem(x + d, nx)) for d in sorted(range(1, nx), key=lambda d: -hops(d, nx))]
    ys = [(d - 1, lax.rem(y + d, ny)) for d in sorted(range(1, ny), key=lambda d: -hops(d, ny))]
    zs = [(d - 1, lax.rem(z + d, nz)) for d in sorted(range(1, nz), key=lambda d: -hops(d, nz))]
    fs = sorted(((dz, dc) for dz in range(nz) for dc in range(nc) if dz or dc), key=lambda d: -hops(d[0], nz))
    fs = [(dz * nc + dc - 1, (x, y, lax.rem(z + dz, nz), lax.rem(c + dc, nc))) for dz, dc in fs]
    barrier = pltpu.get_barrier_semaphore()
    peers = [to for _, to in fs] + [(x, p, z, c) for _, p in ys] + [(p, y, z, c) for _, p in xs]
    for peer in peers:
        pl.semaphore_signal(barrier, inc=1, device_id=peer, device_id_type=pl.DeviceIdType.MESH)
    loads = [(lens, vlen), (piv, vpiv), (res_re, live.at[:, pl.ds(0, bins)]), (res_im, live.at[:, pl.ds(bins, bins)])]
    loads += [(basis_re, basis.at[0]), (basis_im, basis.at[1])]
    loads = [pltpu.make_async_copy(src, dst, in_s.at[i]) for i, (src, dst) in enumerate(loads)]
    for load in loads:
        load.start()

    started = []
    anyone = fs[0][1]

    def described(src, dst, send, recv, to):
        return pltpu.make_async_remote_copy(
            src_ref=src, dst_ref=dst, send_sem=send, recv_sem=recv, device_id=to,
            device_id_type=pl.DeviceIdType.MESH,
        )

    def begin(src, dst, send, recv, to):
        copy = described(src, dst, send, recv, to)
        copy.start()
        return copy

    def push(src, dst, send, recv, to):
        copy = begin(src, dst, send, recv, to)
        started.append(copy)
        return copy

    def arrived(copies):
        for copy in copies:
            copy.wait_recv()

    finals = []

    def fan(pairs, send, recv, extent):
        for src, dst, to in pairs:
            begin(src, dst, send, recv, to)
        whole = described(extent, extent, send, recv, anyone)
        finals.append(whole)
        return whole

    def chunk_of(i, size):
        return pl.ds(pl.multiple_of(i * size, size), size)

    for load in loads[:4]:
        load.wait()
    diagonal = lax.broadcasted_iota(jnp.int32, (rows, rows), 0) == lax.broadcasted_iota(jnp.int32, (rows, rows), 1)
    ends = jnp.sum(jnp.where(diagonal, vlen[...] * BIN_BLOCK, 0).astype(F32), axis=1, keepdims=True)
    first_bin = f * bins

    def mask_of(part):
        count = part.stop - part.start
        at = first_bin + lax.broadcasted_iota(jnp.int32, (count, bins), 1)
        return (at.astype(F32) < ends[part, :]).astype(F32)

    blocks = [slice(r, min(r + 64, rows)) for r in range(0, rows, 64)]
    for part in blocks:
        mask = mask_of(part)
        live[part, :bins] = live[part, :bins] * mask
        live[part, bins:] = live[part, bins:] * mask
    to_row = lax.broadcasted_iota(jnp.int32, (emb, npiv), 0)
    of_row = lax.broadcasted_iota(jnp.int32, (emb, npiv), 1) == lax.rem(to_row, 4) * (nx * ny) + to_row // 8
    wanted = jnp.sum(jnp.where(of_row, vpiv[...], 0).astype(F32), axis=1, keepdims=True)
    own = (x * ny + y) * rows + lax.broadcasted_iota(jnp.int32, (emb, rows), 1)
    select = (wanted == own.astype(F32)).astype(F32).astype(BF16)
    is_im = lax.rem(lax.broadcasted_iota(jnp.int32, (emb, bins), 0), 8) // 4
    picked[...] = jnp.where(is_im == 0, chosen(select, live[:, :bins]), chosen(select, live[:, bins:]))

    pl.semaphore_wait(barrier, len(peers))

    half, piece = bins // 2, span // 2
    ahead, behind = pl.ds(0, half), pl.ds(half, half)
    right, left, across = (lax.rem(x + d, nx) for d in (1, nx - 1, 2))
    ways = (((right, y, z, c), right, ahead), ((left, y, z, c), left, behind))
    far_copies = []
    for i in range(2):
        for k, (to, _, lanes) in enumerate(ways):
            at = pl.ds(pl.multiple_of(across * span + i * piece, piece), piece)
            far_copies.append(
                push(picked.at[at, lanes], far.at[k, pl.ds(i * piece, piece)], rf_s.at[i, k], rf_r.at[i, k], to)
            )

    for i, value in enumerate(halves(live[...])):
        live_h[i] = value
    for load in loads[4:]:
        load.wait()
    for i in range(2):
        high, low = halves(basis[i])
        base[2 * i] = high
        base[2 * i + 1] = low
    b_re = (base[0], base[1])
    b_im = (base[2], base[3])
    plus = jnp.concatenate([basis[0] + basis[1], basis[1] - basis[0]], axis=1)
    right_side = tuple(jnp.concatenate([base[i], base[2 + i]], axis=1) for i in range(2))
    both = product(halves(plus), right_side, NT)

    def scatter_rows(part, value):
        size = part.shape[2]
        for i in range(nc):
            for j in range(nz):
                at = (i * nz + j) * size
                part[i, j] = value[at : at + size]

    def pair_up(k, part, got):
        return push(part.at[1 - c], got, p_s.at[k], p_r.at[k], (x, y, z, 1 - c))

    def scatter(k, pair, part, got, summed, inward):
        arrived([pair])
        summed[...] = part[c] + got[...]
        return fan([(summed.at[p], inward.at[i], (x, y, p, c)) for i, p in zs], zs_s.at[k], zs_r.at[k], inward)

    def gathered(copies, summed, inward):
        arrived([copies])
        total = summed[z]
        for i in range(nz - 1):
            total = total + inward[i]
        return total

    def spread(k, total, full, extent):
        full[c, z] = total
        at = full.at[c, z]
        return fan([(at, at, (x, y, p, c)) for i, p in zs], zg_s.at[k], zg_r.at[k], extent)

    def share(k, copies, full):
        arrived([copies])
        return push(full.at[c], full.at[c], c_s.at[k], c_r.at[k], (x, y, z, 1 - c))

    near_started = [
        (picked.at[chunk_of(next_x, span), other], near.at[k, :, other], to)
        for k, ((to, next_x, _), other) in enumerate(zip(ways, (behind, ahead)))
    ]
    near_begun = fan(near_started, rn_s.at[0], rn_r.at[0], far)
    scatter_rows(xpart, both)
    x_pair = pair_up(0, xpart, xpair)
    turned_side = tuple(jnp.concatenate([-base[2 + i], base[i]], axis=1) for i in range(2))
    both = tuple(jnp.concatenate([right_side[i], turned_side[i]], axis=0) for i in range(2))
    scatter_rows(dpart, product((live_h[0], live_h[1]), both, NT))
    x_scatter = scatter(0, x_pair, xpart, xpair, xhalf, xin)
    d_pair = pair_up(2, dpart, dpair)

    relays = []
    for i in range(2):
        for k, (to, next_x, lanes) in enumerate(ways):
            arrived([far_copies[2 * i + k]])
            at = pl.ds(pl.multiple_of(next_x * span + i * piece, piece), piece)
            part = pl.ds(i * piece, piece)
            relay[k, i * piece : (i + 1) * piece] = (
                picked[at, k * half : (k + 1) * half] + far[k, i * piece : (i + 1) * piece]
            )
            relays.append(push(relay.at[k, part], near.at[k, part, lanes], rr_s.at[i, k], rr_r.at[i, k], to))
    d_scatter = scatter(2, d_pair, dpart, dpair, dhalf, din)
    arrived([near_begun, *relays])
    ysum[...] = picked[chunk_of(x, span), :] + near[0] + near[1]
    y_copies = fan([(ysum.at[chunk_of(p, 8)], yr.at[i], (x, p, z, c)) for i, p in ys], ry_s.at[0], ry_r.at[0], yr)
    arrived([y_copies])
    chunk = ysum[chunk_of(y, 8), :]
    for i in range(ny - 1):
        chunk = chunk + yr[i]

    mine = x * ny + y
    order = sorted(range(1, ny), key=lambda d: min(d, ny - d))


    def gather(buf, sems, y_extent, x_extent):
        ysend, yrecv, xsend, xrecv = sems

        def rows_of(d):
            return buf.at[pl.ds(pl.multiple_of((x * ny + lax.rem(y + ny - d, ny)) * 8, 8), 8)]

        own_rows = rows_of(0)
        along_y = {
            i + 1: begin(own_rows, own_rows, ysend.at[0], yrecv.at[i], (x, p, z, c)) for i, p in ys
        }

        def forward(d):
            if d:
                arrived([along_y[d]])
            for _, p in xs:
                begin(rows_of(d), rows_of(d), xsend.at[0], xrecv.at[0], (p, y, z, c))

        forward(0)
        last = described(x_extent, x_extent, xsend.at[0], xrecv.at[0], anyone)
        finals.extend([described(y_extent, y_extent, ysend.at[0], yrecv.at[0], anyone), last])
        return forward, last

    pall[chunk_of(mine, 8), :] = chunk
    p_forward, p_last = gather(pall, (py_s, py_r, px_s, px_r), yr, picked.at[pl.ds(0, (nx - 1) * span)])
    sign_k = jnp.where(lax.broadcasted_iota(jnp.int32, (8, nb), 0) < 4, 1.0, -1.0).astype(F32)
    a, b = short_product(chunk, (b_re, b_im), NT)
    kout[...] = a + sign_k * pltpu.roll(b, 4, 0)
    k_copies = fan([(kout, kin.at[i], to) for i, to in fs], k_s.at[0], k_r.at[0], kin)
    x_spread = spread(0, gathered(x_scatter, xhalf, xin), xfull, xin)
    d_spread = spread(2, gathered(d_scatter, dhalf, din), dfull, din)
    for d in order:
        p_forward(d)
    arrived([k_copies])
    proj = kout[...]
    for i in range(len(fs)):
        proj = proj + kin[i]
    kall[chunk_of(mine, 8), :] = proj
    k_forward, k_last = gather(kall, (ky_s, ky_r, kx_s, kx_r), kin.at[pl.ds(0, ny - 1)], kspan)
    arrived([p_last])

    def set_block(top):
        n = top[0].shape[1] // 2
        for i, above in enumerate(top):
            wt[i, :npiv] = above
            wt[i, npiv:, :n] = -above[:, n:]
            wt[i, npiv:, n:] = above[:, :n]

    to_row = lax.broadcasted_iota(jnp.int32, (emb, emb), 0)
    from_row = lax.broadcasted_iota(jnp.int32, (emb, emb), 1)
    by_part = (from_row == lax.rem(to_row, nx * ny) * 8 + to_row // (nx * ny)).astype(F32).astype(BF16)

    def by_parts(a):
        return tuple(dot(by_part, part, NN).astype(BF16) for part in halves(a))

    pivot_halves = by_parts(pall[...])
    pivots = pivot_halves[0].astype(F32) + pivot_halves[1].astype(F32)
    mixed = jnp.concatenate([pivots[:npiv] - pivots[npiv:], pivots[:npiv] + pivots[npiv:]], axis=1)
    top = tuple(as_rows(part) for part in pivot_halves)
    gram = product(top, halves(mixed), NT)
    for i in range(nz * nc):
        gpart[i] = gram[i * gpart.shape[1] : (i + 1) * gpart.shape[1]]
    g_scatter = fan([(gpart.at[to[2] * nc + to[3]], gin.at[i], to) for i, to in fs], g_s.at[0], g_r.at[0], gin)
    set_block(top)
    scatter_rows(cpart, product((live_h[0], live_h[1]), (wt[0], wt[1]), NT))
    c_pair = pair_up(1, cpart, cpair)
    c_scatter = scatter(1, c_pair, cpart, cpair, chalf, cin)
    for d in order:
        k_forward(d)
    x_last = share(0, x_spread, xfull)
    d_last = share(2, d_spread, dfull)
    arrived([g_scatter])
    total = gpart[f]
    for i in range(len(fs)):
        total = total + gin[i]
    gfull[f] = total
    g_gather = fan([(gfull.at[f], gfull.at[f], to) for _, to in fs], g_s.at[1], g_r.at[1], gin)
    c_spread = spread(1, gathered(c_scatter, chalf, cin), cfull, cin)
    arrived([x_last, d_last])
    arrived([k_last])

    inner = halves(xfull[...].reshape(nb, nb))

    def times_inner(both):
        straight, across = product(both, inner, NN), product(both, inner, NT)
        return crossed(0.5 * (straight + across), 0.5 * (straight - across))

    proj_halves = by_parts(kall[...])
    proj = proj_halves[0].astype(F32) + proj_halves[1].astype(F32)
    taken = 2.0 * proj - times_inner(proj_halves)
    taken_halves = halves(taken)
    rest = halves(as_rows(proj - times_inner(taken_halves)))
    k_both = tuple(embedded(as_rows(part)) for part in proj_halves)
    t_rows = tuple(as_rows(part) for part in taken_halves)
    t_both = tuple(embedded(part) for part in t_rows)
    less = product(t_rows, k_both, NT) + product(rest, t_both, NT)
    cross_less = product(halves(dfull[...].reshape(rows, 2 * nb)), t_both, NT)
    taken = taken_halves
    set_block(halves(as_rows(pivots - crossed(product(taken, b_re, NN), product(taken, b_im, NN)))))
    w = (wt[0], wt[1])
    arrived([g_gather])

    gram = gfull[...].reshape(npiv, npiv)
    turned = gram.T
    gram = jnp.concatenate([0.5 * (gram + turned), 0.5 * (gram - turned)], axis=1) - less
    eye = lax.broadcasted_iota(jnp.int32, (npiv, emb), 0) == lax.broadcasted_iota(jnp.int32, (npiv, emb), 1)
    ident = eye.astype(F32)
    diag = gram * ident
    scale_col = 1.0 / jnp.sqrt(jnp.sum(diag, axis=1, keepdims=True) + EPSILON)
    scale_row = 1.0 / jnp.sqrt(jnp.sum(diag[:, :npiv], axis=0, keepdims=True) + EPSILON)
    scale_row = jnp.concatenate([scale_row, scale_row], axis=1)
    gram = gram * (scale_col * scale_row)
    bound = jnp.max(jnp.sum(jnp.abs(gram), axis=1, keepdims=True), axis=0, keepdims=True)
    your = gram / bound
    zed = None

    def times(left, right):
        return product(left, tuple(embedded(part) for part in right), NN)

    for step in range(NS_STEPS):
        if step == 3:
            c_last = share(1, c_spread, cfull)
        yh = halves(your)
        mix = your if zed is None else times(zh, yh)
        s = 1.5 * ident - 0.5 * mix
        sh = halves(s)
        if step < NS_STEPS - 1:
            your = times(yh, sh)
        zed = s if zed is None else times(sh, zh)
        zh = halves(zed)
    zed = zed * (1.0 / jnp.sqrt(bound))

    zed_e = tuple(embedded(part) for part in halves(zed))
    arrived([c_last])
    cross = cfull[...].reshape(rows, emb) - cross_less
    coef = product(halves(cross * scale_row), zed_e, NT)
    coef_re[...] = coef[:, :npiv]
    coef_im[...] = coef[:, npiv:]
    back = product(halves(product(halves(coef), zed_e, NN) * scale_row), w, NN)
    sums = []
    for part in blocks:
        mask = mask_of(part)
        real = (live[part, :bins] - back[part, :bins]) * mask
        imag = (live[part, bins:] - back[part, bins:]) * mask
        new_re[part, :] = real
        new_im[part, :] = imag
        square = real * real + imag * imag
        sums.append(sum(square[:, i : i + 128] for i in range(0, bins, 128)))
    ones = jnp.ones((8, 128), BF16)
    summed = sum(dot(ones, part, NT) for part in thirds(jnp.concatenate(sums, axis=0)))
    eout[...] = summed[0:1, :]
    ein[f] = summed[0:1, :]
    e_copies = fan([(eout, ein.at[f], to) for _, to in fs], e_s.at[0], e_r.at[0], ein.at[pl.ds(0, len(fs))])
    results = [(coef_re, out_coef_re), (coef_im, out_coef_im), (new_re, out_new_re), (new_im, out_new_im), (err, out_err)]
    results = [pltpu.make_async_copy(src, dst, out_s.at[i]) for i, (src, dst) in enumerate(results)]
    for result in results[:4]:
        result.start()
    arrived([e_copies])
    total = ein[0]
    for i in range(1, nz * nc):
        total = total + ein[i]
    err[...] = total / (BIN_BLOCK * vlen[...]).astype(F32)
    results[4].start()

    for copy in started + finals:
        copy.wait_send()
    for result in results:
        result.wait()


def handed_out(*refs):
    count = len(refs) // 2
    copies = [pltpu.make_async_copy(refs[i], refs[count + i], refs[-1].at[i]) for i in range(count)]
    for copy in copies:
        copy.start()
    for copy in copies:
        copy.wait()


def body(torus, res_re, res_im, basis_re, basis_im, lengths, pivots):
    nx, ny, nz, nc = torus
    rows, bins = res_re.shape
    nb = basis_re.shape[0]
    emb = 8 * nx * ny
    nf = nz * nc
    span = 8 * ny
    vmem = pltpu.VMEM
    dma = pltpu.SemaphoreType.DMA
    shapes = [(rows, emb // 2), (rows, emb // 2), (rows, bins), (rows, bins), (1, rows)]

    def summed(count, width):
        part = count // nf
        whole, across = vmem((nc, nz, part, width), F32), vmem((nz, part, width), F32)
        return [whole, across, across, vmem((nz - 1, part, width), F32), whole]

    scratch = [
        vmem((rows, 2 * bins), F32),
        vmem((2, rows, 2 * bins), BF16),
        vmem((2, nb, bins), F32),
        vmem((4, nb, bins), BF16),
        vmem((1, rows), jnp.int32),
        vmem((1, emb // 2), jnp.int32),
        vmem((emb, bins), F32),
        vmem((2, span, bins // 2), F32),
        vmem((2, span, bins // 2), F32),
        vmem((2, span, bins), F32),
        vmem((span, bins), F32),
        vmem((ny - 1, 8, bins), F32),
        vmem((8, nb), F32),
        vmem((nf - 1, 8, nb), F32),
        vmem((emb, bins), F32),
        vmem((emb, nb), F32),
        vmem((2, emb, 2 * bins), BF16),
        *[vmem(shape, F32) for shape in shapes],
        *summed(nb, nb),
        *[vmem((count, emb // 2 // nf, emb // 2), F32) for count in (nf, nf - 1, nf)],
        vmem(((nx - 1) * ny, 8, nb), F32),
        *summed(rows, emb),
        *summed(rows, 2 * nb),
        vmem((1, rows), F32), vmem((nf, 1, rows), F32),
        dma((6,)),
        *[dma((2, 2))] * 2, *[dma((1,))] * 2, *[dma((2, 2))] * 2, *[dma((1,))] * 4, *[dma((3,))] * 2,
        *[dma((1,)), dma((ny - 1,)), dma((1,)), dma((1,))] * 2,
        *[dma((3,))] * 6, *[dma((2,))] * 2, *[dma((1,))] * 2,
        dma((5,)),
    ]
    here = pl.BlockSpec(memory_space=pltpu.VMEM)
    there = pl.BlockSpec(memory_space=pl.ANY)
    results = pl.pallas_call(
        functools.partial(kernel, torus),
        out_shape=[vmem(shape, F32) for shape in shapes],
        in_specs=[there] * 6,
        out_specs=[there] * 5,
        scratch_shapes=scratch,
        compiler_params=pltpu.CompilerParams(collective_id=0, has_side_effects=True),
    )(res_re, res_im, basis_re, basis_im, lengths.reshape(1, rows), pivots.reshape(1, emb // 2))
    coef_re, coef_im, new_re, new_im, err = pl.pallas_call(
        handed_out,
        out_shape=[jax.ShapeDtypeStruct(shape, F32) for shape in shapes],
        in_specs=[here] * 5,
        out_specs=[there] * 5,
        scratch_shapes=[dma((5,))],
    )(*[pltpu.with_memory_space_constraint(result, pltpu.VMEM) for result in results])
    return coef_re, coef_im, new_re, new_im, err.reshape(rows)


def build(mesh, torus):
    axes = Mesh(mesh.devices.reshape(torus), AXES)
    wave, freq = ("x", "y"), ("z", "core")
    in_specs = (P(wave, freq), P(wave, freq), P(None, freq), P(None, freq), P(wave), P())
    out_specs = (P(wave, None), P(wave, None), P(wave, freq), P(wave, freq), P(wave))
    return jax.shard_map(
        functools.partial(body, torus), mesh=axes, in_specs=in_specs, out_specs=out_specs, check_vma=False
    )


def solution(mesh):
    return build(mesh, TORUS)
```

```python
import functools

import jax
import jax.numpy as jnp
from jax import lax
from jax.experimental import pallas as pl
from jax.experimental.pallas import tpu as pltpu
from jax.sharding import Mesh
from jax.sharding import PartitionSpec as P

BIN_BLOCK = 128
NS_STEPS = 6
EPSILON = 1e-06
TORUS = (4, 8, 8, 2)
AXES = ("x", "y", "z", "core")
F32 = jnp.float32
BF16 = jnp.bfloat16


def dot(left, right, dims):
    return lax.dot_general(left, right, (dims, ((), ())), preferred_element_type=F32)


NN = ((1,), (0,))
NT = ((1,), (1,))


def halves(a):
    high = a.astype(BF16)
    return high, (a - high.astype(F32)).astype(BF16)


def thirds(a):
    high = a.astype(BF16)
    rest = a - high.astype(F32)
    mid = rest.astype(BF16)
    return high, mid, (rest - mid.astype(F32)).astype(BF16)


def joined(left, right, dims):
    lh, ll = left
    rh, rl = right
    along = dims[1][0]
    return dot(jnp.concatenate([lh, ll, lh], axis=1), jnp.concatenate([rh, rh, rl], axis=along), dims)


def product(left, right, dims):
    lh, ll = left
    rh, rl = right
    rows = lh.shape[0]
    both = dot(jnp.concatenate([lh, ll], axis=0), rh, dims)
    return both[:rows] + (both[rows:] + dot(lh, rl, dims))


def chosen(select, a):
    parts = thirds(a)
    return dot(jnp.concatenate([select] * 3, axis=1), jnp.concatenate(parts, axis=0), NN)


def embedded(row):
    n = row.shape[1] // 2
    return jnp.concatenate([row, jnp.concatenate([-row[:, n:], row[:, :n]], axis=1)], axis=0)


def crossed(a, b):
    n = a.shape[0] // 2
    return jnp.concatenate([a[:n] - b[n:], a[n:] + b[:n]], axis=0)


def as_rows(a):
    n = a.shape[0] // 2
    return jnp.concatenate([a[:n], a[n:]], axis=1)


def short_product(chunk, rights, dims):
    high = chunk.astype(BF16).astype(F32)
    both = jnp.concatenate([high, chunk - high], axis=0).astype(BF16)
    out = []
    for rh, rl in rights:
        a = dot(both, rh, dims)
        b = dot(both, rl, dims)
        out.append((a[:8] + a[8:]) + (b[:8] + b[8:]))
    return out


def kernel(
    torus,
    res_re, res_im, basis_re, basis_im, lens, piv,
    out_coef_re, out_coef_im, out_new_re, out_new_im, out_err,
    live, live_h, basis, base, vlen, vpiv, picked, far, relay, near, ysum, yr, kout, kin, pall, kall, wt,
    coef_re, coef_im, new_re, new_im, err,
    xpart, xpair, xhalf, xin, xfull, gpart, gin, gfull, kspan,
    cpart, cpair, chalf, cin, cfull, dpart, dpair, dhalf, din, dfull, eout, ein,
    in_s, rf_s, rf_r, rn_s, rn_r, ry_s, ry_r, k_s, k_r, p_s, p_r, py_s, py_r, px_s, px_r, ky_s, ky_r, kx_s, kx_r,
    zs_s, zs_r, zg_s, zg_r, cz_r, c_s, c_r, g_s, g_r, e_s, e_r, out_s,
):
    nx, ny, nz, nc = torus
    x, y, z, c = (lax.axis_index(a) for a in AXES)
    f = z * nc + c
    rows, bins = res_re.shape
    emb = 8 * nx * ny
    npiv = emb // 2
    nb = basis_re.shape[0]
    span = 8 * ny

    def hops(d, n):
        return min(d, n - d)

    xs = [(d - 1, lax.rem(x + d, nx)) for d in sorted(range(1, nx), key=lambda d: -hops(d, nx))]
    ys = [(d - 1, lax.rem(y + d, ny)) for d in sorted(range(1, ny), key=lambda d: -hops(d, ny))]
    zs = [(d - 1, lax.rem(z + d, nz)) for d in sorted(range(1, nz), key=lambda d: -hops(d, nz))]
    fs = sorted(((dz, dc) for dz in range(nz) for dc in range(nc) if dz or dc), key=lambda d: -hops(d[0], nz))
    fs = [(dz * nc + dc - 1, (x, y, lax.rem(z + dz, nz), lax.rem(c + dc, nc))) for dz, dc in fs]
    barrier = pltpu.get_barrier_semaphore()
    peers = [to for _, to in fs] + [(x, p, z, c) for _, p in ys] + [(p, y, z, c) for _, p in xs]
    for peer in peers:
        pl.semaphore_signal(barrier, inc=1, device_id=peer, device_id_type=pl.DeviceIdType.MESH)
    loads = [(lens, vlen), (piv, vpiv), (res_re, live.at[:, pl.ds(0, bins)]), (res_im, live.at[:, pl.ds(bins, bins)])]
    loads += [(basis_re, basis.at[0]), (basis_im, basis.at[1])]
    loads = [pltpu.make_async_copy(src, dst, in_s.at[i]) for i, (src, dst) in enumerate(loads)]
    for load in loads:
        load.start()

    started = []
    anyone = fs[0][1]

    def described(src, dst, send, recv, to):
        return pltpu.make_async_remote_copy(
            src_ref=src, dst_ref=dst, send_sem=send, recv_sem=recv, device_id=to,
            device_id_type=pl.DeviceIdType.MESH,
        )

    def begin(src, dst, send, recv, to):
        copy = described(src, dst, send, recv, to)
        copy.start()
        return copy

    def push(src, dst, send, recv, to):
        copy = begin(src, dst, send, recv, to)
        started.append(copy)
        return copy

    def arrived(copies):
        for copy in copies:
            copy.wait_recv()

    finals = []

    def fan(pairs, send, recv, extent):
        for src, dst, to in pairs:
            begin(src, dst, send, recv, to)
        whole = described(extent, extent, send, recv, anyone)
        finals.append(whole)
        return whole

    def chunk_of(i, size):
        return pl.ds(pl.multiple_of(i * size, size), size)

    for load in loads[:4]:
        load.wait()
    diagonal = lax.broadcasted_iota(jnp.int32, (rows, rows), 0) == lax.broadcasted_iota(jnp.int32, (rows, rows), 1)
    ends = jnp.sum(jnp.where(diagonal, vlen[...] * BIN_BLOCK, 0).astype(F32), axis=1, keepdims=True)
    first_bin = f * bins

    def mask_of(part):
        count = part.stop - part.start
        at = first_bin + lax.broadcasted_iota(jnp.int32, (count, bins), 1)
        return (at.astype(F32) < ends[part, :]).astype(F32)

    blocks = [slice(r, min(r + 64, rows)) for r in range(0, rows, 64)]
    for part in blocks:
        mask = mask_of(part)
        live[part, :bins] = live[part, :bins] * mask
        live[part, bins:] = live[part, bins:] * mask
    to_row = lax.broadcasted_iota(jnp.int32, (emb, npiv), 0)
    of_row = lax.broadcasted_iota(jnp.int32, (emb, npiv), 1) == lax.rem(to_row, 4) * (nx * ny) + to_row // 8
    wanted = jnp.sum(jnp.where(of_row, vpiv[...], 0).astype(F32), axis=1, keepdims=True)
    own = (x * ny + y) * rows + lax.broadcasted_iota(jnp.int32, (emb, rows), 1)
    select = (wanted == own.astype(F32)).astype(F32).astype(BF16)
    is_im = lax.rem(lax.broadcasted_iota(jnp.int32, (emb, bins), 0), 8) // 4
    for i, value in enumerate(halves(live[...])):
        live_h[i] = value
    both = sum(dot(select, live_h[i], NN) for i in range(2))
    picked[...] = jnp.where(is_im == 0, both[:, :bins], both[:, bins:])

    pl.semaphore_wait(barrier, len(peers))

    half, piece = bins // 2, span // 2
    ahead, behind = pl.ds(0, half), pl.ds(half, half)
    right, left, across = (lax.rem(x + d, nx) for d in (1, nx - 1, 2))
    ways = (((right, y, z, c), right, ahead), ((left, y, z, c), left, behind))
    far_copies = []
    for i in range(2):
        for k, (to, _, lanes) in enumerate(ways):
            at = pl.ds(pl.multiple_of(across * span + i * piece, piece), piece)
            far_copies.append(
                begin(picked.at[at, lanes], far.at[k, pl.ds(i * piece, piece)], rf_s.at[0], rf_r.at[i, k], to)
            )

    for load in loads[4:]:
        load.wait()
    for i in range(2):
        high, low = halves(basis[i])
        base[2 * i] = high
        base[2 * i + 1] = low
    b_re = (base[0], base[1])
    b_im = (base[2], base[3])
    plus = jnp.concatenate([basis[0] + basis[1], basis[1] - basis[0]], axis=1)
    right_side = tuple(jnp.concatenate([base[i], base[2 + i]], axis=1) for i in range(2))
    both = joined(halves(plus), right_side, NT)

    def scatter_rows(part, value):
        size = part.shape[2]
        for i in range(nc):
            for j in range(nz):
                at = (i * nz + j) * size
                part[i, j] = value[at : at + size]

    def pair_up(k, part, got):
        return push(part.at[1 - c], got, p_s.at[k], p_r.at[k], (x, y, z, 1 - c))

    def scatter(k, pair, part, got, summed, inward):
        arrived([pair])
        summed[...] = part[c] + got[...]
        return fan([(summed.at[p], inward.at[i], (x, y, p, c)) for i, p in zs], zs_s.at[k], zs_r.at[k], inward)

    def gathered(copies, summed, inward):
        arrived([copies])
        total = summed[z]
        for i in range(nz - 1):
            total = total + inward[i]
        return total

    def spread(k, total, full, extent):
        full[c, z] = total
        at = full.at[c, z]
        return fan([(at, at, (x, y, p, c)) for i, p in zs], zg_s.at[k], zg_r.at[k], extent)

    def share(k, copies, full):
        arrived([copies])
        return push(full.at[c], full.at[c], c_s.at[k], c_r.at[k], (x, y, z, 1 - c))

    near_started = [
        (picked.at[chunk_of(next_x, span), other], near.at[k, :, other], to)
        for k, ((to, next_x, _), other) in enumerate(zip(ways, (behind, ahead)))
    ]
    for src, dst, to in near_started:
        begin(src, dst, rn_s.at[0], rn_r.at[0], to)
    near_begun = described(near, near, rn_s.at[0], rn_r.at[0], anyone)
    finals.append(near_begun)
    scatter_rows(xpart, both)
    x_pair = pair_up(0, xpart, xpair)
    turned_side = tuple(jnp.concatenate([-base[2 + i], base[i]], axis=1) for i in range(2))
    both = tuple(jnp.concatenate([right_side[i], turned_side[i]], axis=0) for i in range(2))
    scatter_rows(dpart, joined((live_h[0], live_h[1]), both, NT))
    x_scatter = scatter(0, x_pair, xpart, xpair, xhalf, xin)
    d_pair = pair_up(2, dpart, dpair)

    for i in range(2):
        for k, (to, next_x, lanes) in enumerate(ways):
            arrived([far_copies[2 * i + k]])
            at = pl.ds(pl.multiple_of(next_x * span + i * piece, piece), piece)
            part = pl.ds(i * piece, piece)
            relay[k, i * piece : (i + 1) * piece] = (
                picked[at, k * half : (k + 1) * half] + far[k, i * piece : (i + 1) * piece]
            )
            begin(relay.at[k, part], near.at[k, part, lanes], rn_s.at[0], rn_r.at[0], to)
    finals.append(described(far, far, rf_s.at[0], rf_r.at[0, 0], anyone))
    d_scatter = scatter(2, d_pair, dpart, dpair, dhalf, din)
    arrived([near_begun])
    ysum[...] = picked[chunk_of(x, span), :] + near[0] + near[1]
    y_copies = fan([(ysum.at[chunk_of(p, 8)], yr.at[i], (x, p, z, c)) for i, p in ys], ry_s.at[0], ry_r.at[0], yr)
    arrived([y_copies])
    chunk = ysum[chunk_of(y, 8), :]
    for i in range(ny - 1):
        chunk = chunk + yr[i]

    mine = x * ny + y
    order = sorted(range(1, ny), key=lambda d: min(d, ny - d))


    def gather(buf, sems, y_extent, x_extent):
        ysend, yrecv, xsend, xrecv = sems

        def rows_of(d):
            return buf.at[pl.ds(pl.multiple_of((x * ny + lax.rem(y + ny - d, ny)) * 8, 8), 8)]

        own_rows = rows_of(0)
        along_y = {
            i + 1: begin(own_rows, own_rows, ysend.at[0], yrecv.at[i], (x, p, z, c)) for i, p in ys
        }

        def forward(d):
            if d:
                arrived([along_y[d]])
            for _, p in xs:
                begin(rows_of(d), rows_of(d), xsend.at[0], xrecv.at[0], (p, y, z, c))

        forward(0)
        last = described(x_extent, x_extent, xsend.at[0], xrecv.at[0], anyone)
        finals.extend([described(y_extent, y_extent, ysend.at[0], yrecv.at[0], anyone), last])
        return forward, last

    pall[chunk_of(mine, 8), :] = chunk
    p_forward, p_last = gather(pall, (py_s, py_r, px_s, px_r), yr, picked.at[pl.ds(0, (nx - 1) * span)])
    sign_k = jnp.where(lax.broadcasted_iota(jnp.int32, (8, nb), 0) < 4, 1.0, -1.0).astype(F32)
    a, b = short_product(chunk, (b_re, b_im), NT)
    kout[...] = a + sign_k * pltpu.roll(b, 4, 0)
    k_copies = fan([(kout, kin.at[i], to) for i, to in fs], k_s.at[0], k_r.at[0], kin)
    x_spread = spread(0, gathered(x_scatter, xhalf, xin), xfull, xin)
    d_spread = spread(2, gathered(d_scatter, dhalf, din), dfull, din)
    for d in order:
        p_forward(d)
    arrived([k_copies])
    proj = kout[...]
    for i in range(len(fs)):
        proj = proj + kin[i]
    kall[chunk_of(mine, 8), :] = proj
    k_forward, k_last = gather(kall, (ky_s, ky_r, kx_s, kx_r), kin.at[pl.ds(0, ny - 1)], kspan)
    arrived([p_last])

    def set_block(top):
        n = top[0].shape[1] // 2
        for i, above in enumerate(top):
            wt[i, :npiv] = above
            wt[i, npiv:, :n] = -above[:, n:]
            wt[i, npiv:, n:] = above[:, :n]

    to_row = lax.broadcasted_iota(jnp.int32, (emb, emb), 0)
    from_row = lax.broadcasted_iota(jnp.int32, (emb, emb), 1)
    by_part = (from_row == lax.rem(to_row, nx * ny) * 8 + to_row // (nx * ny)).astype(F32).astype(BF16)

    def by_parts(a):
        return tuple(dot(by_part, part, NN).astype(BF16) for part in halves(a))

    pivot_halves = by_parts(pall[...])
    pivots = pivot_halves[0].astype(F32) + pivot_halves[1].astype(F32)
    mixed = jnp.concatenate([pivots[:npiv] - pivots[npiv:], pivots[:npiv] + pivots[npiv:]], axis=1)
    top = tuple(as_rows(part) for part in pivot_halves)
    gram = product(top, halves(mixed), NT)
    for i in range(nz * nc):
        gpart[i] = gram[i * gpart.shape[1] : (i + 1) * gpart.shape[1]]
    g_scatter = fan([(gpart.at[to[2] * nc + to[3]], gin.at[i], to) for i, to in fs], g_s.at[0], g_r.at[0], gin)
    set_block(top)
    scatter_rows(cpart, product((live_h[0], live_h[1]), (wt[0], wt[1]), NT))
    c_pair = pair_up(1, cpart, cpair)
    c_scatter = scatter(1, c_pair, cpart, cpair, chalf, cin)
    for d in order:
        k_forward(d)
    x_last = share(0, x_spread, xfull)
    d_last = share(2, d_spread, dfull)
    arrived([g_scatter])
    total = gpart[f]
    for i in range(len(fs)):
        total = total + gin[i]
    gfull[f] = total
    g_gather = fan([(gfull.at[f], gfull.at[f], to) for _, to in fs], g_s.at[1], g_r.at[1], gin)
    cfull[c, z] = gathered(c_scatter, chalf, cin)
    c_own = cfull.at[c, z]
    c_spread = {i: begin(c_own, c_own, zg_s.at[1], cz_r.at[i], (x, y, p, c)) for i, p in zs}
    begin(c_own, c_own, c_s.at[1], c_r.at[1], (x, y, z, 1 - c))
    c_last = described(cfull.at[c], cfull.at[c], c_s.at[1], c_r.at[1], anyone)
    finals.extend([described(cin, cin, zg_s.at[1], zg_r.at[1], anyone), c_last])
    arrived([x_last, d_last])
    arrived([k_last])

    inner = halves(xfull[...].reshape(nb, nb))

    def times_inner(both):
        straight, across = product(both, inner, NN), product(both, inner, NT)
        return crossed(0.5 * (straight + across), 0.5 * (straight - across))

    proj_halves = by_parts(kall[...])
    proj = proj_halves[0].astype(F32) + proj_halves[1].astype(F32)
    taken = 2.0 * proj - times_inner(proj_halves)
    taken_halves = halves(taken)
    rest = halves(as_rows(proj - times_inner(taken_halves)))
    k_both = tuple(embedded(as_rows(part)) for part in proj_halves)
    t_rows = tuple(as_rows(part) for part in taken_halves)
    t_both = tuple(embedded(part) for part in t_rows)
    less = product(t_rows, k_both, NT) + product(rest, t_both, NT)
    cross_less = product(halves(dfull[...].reshape(rows, 2 * nb)), t_both, NT)
    taken = taken_halves
    set_block(halves(as_rows(pivots - crossed(product(taken, b_re, NN), product(taken, b_im, NN)))))
    w = (wt[0], wt[1])
    arrived([g_gather])

    gram = gfull[...].reshape(npiv, npiv)
    turned = gram.T
    gram = jnp.concatenate([0.5 * (gram + turned), 0.5 * (gram - turned)], axis=1) - less
    eye = lax.broadcasted_iota(jnp.int32, (npiv, emb), 0) == lax.broadcasted_iota(jnp.int32, (npiv, emb), 1)
    ident = eye.astype(F32)
    diag = gram * ident
    scale_col = 1.0 / jnp.sqrt(jnp.sum(diag, axis=1, keepdims=True) + EPSILON)
    scale_row = 1.0 / jnp.sqrt(jnp.sum(diag[:, :npiv], axis=0, keepdims=True) + EPSILON)
    scale_row = jnp.concatenate([scale_row, scale_row], axis=1)
    gram = gram * (scale_col * scale_row)
    bound = jnp.max(jnp.sum(jnp.abs(gram), axis=1, keepdims=True), axis=0, keepdims=True)
    your = gram / bound
    zed = None

    def times(left, right):
        return product(left, tuple(embedded(part) for part in right), NN)

    for step in range(NS_STEPS):
        if step == NS_STEPS - 1:
            for i in sorted(range(nz - 1), key=lambda i: hops(i + 1, nz)):
                arrived([c_spread[i]])
                theirs = cfull.at[c, lax.rem(z + nz - 1 - i, nz)]
                begin(theirs, theirs, c_s.at[1], c_r.at[1], (x, y, z, 1 - c))
        yh = halves(your)
        mix = your if zed is None else times(zh, yh)
        s = 1.5 * ident - 0.5 * mix
        sh = halves(s)
        if step < NS_STEPS - 1:
            your = times(yh, sh)
        zed = s if zed is None else times(sh, zh)
        zh = halves(zed)
    zed = zed * (1.0 / jnp.sqrt(bound))

    zed_e = tuple(embedded(part) for part in halves(zed))
    arrived([c_last])
    cross = cfull[...].reshape(rows, emb) - cross_less
    coef = product(halves(cross * scale_row), zed_e, NT)
    coef_re[...] = coef[:, :npiv]
    coef_im[...] = coef[:, npiv:]
    back = product(halves(product(halves(coef), zed_e, NN) * scale_row), w, NN)
    sums = []
    for part in blocks:
        mask = mask_of(part)
        real = (live[part, :bins] - back[part, :bins]) * mask
        imag = (live[part, bins:] - back[part, bins:]) * mask
        new_re[part, :] = real
        new_im[part, :] = imag
        square = real * real + imag * imag
        sums.append(sum(square[:, i : i + 128] for i in range(0, bins, 128)))
    ones = jnp.ones((8, 128), BF16)
    summed = sum(dot(ones, part, NT) for part in thirds(jnp.concatenate(sums, axis=0)))
    eout[...] = summed[0:1, :]
    ein[f] = summed[0:1, :]
    e_copies = fan([(eout, ein.at[f], to) for _, to in fs], e_s.at[0], e_r.at[0], ein.at[pl.ds(0, len(fs))])
    results = [(coef_re, out_coef_re), (coef_im, out_coef_im), (new_re, out_new_re), (new_im, out_new_im), (err, out_err)]
    results = [pltpu.make_async_copy(src, dst, out_s.at[i]) for i, (src, dst) in enumerate(results)]
    for result in results[:4]:
        result.start()
    arrived([e_copies])
    total = ein[0]
    for i in range(1, nz * nc):
        total = total + ein[i]
    err[...] = total / (BIN_BLOCK * vlen[...]).astype(F32)
    results[4].start()

    for copy in started + finals:
        copy.wait_send()
    for result in results:
        result.wait()


def handed_out(*refs):
    count = len(refs) // 2
    copies = [pltpu.make_async_copy(refs[i], refs[count + i], refs[-1].at[i]) for i in range(count)]
    for copy in copies:
        copy.start()
    for copy in copies:
        copy.wait()


def body(torus, res_re, res_im, basis_re, basis_im, lengths, pivots):
    nx, ny, nz, nc = torus
    rows, bins = res_re.shape
    nb = basis_re.shape[0]
    emb = 8 * nx * ny
    nf = nz * nc
    span = 8 * ny
    vmem = pltpu.VMEM
    dma = pltpu.SemaphoreType.DMA
    shapes = [(rows, emb // 2), (rows, emb // 2), (rows, bins), (rows, bins), (1, rows)]

    def summed(count, width):
        part = count // nf
        whole, across = vmem((nc, nz, part, width), F32), vmem((nz, part, width), F32)
        return [whole, across, across, vmem((nz - 1, part, width), F32), whole]

    scratch = [
        vmem((rows, 2 * bins), F32),
        vmem((2, rows, 2 * bins), BF16),
        vmem((2, nb, bins), F32),
        vmem((4, nb, bins), BF16),
        vmem((1, rows), jnp.int32),
        vmem((1, emb // 2), jnp.int32),
        vmem((emb, bins), F32),
        vmem((2, span, bins // 2), F32),
        vmem((2, span, bins // 2), F32),
        vmem((2, span, bins), F32),
        vmem((span, bins), F32),
        vmem((ny - 1, 8, bins), F32),
        vmem((8, nb), F32),
        vmem((nf - 1, 8, nb), F32),
        vmem((emb, bins), F32),
        vmem((emb, nb), F32),
        vmem((2, emb, 2 * bins), BF16),
        *[vmem(shape, F32) for shape in shapes],
        *summed(nb, nb),
        *[vmem((count, emb // 2 // nf, emb // 2), F32) for count in (nf, nf - 1, nf)],
        vmem(((nx - 1) * ny, 8, nb), F32),
        *summed(rows, emb),
        *summed(rows, 2 * nb),
        vmem((1, rows), F32), vmem((nf, 1, rows), F32),
        dma((6,)),
        dma((1,)), dma((2, 2)), *[dma((1,))] * 6, *[dma((3,))] * 2,
        *[dma((1,)), dma((ny - 1,)), dma((1,)), dma((1,))] * 2,
        *[dma((3,))] * 4, dma((nz - 1,)), *[dma((3,))] * 2, *[dma((2,))] * 2, *[dma((1,))] * 2,
        dma((5,)),
    ]
    here = pl.BlockSpec(memory_space=pltpu.VMEM)
    there = pl.BlockSpec(memory_space=pl.ANY)
    results = pl.pallas_call(
        functools.partial(kernel, torus),
        out_shape=[vmem(shape, F32) for shape in shapes],
        in_specs=[there] * 6,
        out_specs=[there] * 5,
        scratch_shapes=scratch,
        compiler_params=pltpu.CompilerParams(collective_id=0, has_side_effects=True),
    )(res_re, res_im, basis_re, basis_im, lengths.reshape(1, rows), pivots.reshape(1, emb // 2))
    coef_re, coef_im, new_re, new_im, err = pl.pallas_call(
        handed_out,
        out_shape=[jax.ShapeDtypeStruct(shape, F32) for shape in shapes],
        in_specs=[here] * 5,
        out_specs=[there] * 5,
        scratch_shapes=[dma((5,))],
    )(*[pltpu.with_memory_space_constraint(result, pltpu.VMEM) for result in results])
    return coef_re, coef_im, new_re, new_im, err.reshape(rows)


def build(mesh, torus):
    axes = Mesh(mesh.devices.reshape(torus), AXES)
    wave, freq = ("x", "y"), ("z", "core")
    in_specs = (P(wave, freq), P(wave, freq), P(None, freq), P(None, freq), P(wave), P())
    out_specs = (P(wave, None), P(wave, None), P(wave, freq), P(wave, freq), P(wave))
    return jax.shard_map(
        functools.partial(body, torus), mesh=axes, in_specs=in_specs, out_specs=out_specs, check_vma=False
    )


def solution(mesh):
    return build(mesh, TORUS)
```

```python
import functools

import jax
import jax.numpy as jnp
from jax import lax
from jax.experimental import pallas as pl
from jax.experimental.pallas import tpu as pltpu
from jax.sharding import Mesh
from jax.sharding import PartitionSpec as P

BIN_BLOCK = 128
NS_STEPS = 6
EPSILON = 1e-06
TORUS = (4, 8, 8, 2)
AXES = ("x", "y", "z", "core")
F32 = jnp.float32
BF16 = jnp.bfloat16


def dot(left, right, dims):
    return lax.dot_general(left, right, (dims, ((), ())), preferred_element_type=F32)


NN = ((1,), (0,))
NT = ((1,), (1,))


def halves(a):
    high = a.astype(BF16)
    return high, (a - high.astype(F32)).astype(BF16)


def thirds(a):
    high = a.astype(BF16)
    rest = a - high.astype(F32)
    mid = rest.astype(BF16)
    return high, mid, (rest - mid.astype(F32)).astype(BF16)


def joined(left, right, dims):
    lh, ll = left
    rh, rl = right
    along = dims[1][0]
    return dot(jnp.concatenate([lh, ll, lh], axis=1), jnp.concatenate([rh, rh, rl], axis=along), dims)


def product(left, right, dims):
    lh, ll = left
    rh, rl = right
    rows = lh.shape[0]
    both = dot(jnp.concatenate([lh, ll], axis=0), rh, dims)
    return both[:rows] + (both[rows:] + dot(lh, rl, dims))


def chosen(select, a):
    parts = thirds(a)
    return dot(jnp.concatenate([select] * 3, axis=1), jnp.concatenate(parts, axis=0), NN)


def embedded(row):
    n = row.shape[1] // 2
    return jnp.concatenate([row, jnp.concatenate([-row[:, n:], row[:, :n]], axis=1)], axis=0)


def crossed(a, b):
    n = a.shape[0] // 2
    return jnp.concatenate([a[:n] - b[n:], a[n:] + b[:n]], axis=0)


def as_rows(a):
    n = a.shape[0] // 2
    return jnp.concatenate([a[:n], a[n:]], axis=1)


def short_product(chunk, rights, dims):
    high = chunk.astype(BF16).astype(F32)
    both = jnp.concatenate([high, chunk - high], axis=0).astype(BF16)
    out = []
    for rh, rl in rights:
        a = dot(both, rh, dims)
        b = dot(both, rl, dims)
        out.append((a[:8] + a[8:]) + (b[:8] + b[8:]))
    return out


def kernel(
    torus,
    res_re, res_im, basis_re, basis_im, lens, piv,
    out_coef_re, out_coef_im, out_new_re, out_new_im, out_err,
    live, live_h, basis, base, vlen, vpiv, picked, far, relay, near, ysum, yr, kout, kin, pall, kall, wt,
    coef_re, coef_im, new_re, new_im, err,
    xpart, xpair, xhalf, xin, xfull, gpart, gin, gfull, kspan,
    cpart, cpair, chalf, cin, cfull, dpart, dpair, dhalf, din, dfull, eout, ein,
    in_s, rf_s, rf_r, rn_s, rn_r, ry_s, ry_r, k_s, k_r, p_s, p_r, py_s, py_r, px_s, px_r, ky_s, ky_r, kx_s, kx_r,
    zs_s, zs_r, zg_s, zg_r, cz_r, c_s, c_r, g_s, g_r, e_s, e_r, out_s,
):
    nx, ny, nz, nc = torus
    x, y, z, c = (lax.axis_index(a) for a in AXES)
    f = z * nc + c
    rows, bins = res_re.shape
    emb = 8 * nx * ny
    npiv = emb // 2
    nb = basis_re.shape[0]
    span = 8 * ny

    def hops(d, n):
        return min(d, n - d)

    xs = [(d - 1, lax.rem(x + d, nx)) for d in sorted(range(1, nx), key=lambda d: -hops(d, nx))]
    ys = [(d - 1, lax.rem(y + d, ny)) for d in sorted(range(1, ny), key=lambda d: -hops(d, ny))]
    zs = [(d - 1, lax.rem(z + d, nz)) for d in sorted(range(1, nz), key=lambda d: -hops(d, nz))]
    fs = sorted(((dz, dc) for dz in range(nz) for dc in range(nc) if dz or dc), key=lambda d: -hops(d[0], nz))
    fs = [(dz * nc + dc - 1, (x, y, lax.rem(z + dz, nz), lax.rem(c + dc, nc))) for dz, dc in fs]
    barrier = pltpu.get_barrier_semaphore()
    peers = [(hops(i + 1, ny), (x, p, z, c)) for i, p in ys] + [(hops(i + 1, nx), (p, y, z, c)) for i, p in xs]
    peers += [(hops((i + 1) // nc, nz), to) for i, to in fs]
    peers = [to for _, to in sorted(peers, key=lambda peer: -peer[0])]
    for peer in peers:
        pl.semaphore_signal(barrier, inc=1, device_id=peer, device_id_type=pl.DeviceIdType.MESH)
    loads = [(lens, vlen), (piv, vpiv), (res_re, live.at[:, pl.ds(0, bins)]), (res_im, live.at[:, pl.ds(bins, bins)])]
    loads += [(basis_re, basis.at[0]), (basis_im, basis.at[1])]
    loads = [pltpu.make_async_copy(src, dst, in_s.at[i]) for i, (src, dst) in enumerate(loads)]
    for load in loads:
        load.start()

    started = []
    anyone = fs[0][1]

    def described(src, dst, send, recv, to):
        return pltpu.make_async_remote_copy(
            src_ref=src, dst_ref=dst, send_sem=send, recv_sem=recv, device_id=to,
            device_id_type=pl.DeviceIdType.MESH,
        )

    def begin(src, dst, send, recv, to):
        copy = described(src, dst, send, recv, to)
        copy.start()
        return copy

    def push(src, dst, send, recv, to):
        copy = begin(src, dst, send, recv, to)
        started.append(copy)
        return copy

    def arrived(copies):
        for copy in copies:
            copy.wait_recv()

    finals = []

    def fan(pairs, send, recv, extent):
        for src, dst, to in pairs:
            begin(src, dst, send, recv, to)
        whole = described(extent, extent, send, recv, anyone)
        finals.append(whole)
        return whole

    def chunk_of(i, size):
        return pl.ds(pl.multiple_of(i * size, size), size)

    for load in loads[:4]:
        load.wait()
    diagonal = lax.broadcasted_iota(jnp.int32, (rows, rows), 0) == lax.broadcasted_iota(jnp.int32, (rows, rows), 1)
    ends = jnp.sum(jnp.where(diagonal, vlen[...] * BIN_BLOCK, 0).astype(F32), axis=1, keepdims=True)
    first_bin = f * bins

    def mask_of(part):
        count = part.stop - part.start
        at = first_bin + lax.broadcasted_iota(jnp.int32, (count, bins), 1)
        return (at.astype(F32) < ends[part, :]).astype(F32)

    blocks = [slice(r, min(r + 64, rows)) for r in range(0, rows, 64)]
    for part in blocks:
        mask = mask_of(part)
        live[part, :bins] = live[part, :bins] * mask
        live[part, bins:] = live[part, bins:] * mask
    to_row = lax.broadcasted_iota(jnp.int32, (emb, npiv), 0)
    of_row = lax.broadcasted_iota(jnp.int32, (emb, npiv), 1) == lax.rem(to_row, 4) * (nx * ny) + to_row // 8
    wanted = jnp.sum(jnp.where(of_row, vpiv[...], 0).astype(F32), axis=1, keepdims=True)
    own = (x * ny + y) * rows + lax.broadcasted_iota(jnp.int32, (emb, rows), 1)
    select = (wanted == own.astype(F32)).astype(F32).astype(BF16)
    is_im = lax.rem(lax.broadcasted_iota(jnp.int32, (emb, bins), 0), 8) // 4
    for i, value in enumerate(halves(live[...])):
        live_h[i] = value
    both = sum(dot(select, live_h[i], NN) for i in range(2))
    picked[...] = jnp.where(is_im == 0, both[:, :bins], both[:, bins:])

    pl.semaphore_wait(barrier, len(peers))

    half, pieces = bins // 2, 4
    piece = span // pieces
    ahead, behind = pl.ds(0, half), pl.ds(half, half)
    right, left, across = (lax.rem(x + d, nx) for d in (1, nx - 1, 2))
    ways = (((right, y, z, c), right, ahead), ((left, y, z, c), left, behind))
    far_copies = []
    for i in range(pieces):
        for k, (to, _, lanes) in enumerate(ways):
            at = pl.ds(pl.multiple_of(across * span + i * piece, piece), piece)
            far_copies.append(
                begin(picked.at[at, lanes], far.at[k, pl.ds(i * piece, piece)], rf_s.at[0], rf_r.at[i, k], to)
            )

    for load in loads[4:]:
        load.wait()
    for i in range(2):
        high, low = halves(basis[i])
        base[2 * i] = high
        base[2 * i + 1] = low
    b_re = (base[0], base[1])
    b_im = (base[2], base[3])
    plus = jnp.concatenate([basis[0] + basis[1], basis[1] - basis[0]], axis=1)
    right_side = tuple(jnp.concatenate([base[i], base[2 + i]], axis=1) for i in range(2))
    both = joined(halves(plus), right_side, NT)

    def scatter_rows(part, value):
        size = part.shape[2]
        for i in range(nc):
            for j in range(nz):
                at = (i * nz + j) * size
                part[i, j] = value[at : at + size]

    def pair_up(k, part, got):
        return push(part.at[1 - c], got, p_s.at[k], p_r.at[k], (x, y, z, 1 - c))

    def scatter(k, pair, part, got, summed, inward):
        arrived([pair])
        summed[...] = part[c] + got[...]
        return fan([(summed.at[p], inward.at[i], (x, y, p, c)) for i, p in zs], zs_s.at[k], zs_r.at[k], inward)

    def gathered(copies, summed, inward):
        arrived([copies])
        total = summed[z]
        for i in range(nz - 1):
            total = total + inward[i]
        return total

    def spread(k, total, full, extent):
        full[c, z] = total
        at = full.at[c, z]
        return fan([(at, at, (x, y, p, c)) for i, p in zs], zg_s.at[k], zg_r.at[k], extent)

    def share(k, copies, full):
        arrived([copies])
        return push(full.at[c], full.at[c], c_s.at[k], c_r.at[k], (x, y, z, 1 - c))

    near_started = [
        (picked.at[chunk_of(next_x, span), other], near.at[k, :, other], to)
        for k, ((to, next_x, _), other) in enumerate(zip(ways, (behind, ahead)))
    ]
    for src, dst, to in near_started:
        begin(src, dst, rn_s.at[0], rn_r.at[0], to)
    near_begun = described(near, near, rn_s.at[0], rn_r.at[0], anyone)
    finals.append(near_begun)
    scatter_rows(xpart, both)
    x_pair = pair_up(0, xpart, xpair)
    turned_side = tuple(jnp.concatenate([-base[2 + i], base[i]], axis=1) for i in range(2))
    both = tuple(jnp.concatenate([right_side[i], turned_side[i]], axis=0) for i in range(2))
    scatter_rows(dpart, joined((live_h[0], live_h[1]), both, NT))
    x_scatter = scatter(0, x_pair, xpart, xpair, xhalf, xin)
    d_pair = pair_up(2, dpart, dpair)

    for i in range(pieces):
        for k, (to, next_x, lanes) in enumerate(ways):
            arrived([far_copies[2 * i + k]])
            at = pl.ds(pl.multiple_of(next_x * span + i * piece, piece), piece)
            part = pl.ds(i * piece, piece)
            relay[k, i * piece : (i + 1) * piece] = (
                picked[at, k * half : (k + 1) * half] + far[k, i * piece : (i + 1) * piece]
            )
            begin(relay.at[k, part], near.at[k, part, lanes], rn_s.at[0], rn_r.at[0], to)
    finals.append(described(far, far, rf_s.at[0], rf_r.at[0, 0], anyone))
    d_scatter = scatter(2, d_pair, dpart, dpair, dhalf, din)
    arrived([near_begun])
    ysum[...] = picked[chunk_of(x, span), :] + near[0] + near[1]
    y_copies = fan([(ysum.at[chunk_of(p, 8)], yr.at[i], (x, p, z, c)) for i, p in ys], ry_s.at[0], ry_r.at[0], yr)
    arrived([y_copies])
    chunk = ysum[chunk_of(y, 8), :]
    for i in range(ny - 1):
        chunk = chunk + yr[i]

    mine = x * ny + y
    order = sorted(range(1, ny), key=lambda d: min(d, ny - d))


    def gather(buf, sems, y_extent, x_extent):
        ysend, yrecv, xsend, xrecv = sems

        def rows_of(d):
            return buf.at[pl.ds(pl.multiple_of((x * ny + lax.rem(y + ny - d, ny)) * 8, 8), 8)]

        own_rows = rows_of(0)
        along_y = {
            i + 1: begin(own_rows, own_rows, ysend.at[0], yrecv.at[i], (x, p, z, c)) for i, p in ys
        }

        def forward(d):
            if d:
                arrived([along_y[d]])
            for _, p in xs:
                begin(rows_of(d), rows_of(d), xsend.at[0], xrecv.at[0], (p, y, z, c))

        forward(0)
        last = described(x_extent, x_extent, xsend.at[0], xrecv.at[0], anyone)
        finals.extend([described(y_extent, y_extent, ysend.at[0], yrecv.at[0], anyone), last])
        return forward, last

    pall[chunk_of(mine, 8), :] = chunk
    p_forward, p_last = gather(pall, (py_s, py_r, px_s, px_r), yr, picked.at[pl.ds(0, (nx - 1) * span)])
    sign_k = jnp.where(lax.broadcasted_iota(jnp.int32, (8, nb), 0) < 4, 1.0, -1.0).astype(F32)
    a, b = short_product(chunk, (b_re, b_im), NT)
    kout[...] = a + sign_k * pltpu.roll(b, 4, 0)
    k_copies = fan([(kout, kin.at[i], to) for i, to in fs], k_s.at[0], k_r.at[0], kin)
    x_spread = spread(0, gathered(x_scatter, xhalf, xin), xfull, xin)
    d_spread = spread(2, gathered(d_scatter, dhalf, din), dfull, din)
    for d in order:
        p_forward(d)
    arrived([k_copies])
    proj = kout[...]
    for i in range(len(fs)):
        proj = proj + kin[i]
    kall[chunk_of(mine, 8), :] = proj
    k_forward, k_last = gather(kall, (ky_s, ky_r, kx_s, kx_r), kin.at[pl.ds(0, ny - 1)], kspan)
    arrived([p_last])

    def set_block(top):
        n = top[0].shape[1] // 2
        for i, above in enumerate(top):
            wt[i, :npiv] = above
            wt[i, npiv:, :n] = -above[:, n:]
            wt[i, npiv:, n:] = above[:, :n]

    to_row = lax.broadcasted_iota(jnp.int32, (emb, emb), 0)
    from_row = lax.broadcasted_iota(jnp.int32, (emb, emb), 1)
    by_part = (from_row == lax.rem(to_row, nx * ny) * 8 + to_row // (nx * ny)).astype(F32).astype(BF16)

    def by_parts(a):
        return tuple(dot(by_part, part, NN).astype(BF16) for part in halves(a))

    pivot_halves = by_parts(pall[...])
    pivots = pivot_halves[0].astype(F32) + pivot_halves[1].astype(F32)
    mixed = jnp.concatenate([pivots[:npiv] - pivots[npiv:], pivots[:npiv] + pivots[npiv:]], axis=1)
    top = tuple(as_rows(part) for part in pivot_halves)
    gram = product(top, halves(mixed), NT)
    for i in range(nz * nc):
        gpart[i] = gram[i * gpart.shape[1] : (i + 1) * gpart.shape[1]]
    g_scatter = fan([(gpart.at[to[2] * nc + to[3]], gin.at[i], to) for i, to in fs], g_s.at[0], g_r.at[0], gin)
    set_block(top)
    scatter_rows(cpart, product((live_h[0], live_h[1]), (wt[0], wt[1]), NT))
    c_pair = pair_up(1, cpart, cpair)
    c_scatter = scatter(1, c_pair, cpart, cpair, chalf, cin)
    for d in order:
        k_forward(d)
    x_last = share(0, x_spread, xfull)
    d_last = share(2, d_spread, dfull)
    arrived([g_scatter])
    total = gpart[f]
    for i in range(len(fs)):
        total = total + gin[i]
    gfull[f] = total
    g_gather = fan([(gfull.at[f], gfull.at[f], to) for _, to in fs], g_s.at[1], g_r.at[1], gin)
    cfull[c, z] = gathered(c_scatter, chalf, cin)
    c_own = cfull.at[c, z]
    c_spread = {i: begin(c_own, c_own, zg_s.at[1], cz_r.at[i], (x, y, p, c)) for i, p in zs}
    begin(c_own, c_own, c_s.at[1], c_r.at[1], (x, y, z, 1 - c))
    c_last = described(cfull.at[c], cfull.at[c], c_s.at[1], c_r.at[1], anyone)
    finals.extend([described(cin, cin, zg_s.at[1], zg_r.at[1], anyone), c_last])
    arrived([x_last, d_last])
    arrived([k_last])

    inner = halves(xfull[...].reshape(nb, nb))

    def times_inner(both):
        straight, across = product(both, inner, NN), product(both, inner, NT)
        return crossed(0.5 * (straight + across), 0.5 * (straight - across))

    proj_halves = by_parts(kall[...])
    proj = proj_halves[0].astype(F32) + proj_halves[1].astype(F32)
    taken = 2.0 * proj - times_inner(proj_halves)
    taken_halves = halves(taken)
    rest = halves(as_rows(proj - times_inner(taken_halves)))
    k_both = tuple(embedded(as_rows(part)) for part in proj_halves)
    t_rows = tuple(as_rows(part) for part in taken_halves)
    t_both = tuple(embedded(part) for part in t_rows)
    less = product(t_rows, k_both, NT) + product(rest, t_both, NT)
    cross_less = product(halves(dfull[...].reshape(rows, 2 * nb)), t_both, NT)
    taken = taken_halves
    set_block(halves(as_rows(pivots - crossed(product(taken, b_re, NN), product(taken, b_im, NN)))))
    w = (wt[0], wt[1])
    arrived([g_gather])

    gram = gfull[...].reshape(npiv, npiv)
    turned = gram.T
    gram = jnp.concatenate([0.5 * (gram + turned), 0.5 * (gram - turned)], axis=1) - less
    eye = lax.broadcasted_iota(jnp.int32, (npiv, emb), 0) == lax.broadcasted_iota(jnp.int32, (npiv, emb), 1)
    ident = eye.astype(F32)
    diag = gram * ident
    scale_col = 1.0 / jnp.sqrt(jnp.sum(diag, axis=1, keepdims=True) + EPSILON)
    scale_row = 1.0 / jnp.sqrt(jnp.sum(diag[:, :npiv], axis=0, keepdims=True) + EPSILON)
    scale_row = jnp.concatenate([scale_row, scale_row], axis=1)
    gram = gram * (scale_col * scale_row)
    bound = jnp.max(jnp.sum(jnp.abs(gram), axis=1, keepdims=True), axis=0, keepdims=True)
    your = gram / bound
    zed = None

    def times(left, right):
        return product(left, tuple(embedded(part) for part in right), NN)

    for step in range(NS_STEPS):
        if step == NS_STEPS - 1:
            for i in sorted(range(nz - 1), key=lambda i: hops(i + 1, nz)):
                arrived([c_spread[i]])
                theirs = cfull.at[c, lax.rem(z + nz - 1 - i, nz)]
                begin(theirs, theirs, c_s.at[1], c_r.at[1], (x, y, z, 1 - c))
        yh = halves(your)
        mix = your if zed is None else times(zh, yh)
        s = 1.5 * ident - 0.5 * mix
        sh = halves(s)
        if step < NS_STEPS - 1:
            your = times(yh, sh)
        zed = s if zed is None else times(sh, zh)
        zh = halves(zed)
    zed = zed * (1.0 / jnp.sqrt(bound))

    zed_e = tuple(embedded(part) for part in halves(zed))
    arrived([c_last])
    cross = cfull[...].reshape(rows, emb) - cross_less
    coef = product(halves(cross * scale_row), zed_e, NT)
    coef_re[...] = coef[:, :npiv]
    coef_im[...] = coef[:, npiv:]
    back = product(halves(product(halves(coef), zed_e, NN) * scale_row), w, NN)
    sums = []
    for part in blocks:
        mask = mask_of(part)
        real = (live[part, :bins] - back[part, :bins]) * mask
        imag = (live[part, bins:] - back[part, bins:]) * mask
        new_re[part, :] = real
        new_im[part, :] = imag
        square = real * real + imag * imag
        sums.append(sum(square[:, i : i + 128] for i in range(0, bins, 128)))
    ones = jnp.ones((8, 128), BF16)
    summed = sum(dot(ones, part, NT) for part in thirds(jnp.concatenate(sums, axis=0)))
    eout[...] = summed[0:1, :]
    ein[f] = summed[0:1, :]
    e_copies = fan([(eout, ein.at[f], to) for _, to in fs], e_s.at[0], e_r.at[0], ein.at[pl.ds(0, len(fs))])
    results = [(coef_re, out_coef_re), (coef_im, out_coef_im), (new_re, out_new_re), (new_im, out_new_im), (err, out_err)]
    results = [pltpu.make_async_copy(src, dst, out_s.at[i]) for i, (src, dst) in enumerate(results)]
    for result in results[:4]:
        result.start()
    arrived([e_copies])
    total = ein[0]
    for i in range(1, nz * nc):
        total = total + ein[i]
    err[...] = total / (BIN_BLOCK * vlen[...]).astype(F32)
    results[4].start()

    for copy in started + finals:
        copy.wait_send()
    for result in results:
        result.wait()


def handed_out(*refs):
    count = len(refs) // 2
    copies = [pltpu.make_async_copy(refs[i], refs[count + i], refs[-1].at[i]) for i in range(count)]
    for copy in copies:
        copy.start()
    for copy in copies:
        copy.wait()


def body(torus, res_re, res_im, basis_re, basis_im, lengths, pivots):
    nx, ny, nz, nc = torus
    rows, bins = res_re.shape
    nb = basis_re.shape[0]
    emb = 8 * nx * ny
    nf = nz * nc
    span = 8 * ny
    vmem = pltpu.VMEM
    dma = pltpu.SemaphoreType.DMA
    shapes = [(rows, emb // 2), (rows, emb // 2), (rows, bins), (rows, bins), (1, rows)]

    def summed(count, width):
        part = count // nf
        whole, across = vmem((nc, nz, part, width), F32), vmem((nz, part, width), F32)
        return [whole, across, across, vmem((nz - 1, part, width), F32), whole]

    scratch = [
        vmem((rows, 2 * bins), F32),
        vmem((2, rows, 2 * bins), BF16),
        vmem((2, nb, bins), F32),
        vmem((4, nb, bins), BF16),
        vmem((1, rows), jnp.int32),
        vmem((1, emb // 2), jnp.int32),
        vmem((emb, bins), F32),
        vmem((2, span, bins // 2), F32),
        vmem((2, span, bins // 2), F32),
        vmem((2, span, bins), F32),
        vmem((span, bins), F32),
        vmem((ny - 1, 8, bins), F32),
        vmem((8, nb), F32),
        vmem((nf - 1, 8, nb), F32),
        vmem((emb, bins), F32),
        vmem((emb, nb), F32),
        vmem((2, emb, 2 * bins), BF16),
        *[vmem(shape, F32) for shape in shapes],
        *summed(nb, nb),
        *[vmem((count, emb // 2 // nf, emb // 2), F32) for count in (nf, nf - 1, nf)],
        vmem(((nx - 1) * ny, 8, nb), F32),
        *summed(rows, emb),
        *summed(rows, 2 * nb),
        vmem((1, rows), F32), vmem((nf, 1, rows), F32),
        dma((6,)),
        dma((1,)), dma((4, 2)), *[dma((1,))] * 6, *[dma((3,))] * 2,
        *[dma((1,)), dma((ny - 1,)), dma((1,)), dma((1,))] * 2,
        *[dma((3,))] * 4, dma((nz - 1,)), *[dma((3,))] * 2, *[dma((2,))] * 2, *[dma((1,))] * 2,
        dma((5,)),
    ]
    here = pl.BlockSpec(memory_space=pltpu.VMEM)
    there = pl.BlockSpec(memory_space=pl.ANY)
    results = pl.pallas_call(
        functools.partial(kernel, torus),
        out_shape=[vmem(shape, F32) for shape in shapes],
        in_specs=[there] * 6,
        out_specs=[there] * 5,
        scratch_shapes=scratch,
        compiler_params=pltpu.CompilerParams(collective_id=0, has_side_effects=True),
    )(res_re, res_im, basis_re, basis_im, lengths.reshape(1, rows), pivots.reshape(1, emb // 2))
    coef_re, coef_im, new_re, new_im, err = pl.pallas_call(
        handed_out,
        out_shape=[jax.ShapeDtypeStruct(shape, F32) for shape in shapes],
        in_specs=[here] * 5,
        out_specs=[there] * 5,
        scratch_shapes=[dma((5,))],
    )(*[pltpu.with_memory_space_constraint(result, pltpu.VMEM) for result in results])
    return coef_re, coef_im, new_re, new_im, err.reshape(rows)


def build(mesh, torus):
    axes = Mesh(mesh.devices.reshape(torus), AXES)
    wave, freq = ("x", "y"), ("z", "core")
    in_specs = (P(wave, freq), P(wave, freq), P(None, freq), P(None, freq), P(wave), P())
    out_specs = (P(wave, None), P(wave, None), P(wave, freq), P(wave, freq), P(wave))
    return jax.shard_map(
        functools.partial(body, torus), mesh=axes, in_specs=in_specs, out_specs=out_specs, check_vma=False
    )


def solution(mesh):
    return build(mesh, TORUS)
```

```python
import functools

import jax
import jax.numpy as jnp
from jax import lax
from jax.experimental import pallas as pl
from jax.experimental.pallas import tpu as pltpu
from jax.sharding import Mesh
from jax.sharding import PartitionSpec as P

BIN_BLOCK = 128
NS_STEPS = 6
EPSILON = 1e-06
TORUS = (4, 8, 8, 2)
AXES = ("x", "y", "z", "core")
F32 = jnp.float32
BF16 = jnp.bfloat16


def dot(left, right, dims):
    return lax.dot_general(left, right, (dims, ((), ())), preferred_element_type=F32)


NN = ((1,), (0,))
NT = ((1,), (1,))


def halves(a):
    high = a.astype(BF16)
    return high, (a - high.astype(F32)).astype(BF16)


def thirds(a):
    high = a.astype(BF16)
    rest = a - high.astype(F32)
    mid = rest.astype(BF16)
    return high, mid, (rest - mid.astype(F32)).astype(BF16)


def joined(left, right, dims):
    lh, ll = left
    rh, rl = right
    along = dims[1][0]
    return dot(jnp.concatenate([lh, ll, lh], axis=1), jnp.concatenate([rh, rh, rl], axis=along), dims)


def product(left, right, dims):
    lh, ll = left
    rh, rl = right
    rows = lh.shape[0]
    both = dot(jnp.concatenate([lh, ll], axis=0), rh, dims)
    return both[:rows] + (both[rows:] + dot(lh, rl, dims))


def chosen(select, a):
    parts = thirds(a)
    return dot(jnp.concatenate([select] * 3, axis=1), jnp.concatenate(parts, axis=0), NN)


def embedded(row):
    n = row.shape[1] // 2
    return jnp.concatenate([row, jnp.concatenate([-row[:, n:], row[:, :n]], axis=1)], axis=0)


def crossed(a, b):
    n = a.shape[0] // 2
    return jnp.concatenate([a[:n] - b[n:], a[n:] + b[:n]], axis=0)


def as_rows(a):
    n = a.shape[0] // 2
    return jnp.concatenate([a[:n], a[n:]], axis=1)


def short_product(chunk, rights, dims):
    high = chunk.astype(BF16).astype(F32)
    both = jnp.concatenate([high, chunk - high], axis=0).astype(BF16)
    out = []
    for rh, rl in rights:
        a = dot(both, rh, dims)
        b = dot(both, rl, dims)
        out.append((a[:8] + a[8:]) + (b[:8] + b[8:]))
    return out


def kernel(
    torus,
    res_re, res_im, basis_re, basis_im, lens, piv,
    out_coef_re, out_coef_im, out_new_re, out_new_im, out_err,
    live, live_h, basis, base, vlen, vpiv, picked, far, relay, near, ysum, yr, kout, kin, pall, kall, wt,
    coef_re, coef_im, new_re, new_im, err,
    xpart, xpair, xhalf, xin, xfull, gpart, gin, gfull, kspan,
    cpart, cpair, chalf, cin, cfull, dpart, dpair, dhalf, din, dfull, eout, ein,
    in_s, rf_s, rf_r, rn_s, rn_r, ry_s, ry_r, k_s, k_r, p_s, p_r, py_s, py_r, px_s, px_r, ky_s, ky_r, kx_s, kx_r,
    zs_s, zs_r, zg_s, zg_r, cz_r, c_s, c_r, g_s, g_r, e_s, e_r, out_s,
):
    nx, ny, nz, nc = torus
    x, y, z, c = (lax.axis_index(a) for a in AXES)
    f = z * nc + c
    rows, bins = res_re.shape
    emb = 8 * nx * ny
    npiv = emb // 2
    nb = basis_re.shape[0]
    span = 8 * ny

    def hops(d, n):
        return min(d, n - d)

    xs = [(d - 1, lax.rem(x + d, nx)) for d in sorted(range(1, nx), key=lambda d: -hops(d, nx))]
    ys = [(d - 1, lax.rem(y + d, ny)) for d in sorted(range(1, ny), key=lambda d: -hops(d, ny))]
    zs = [(d - 1, lax.rem(z + d, nz)) for d in sorted(range(1, nz), key=lambda d: -hops(d, nz))]
    fs = sorted(((dz, dc) for dz in range(nz) for dc in range(nc) if dz or dc), key=lambda d: -hops(d[0], nz))
    fs = [(dz * nc + dc - 1, (x, y, lax.rem(z + dz, nz), lax.rem(c + dc, nc))) for dz, dc in fs]
    barrier = pltpu.get_barrier_semaphore()
    peers = [(hops(i + 1, ny), (x, p, z, c)) for i, p in ys] + [(hops(i + 1, nx), (p, y, z, c)) for i, p in xs]
    peers += [(hops((i + 1) // nc, nz), to) for i, to in fs]
    peers = [to for _, to in sorted(peers, key=lambda peer: -peer[0])]
    for peer in peers:
        pl.semaphore_signal(barrier, inc=1, device_id=peer, device_id_type=pl.DeviceIdType.MESH)
    loads = [(lens, vlen), (piv, vpiv), (res_re, live.at[:, pl.ds(0, bins)]), (res_im, live.at[:, pl.ds(bins, bins)])]
    loads += [(basis_re, basis.at[0]), (basis_im, basis.at[1])]
    loads = [pltpu.make_async_copy(src, dst, in_s.at[i]) for i, (src, dst) in enumerate(loads)]
    for load in loads:
        load.start()

    started = []
    anyone = fs[0][1]

    def described(src, dst, send, recv, to):
        return pltpu.make_async_remote_copy(
            src_ref=src, dst_ref=dst, send_sem=send, recv_sem=recv, device_id=to,
            device_id_type=pl.DeviceIdType.MESH,
        )

    def begin(src, dst, send, recv, to):
        copy = described(src, dst, send, recv, to)
        copy.start()
        return copy

    def push(src, dst, send, recv, to):
        copy = begin(src, dst, send, recv, to)
        started.append(copy)
        return copy

    def arrived(copies):
        for copy in copies:
            copy.wait_recv()

    finals = []

    def fan(pairs, send, recv, extent):
        for src, dst, to in pairs:
            begin(src, dst, send, recv, to)
        whole = described(extent, extent, send, recv, anyone)
        finals.append(whole)
        return whole

    def chunk_of(i, size):
        return pl.ds(pl.multiple_of(i * size, size), size)

    for load in loads[:4]:
        load.wait()
    diagonal = lax.broadcasted_iota(jnp.int32, (rows, rows), 0) == lax.broadcasted_iota(jnp.int32, (rows, rows), 1)
    ends = jnp.sum(jnp.where(diagonal, vlen[...] * BIN_BLOCK, 0).astype(F32), axis=1, keepdims=True)
    first_bin = f * bins

    def mask_of(part):
        count = part.stop - part.start
        at = first_bin + lax.broadcasted_iota(jnp.int32, (count, bins), 1)
        return (at.astype(F32) < ends[part, :]).astype(F32)

    blocks = [slice(r, min(r + 64, rows)) for r in range(0, rows, 64)]
    for part in blocks:
        mask = mask_of(part)
        live[part, :bins] = live[part, :bins] * mask
        live[part, bins:] = live[part, bins:] * mask
    to_row = lax.broadcasted_iota(jnp.int32, (emb, npiv), 0)
    of_row = lax.broadcasted_iota(jnp.int32, (emb, npiv), 1) == lax.rem(to_row, 4) * (nx * ny) + to_row // 8
    wanted = jnp.sum(jnp.where(of_row, vpiv[...], 0).astype(F32), axis=1, keepdims=True)
    own = (x * ny + y) * rows + lax.broadcasted_iota(jnp.int32, (emb, rows), 1)
    select = (wanted == own.astype(F32)).astype(F32).astype(BF16)
    is_im = lax.rem(lax.broadcasted_iota(jnp.int32, (emb, bins), 0), 8) // 4
    for i, value in enumerate(halves(live[...])):
        live_h[i] = value
    both = sum(dot(select, live_h[i], NN) for i in range(2))
    picked[...] = jnp.where(is_im == 0, both[:, :bins], both[:, bins:])

    pl.semaphore_wait(barrier, len(peers))

    half, pieces = bins // 2, 4
    piece = span // pieces
    ahead, behind = pl.ds(0, half), pl.ds(half, half)
    right, left, across = (lax.rem(x + d, nx) for d in (1, nx - 1, 2))
    ways = (((right, y, z, c), right, ahead), ((left, y, z, c), left, behind))
    far_copies = []
    for i in range(pieces):
        for k, (to, _, lanes) in enumerate(ways):
            at = pl.ds(pl.multiple_of(across * span + i * piece, piece), piece)
            far_copies.append(
                begin(picked.at[at, lanes], far.at[k, pl.ds(i * piece, piece)], rf_s.at[0], rf_r.at[i, k], to)
            )

    for load in loads[4:]:
        load.wait()
    for i in range(2):
        high, low = halves(basis[i])
        base[2 * i] = high
        base[2 * i + 1] = low
    b_re = (base[0], base[1])
    b_im = (base[2], base[3])
    plus = jnp.concatenate([basis[0] + basis[1], basis[1] - basis[0]], axis=1)
    right_side = tuple(jnp.concatenate([base[i], base[2 + i]], axis=1) for i in range(2))
    both = joined(halves(plus), right_side, NT)

    def scatter_rows(part, value):
        size = part.shape[2]
        for i in range(nc):
            for j in range(nz):
                at = (i * nz + j) * size
                part[i, j] = value[at : at + size]

    def pair_up(k, part, got):
        return push(part.at[1 - c], got, p_s.at[k], p_r.at[k], (x, y, z, 1 - c))

    def scatter(k, pair, part, got, summed, inward):
        arrived([pair])
        summed[...] = part[c] + got[...]
        return fan([(summed.at[p], inward.at[i], (x, y, p, c)) for i, p in zs], zs_s.at[k], zs_r.at[k], inward)

    def gathered(copies, summed, inward):
        arrived([copies])
        total = summed[z]
        for i in range(nz - 1):
            total = total + inward[i]
        return total

    def spread(k, total, full, extent):
        full[c, z] = total
        at = full.at[c, z]
        return fan([(at, at, (x, y, p, c)) for i, p in zs], zg_s.at[k], zg_r.at[k], extent)

    def share(k, copies, full):
        arrived([copies])
        return push(full.at[c], full.at[c], c_s.at[k], c_r.at[k], (x, y, z, 1 - c))

    near_started = [
        (picked.at[chunk_of(next_x, span), other], near.at[k, :, other], to)
        for k, ((to, next_x, _), other) in enumerate(zip(ways, (behind, ahead)))
    ]
    for src, dst, to in near_started:
        begin(src, dst, rn_s.at[0], rn_r.at[0], to)
    near_begun = described(near, near, rn_s.at[0], rn_r.at[0], anyone)
    finals.append(near_begun)
    scatter_rows(xpart, both)
    x_pair = pair_up(0, xpart, xpair)
    turned_side = tuple(jnp.concatenate([-base[2 + i], base[i]], axis=1) for i in range(2))
    both = tuple(jnp.concatenate([right_side[i], turned_side[i]], axis=0) for i in range(2))
    scatter_rows(dpart, joined((live_h[0], live_h[1]), both, NT))
    x_scatter = scatter(0, x_pair, xpart, xpair, xhalf, xin)
    d_pair = pair_up(2, dpart, dpair)

    for i in range(pieces):
        for k, (to, next_x, lanes) in enumerate(ways):
            arrived([far_copies[2 * i + k]])
            at = pl.ds(pl.multiple_of(next_x * span + i * piece, piece), piece)
            part = pl.ds(i * piece, piece)
            relay[k, i * piece : (i + 1) * piece] = (
                picked[at, k * half : (k + 1) * half] + far[k, i * piece : (i + 1) * piece]
            )
            begin(relay.at[k, part], near.at[k, part, lanes], rn_s.at[0], rn_r.at[0], to)
    finals.append(described(far, far, rf_s.at[0], rf_r.at[0, 0], anyone))
    d_scatter = scatter(2, d_pair, dpart, dpair, dhalf, din)
    arrived([near_begun])
    ysum[...] = picked[chunk_of(x, span), :] + near[0] + near[1]
    y_copies = fan([(ysum.at[chunk_of(p, 8)], yr.at[i], (x, p, z, c)) for i, p in ys], ry_s.at[0], ry_r.at[0], yr)
    arrived([y_copies])
    chunk = ysum[chunk_of(y, 8), :]
    for i in range(ny - 1):
        chunk = chunk + yr[i]

    mine = x * ny + y
    order = sorted(range(1, ny), key=lambda d: min(d, ny - d))


    def gather(buf, sems, y_extent, x_extent):
        ysend, yrecv, xsend, xrecv = sems

        def rows_of(d):
            return buf.at[pl.ds(pl.multiple_of((x * ny + lax.rem(y + ny - d, ny)) * 8, 8), 8)]

        own_rows = rows_of(0)
        along_y = {
            i + 1: begin(own_rows, own_rows, ysend.at[0], yrecv.at[i], (x, p, z, c)) for i, p in ys
        }

        def forward(d):
            if d:
                arrived([along_y[d]])
            for _, p in xs:
                begin(rows_of(d), rows_of(d), xsend.at[0], xrecv.at[0], (p, y, z, c))

        forward(0)
        last = described(x_extent, x_extent, xsend.at[0], xrecv.at[0], anyone)
        finals.extend([described(y_extent, y_extent, ysend.at[0], yrecv.at[0], anyone), last])
        return forward, last

    pall[chunk_of(mine, 8), :] = chunk
    p_forward, p_last = gather(pall, (py_s, py_r, px_s, px_r), yr, picked.at[pl.ds(0, (nx - 1) * span)])
    sign_k = jnp.where(lax.broadcasted_iota(jnp.int32, (8, nb), 0) < 4, 1.0, -1.0).astype(F32)
    a, b = short_product(chunk, (b_re, b_im), NT)
    kout[...] = a + sign_k * pltpu.roll(b, 4, 0)
    k_copies = fan([(kout, kin.at[i], to) for i, to in fs], k_s.at[0], k_r.at[0], kin)
    for d in order[:4]:
        p_forward(d)
    x_spread = spread(0, gathered(x_scatter, xhalf, xin), xfull, xin)
    d_spread = spread(2, gathered(d_scatter, dhalf, din), dfull, din)
    for d in order[4:]:
        p_forward(d)
    arrived([k_copies])
    proj = kout[...]
    for i in range(len(fs)):
        proj = proj + kin[i]
    kall[chunk_of(mine, 8), :] = proj
    k_forward, k_last = gather(kall, (ky_s, ky_r, kx_s, kx_r), kin.at[pl.ds(0, ny - 1)], kspan)
    arrived([p_last])

    def set_block(top):
        n = top[0].shape[1] // 2
        for i, above in enumerate(top):
            wt[i, :npiv] = above
            wt[i, npiv:, :n] = -above[:, n:]
            wt[i, npiv:, n:] = above[:, :n]

    to_row = lax.broadcasted_iota(jnp.int32, (emb, emb), 0)
    from_row = lax.broadcasted_iota(jnp.int32, (emb, emb), 1)
    by_part = (from_row == lax.rem(to_row, nx * ny) * 8 + to_row // (nx * ny)).astype(F32).astype(BF16)

    def by_parts(a):
        return tuple(dot(by_part, part, NN).astype(BF16) for part in halves(a))

    pivot_halves = by_parts(pall[...])
    pivots = pivot_halves[0].astype(F32) + pivot_halves[1].astype(F32)
    mixed = jnp.concatenate([pivots[:npiv] - pivots[npiv:], pivots[:npiv] + pivots[npiv:]], axis=1)
    top = tuple(as_rows(part) for part in pivot_halves)
    gram = product(top, halves(mixed), NT)
    for i in range(nz * nc):
        gpart[i] = gram[i * gpart.shape[1] : (i + 1) * gpart.shape[1]]
    g_scatter = fan([(gpart.at[to[2] * nc + to[3]], gin.at[i], to) for i, to in fs], g_s.at[0], g_r.at[0], gin)
    set_block(top)
    scatter_rows(cpart, product((live_h[0], live_h[1]), (wt[0], wt[1]), NT))
    c_pair = pair_up(1, cpart, cpair)
    c_scatter = scatter(1, c_pair, cpart, cpair, chalf, cin)
    for d in order:
        k_forward(d)
    x_last = share(0, x_spread, xfull)
    d_last = share(2, d_spread, dfull)
    arrived([g_scatter])
    total = gpart[f]
    for i in range(len(fs)):
        total = total + gin[i]
    gfull[f] = total
    g_gather = fan([(gfull.at[f], gfull.at[f], to) for _, to in fs], g_s.at[1], g_r.at[1], gin)
    cfull[c, z] = gathered(c_scatter, chalf, cin)
    c_own = cfull.at[c, z]
    c_spread = {i: begin(c_own, c_own, zg_s.at[1], cz_r.at[i], (x, y, p, c)) for i, p in zs}
    begin(c_own, c_own, c_s.at[1], c_r.at[1], (x, y, z, 1 - c))
    c_last = described(cfull.at[c], cfull.at[c], c_s.at[1], c_r.at[1], anyone)
    finals.extend([described(cin, cin, zg_s.at[1], zg_r.at[1], anyone), c_last])
    arrived([x_last, d_last])
    arrived([k_last])

    inner = halves(xfull[...].reshape(nb, nb))

    def times_inner(both):
        straight, across = product(both, inner, NN), product(both, inner, NT)
        return crossed(0.5 * (straight + across), 0.5 * (straight - across))

    proj_halves = by_parts(kall[...])
    proj = proj_halves[0].astype(F32) + proj_halves[1].astype(F32)
    taken = 2.0 * proj - times_inner(proj_halves)
    taken_halves = halves(taken)
    rest = halves(as_rows(proj - times_inner(taken_halves)))
    k_both = tuple(embedded(as_rows(part)) for part in proj_halves)
    t_rows = tuple(as_rows(part) for part in taken_halves)
    t_both = tuple(embedded(part) for part in t_rows)
    less = product(t_rows, k_both, NT) + product(rest, t_both, NT)
    cross_less = product(halves(dfull[...].reshape(rows, 2 * nb)), t_both, NT)
    taken = taken_halves
    set_block(halves(as_rows(pivots - crossed(product(taken, b_re, NN), product(taken, b_im, NN)))))
    w = (wt[0], wt[1])
    arrived([g_gather])

    gram = gfull[...].reshape(npiv, npiv)
    turned = gram.T
    gram = jnp.concatenate([0.5 * (gram + turned), 0.5 * (gram - turned)], axis=1) - less
    eye = lax.broadcasted_iota(jnp.int32, (npiv, emb), 0) == lax.broadcasted_iota(jnp.int32, (npiv, emb), 1)
    ident = eye.astype(F32)
    diag = gram * ident
    scale_col = 1.0 / jnp.sqrt(jnp.sum(diag, axis=1, keepdims=True) + EPSILON)
    scale_row = 1.0 / jnp.sqrt(jnp.sum(diag[:, :npiv], axis=0, keepdims=True) + EPSILON)
    scale_row = jnp.concatenate([scale_row, scale_row], axis=1)
    gram = gram * (scale_col * scale_row)
    bound = jnp.max(jnp.sum(jnp.abs(gram), axis=1, keepdims=True), axis=0, keepdims=True)
    your = gram / bound
    zed = None

    def times(left, right):
        return product(left, tuple(embedded(part) for part in right), NN)

    for step in range(NS_STEPS):
        if step == NS_STEPS - 1:
            for i in sorted(range(nz - 1), key=lambda i: hops(i + 1, nz)):
                arrived([c_spread[i]])
                theirs = cfull.at[c, lax.rem(z + nz - 1 - i, nz)]
                begin(theirs, theirs, c_s.at[1], c_r.at[1], (x, y, z, 1 - c))
        yh = halves(your)
        mix = your if zed is None else times(zh, yh)
        s = 1.5 * ident - 0.5 * mix
        sh = halves(s)
        if step < NS_STEPS - 1:
            your = times(yh, sh)
        zed = s if zed is None else times(sh, zh)
        zh = halves(zed)
    zed = zed * (1.0 / jnp.sqrt(bound))

    zed_e = tuple(embedded(part) for part in halves(zed))
    arrived([c_last])
    cross = cfull[...].reshape(rows, emb) - cross_less
    coef = product(halves(cross * scale_row), zed_e, NT)
    coef_re[...] = coef[:, :npiv]
    coef_im[...] = coef[:, npiv:]
    back = product(halves(product(halves(coef), zed_e, NN) * scale_row), w, NN)
    sums = []
    for part in blocks:
        mask = mask_of(part)
        real = (live[part, :bins] - back[part, :bins]) * mask
        imag = (live[part, bins:] - back[part, bins:]) * mask
        new_re[part, :] = real
        new_im[part, :] = imag
        square = real * real + imag * imag
        sums.append(sum(square[:, i : i + 128] for i in range(0, bins, 128)))
    ones = jnp.ones((8, 128), BF16)
    summed = sum(dot(ones, part, NT) for part in thirds(jnp.concatenate(sums, axis=0)))
    eout[...] = summed[0:1, :]
    ein[f] = summed[0:1, :]
    e_copies = fan([(eout, ein.at[f], to) for _, to in fs], e_s.at[0], e_r.at[0], ein.at[pl.ds(0, len(fs))])
    results = [(coef_re, out_coef_re), (coef_im, out_coef_im), (new_re, out_new_re), (new_im, out_new_im), (err, out_err)]
    results = [pltpu.make_async_copy(src, dst, out_s.at[i]) for i, (src, dst) in enumerate(results)]
    for result in results[:4]:
        result.start()
    arrived([e_copies])
    total = ein[0]
    for i in range(1, nz * nc):
        total = total + ein[i]
    err[...] = total / (BIN_BLOCK * vlen[...]).astype(F32)
    results[4].start()

    for copy in started + finals:
        copy.wait_send()
    for result in results:
        result.wait()


def handed_out(*refs):
    count = len(refs) // 2
    copies = [pltpu.make_async_copy(refs[i], refs[count + i], refs[-1].at[i]) for i in range(count)]
    for copy in copies:
        copy.start()
    for copy in copies:
        copy.wait()


def body(torus, res_re, res_im, basis_re, basis_im, lengths, pivots):
    nx, ny, nz, nc = torus
    rows, bins = res_re.shape
    nb = basis_re.shape[0]
    emb = 8 * nx * ny
    nf = nz * nc
    span = 8 * ny
    vmem = pltpu.VMEM
    dma = pltpu.SemaphoreType.DMA
    shapes = [(rows, emb // 2), (rows, emb // 2), (rows, bins), (rows, bins), (1, rows)]

    def summed(count, width):
        part = count // nf
        whole, across = vmem((nc, nz, part, width), F32), vmem((nz, part, width), F32)
        return [whole, across, across, vmem((nz - 1, part, width), F32), whole]

    scratch = [
        vmem((rows, 2 * bins), F32),
        vmem((2, rows, 2 * bins), BF16),
        vmem((2, nb, bins), F32),
        vmem((4, nb, bins), BF16),
        vmem((1, rows), jnp.int32),
        vmem((1, emb // 2), jnp.int32),
        vmem((emb, bins), F32),
        vmem((2, span, bins // 2), F32),
        vmem((2, span, bins // 2), F32),
        vmem((2, span, bins), F32),
        vmem((span, bins), F32),
        vmem((ny - 1, 8, bins), F32),
        vmem((8, nb), F32),
        vmem((nf - 1, 8, nb), F32),
        vmem((emb, bins), F32),
        vmem((emb, nb), F32),
        vmem((2, emb, 2 * bins), BF16),
        *[vmem(shape, F32) for shape in shapes],
        *summed(nb, nb),
        *[vmem((count, emb // 2 // nf, emb // 2), F32) for count in (nf, nf - 1, nf)],
        vmem(((nx - 1) * ny, 8, nb), F32),
        *summed(rows, emb),
        *summed(rows, 2 * nb),
        vmem((1, rows), F32), vmem((nf, 1, rows), F32),
        dma((6,)),
        dma((1,)), dma((4, 2)), *[dma((1,))] * 6, *[dma((3,))] * 2,
        *[dma((1,)), dma((ny - 1,)), dma((1,)), dma((1,))] * 2,
        *[dma((3,))] * 4, dma((nz - 1,)), *[dma((3,))] * 2, *[dma((2,))] * 2, *[dma((1,))] * 2,
        dma((5,)),
    ]
    here = pl.BlockSpec(memory_space=pltpu.VMEM)
    there = pl.BlockSpec(memory_space=pl.ANY)
    results = pl.pallas_call(
        functools.partial(kernel, torus),
        out_shape=[vmem(shape, F32) for shape in shapes],
        in_specs=[there] * 6,
        out_specs=[there] * 5,
        scratch_shapes=scratch,
        compiler_params=pltpu.CompilerParams(collective_id=0, has_side_effects=True),
    )(res_re, res_im, basis_re, basis_im, lengths.reshape(1, rows), pivots.reshape(1, emb // 2))
    coef_re, coef_im, new_re, new_im, err = pl.pallas_call(
        handed_out,
        out_shape=[jax.ShapeDtypeStruct(shape, F32) for shape in shapes],
        in_specs=[here] * 5,
        out_specs=[there] * 5,
        scratch_shapes=[dma((5,))],
    )(*[pltpu.with_memory_space_constraint(result, pltpu.VMEM) for result in results])
    return coef_re, coef_im, new_re, new_im, err.reshape(rows)


def build(mesh, torus):
    axes = Mesh(mesh.devices.reshape(torus), AXES)
    wave, freq = ("x", "y"), ("z", "core")
    in_specs = (P(wave, freq), P(wave, freq), P(None, freq), P(None, freq), P(wave), P())
    out_specs = (P(wave, None), P(wave, None), P(wave, freq), P(wave, freq), P(wave))
    return jax.shard_map(
        functools.partial(body, torus), mesh=axes, in_specs=in_specs, out_specs=out_specs, check_vma=False
    )


def solution(mesh):
    return build(mesh, TORUS)
```
